32 devices in a mesh: fsdp: 4 (over y, x), rep: 8 (over z, core).
Axes of the slice: x: 2, y: 2, z: 4, core: 2. Of those that a mesh axis runs over, the one named last changes fastest.
Arguments:
- inputs: bfloat16 [8, 5120, 512], P('rep', 'fsdp'), may hold values from -6 to 6
- cotangent: bfloat16 [8, 5120, 512], P('rep', 'fsdp'), may hold values from -6 to 6
- segments: int32 [8, 5120], P('rep'), may hold values from 0 to 12, as said below
- trees: int32 [8, 5120], P('rep'), may hold values from 0 to 1, as said below
- parents: int32 [8, 2, 13], P('rep'), may hold values from 0 to 4, as said below
- w_query: bfloat16 [512, 512], P('fsdp'), may hold values from -0.25 to 0.25
- w_key: bfloat16 [512, 512], P('fsdp'), may hold values from -0.25 to 0.25
- w_value: bfloat16 [512, 512], P('fsdp'), may hold values from -0.25 to 0.25
- w_out: bfloat16 [512, 512], P('fsdp'), may hold values from -4 to 4
- w_hidden: bfloat16 [512, 2048], P('fsdp'), may hold values from -0.25 to 0.25
- w_proj: bfloat16 [2048, 512], P('fsdp'), may hold values from -0.125 to 0.125
- norm1_gain: float32 [512], replicated, may hold values from 0.1 to 1.9
- norm1_bias: float32 [512], replicated, may hold values from -3 to 3
- norm2_gain: float32 [512], replicated, may hold values from 0.1 to 1.9
- norm2_bias: float32 [512], replicated, may hold values from -3 to 3
Outputs:
- output: bfloat16 [8, 5120, 512], P('rep', 'fsdp')
- input_grad: float32 [8, 5120, 512], P('rep', 'fsdp')
- grad_query: float32 [512, 512], P('fsdp')
- grad_key: float32 [512, 512], P('fsdp')
- grad_value: float32 [512, 512], P('fsdp')
- grad_out: float32 [512, 512], P('fsdp')
- grad_hidden: float32 [512, 2048], P('fsdp')
- grad_proj: float32 [2048, 512], P('fsdp')
- grad_norm1_gain: float32 [512], replicated
- grad_norm1_bias: float32 [512], replicated
- grad_norm2_gain: float32 [512], replicated
- grad_norm2_bias: float32 [512], replicated
The draws below stay inside these ranges and needn't reach their ends.
Inputs may be any that keep to these rules, and one draw needn't show every extreme that they name: Segment 0 of a tree is its trunk of 1024 tokens, segments 1 to 4 its branches and 5 to 12 its leaves, 128 tokens each; the tokens of a group come in aligned runs of 128 of one segment. `trees`: every tree has 2560 tokens in its group. `parents`: the trunk and the branches have parent 0; every leaf's parent is a branch, two leaves to a branch.
All inputs are finite; a program needn't handle non-finite values.
Results may differ from the reference program's by a relative error of at most 0.02.
Values may be sent and summed in bfloat16 or wider, within the bound.
A program may use at most 192 MiB of HBM per device.

```python
import jax
import jax.numpy as jnp
from jax import lax

D = 512
HEADS = 8
HEAD_DIM = 64
FF = 2048
TREES = 2
BLOCK = 128
GROUPS = 8
GROUP_TOK = 5120


def tree_layout(key):
    base = jax.random.fold_in(key, 17)
    group_keys = jax.random.split(base, GROUPS)

    def one_group(group_key):
        shift_key, order_key, leaf_key = jax.random.split(group_key, 3)
        shift = jax.random.randint(shift_key, (), 0, TREES)
        slots = jnp.arange(20 * TREES, dtype=jnp.int32)
        tree_of = ((slots + shift) % TREES).astype(jnp.int32)
        orders = jax.vmap(lambda inner: jax.random.permutation(inner, 20))(jax.random.split(order_key, TREES))
        kind = orders[tree_of, slots // TREES].astype(jnp.int32)
        segment = jnp.where(kind < 8, 0, kind - 7).astype(jnp.int32)
        leaves = jax.vmap(lambda inner: jax.random.permutation(inner, 8))(jax.random.split(leaf_key, TREES))
        parent = jnp.concatenate([jnp.zeros((TREES, 5), jnp.int32), (1 + leaves // 2).astype(jnp.int32)], axis=1)
        return (jnp.repeat(segment, BLOCK, total_repeat_length=20 * TREES * BLOCK), jnp.repeat(tree_of, BLOCK, total_repeat_length=20 * TREES * BLOCK), parent)
    return jax.vmap(one_group)(group_keys)


def draw_segments(key, part):
    return tree_layout(key)[0].astype(jnp.int32)


def draw_trees(key, part):
    return tree_layout(key)[1].astype(jnp.int32)


def draw_parents(key, part):
    return tree_layout(key)[2].astype(jnp.int32)


def level_of(rng, extent, shards, low, largest):
    def one(dim, parts):
        heights = jax.random.uniform(jax.random.fold_in(jax.random.fold_in(rng, 6), dim), (parts,), jnp.float32, low / len(shards), largest / len(shards))
        return jnp.repeat(jnp.exp(heights), extent[dim] // parts).reshape((-1,) + (1,) * (len(extent) - dim - 1))

    loudness = one(*shards[0])
    for cut in shards[1:]:
        loudness = loudness * one(*cut)
    return loudness


def bell_draw(own_key, extent, deviation, reach, pieces=(), held_as=jnp.bfloat16):
    loudness = level_of(own_key, extent, pieces, -0.22, 0.18) if pieces else 1.0
    array = jax.random.normal(own_key, extent, jnp.float32) * deviation * loudness
    return jnp.minimum(jnp.maximum(array, -reach), reach).astype(held_as)


def setup_inputs(seed: int = 0) -> dict:
    key_of = jax.random.split(jax.random.key(seed), 16)
    return {
        "inputs": bell_draw(key_of[0], (GROUPS, GROUP_TOK, D), 1.0, 6.0, ((0, 8), (1, 4))),
        "cotangent": bell_draw(key_of[1], (GROUPS, GROUP_TOK, D), 1.0, 6.0, ((0, 8), (1, 4))),
        "segments": draw_segments(jax.random.fold_in(key_of[15], 71), 0),
        "trees": draw_trees(jax.random.fold_in(key_of[15], 71), 0),
        "parents": draw_parents(jax.random.fold_in(key_of[15], 71), 0),
        "w_query": bell_draw(key_of[5], (D, D), D ** -0.5, 0.25, ((0, 4),)),
        "w_key": bell_draw(key_of[6], (D, D), D ** -0.5, 0.25, ((0, 4),)),
        "w_value": bell_draw(key_of[7], (D, D), D ** -0.5, 0.25, ((0, 4),)),
        "w_out": bell_draw(key_of[8], (D, D), (max(D // 256, 1)) ** -0.5, 4.0, ((0, 4),)),
        "w_hidden": bell_draw(key_of[9], (D, FF), D ** -0.5, 0.25, ((0, 4),)),
        "w_proj": bell_draw(key_of[10], (FF, D), FF ** -0.5, 0.125, ((0, 4),)),
        "norm1_gain": jnp.clip(1.0 + 0.18 * jax.random.normal(key_of[11], (D,), jnp.float32), 0.1, 1.9),
        "norm1_bias": bell_draw(key_of[12], (D,), 0.5, 3.0, (), jnp.float32),
        "norm2_gain": jnp.clip(1.0 + 0.18 * jax.random.normal(key_of[13], (D,), jnp.float32), 0.1, 1.9),
        "norm2_bias": bell_draw(key_of[14], (D,), 0.5, 3.0, (), jnp.float32),
    }


@jax.custom_vjp
def low(v):
    return lax.optimization_barrier(v.astype(jnp.bfloat16)).astype(jnp.float32)

@jax.custom_vjp
def low_back(v):
    return v

def low_keep(v):
    return (low(v), None)

def low_pass(kept, grad):
    return (grad,)

def back_keep(v):
    return (v, None)

def back_low(kept, grad):
    return (low(grad),)
low.defvjp(low_keep, low_pass)
low_back.defvjp(back_keep, back_low)

def matmul(left, right):
    return jnp.dot(left, right, precision=lax.Precision.HIGHEST)

def norm_rows(h):
    centred = h - lax.optimization_barrier(jnp.mean(h, axis=-1, keepdims=True))
    return centred * lax.rsqrt(lax.optimization_barrier(jnp.mean(centred * centred, axis=-1, keepdims=True)) + 1e-05)

def group_layer(xg, seg, tree, par, weights):
    wq, wk, wv, wo, w1, w2, g1, c1, g2, c2 = weights
    query = low_back(low(matmul(xg, wq)))
    keys = low_back(low(matmul(xg, wk)))
    values = low_back(low(matmul(xg, wv)))
    first = par[tree, seg]
    second = par[tree, first]
    position = jnp.arange(GROUP_TOK, dtype=jnp.int32)
    qrows = min(512, GROUP_TOK)
    count = GROUP_TOK // qrows
    key_heads = keys.reshape(GROUP_TOK, HEADS, HEAD_DIM)
    value_heads = values.reshape(GROUP_TOK, HEADS, HEAD_DIM)

    @jax.checkpoint
    def attend(items):
        qblk, segq, treeq, firstq, secondq, posq = items
        raw = jnp.einsum('qhd,khd->hqk', qblk, key_heads, precision=lax.Precision.HIGHEST) * 0.125
        scores = low_back(raw)
        same = seg[None, :] == segq[:, None]
        allowed = (tree[None, :] == treeq[:, None]) & (same & (position[None, :] <= posq[:, None]) | (seg[None, :] == firstq[:, None]) & (firstq != segq)[:, None] | (seg[None, :] == secondq[:, None]) & (secondq != firstq)[:, None])
        probs = jax.nn.softmax(jnp.where(allowed[None], scores, -1e+30), axis=-1)
        return jnp.einsum('hqk,khd->qhd', low(probs), value_heads, precision=lax.Precision.HIGHEST)
    items = (query.reshape(count, qrows, HEADS, HEAD_DIM), seg.reshape(count, qrows), tree.reshape(count, qrows), first.reshape(count, qrows), second.reshape(count, qrows), position.reshape(count, qrows))
    context = lax.map(attend, items).reshape(GROUP_TOK, D)
    context = low_back(low(context))
    attended = low_back(matmul(context, wo))
    mid = norm_rows(xg + attended) * g1 + c1
    pre = low_back(matmul(low(mid), w1))
    act = low(jax.nn.gelu(pre, approximate=False))
    branch = low_back(matmul(act, w2))
    return norm_rows(mid + branch) * g2 + c2

def reference(inputs, cotangent, segments, trees, parents, w_query, w_key, w_value, w_out, w_hidden, w_proj, norm1_gain, norm1_bias, norm2_gain, norm2_bias):

    def forward(x, wq, wk, wv, wo, w1, w2, g1, c1, g2, c2):
        weights = (wq, wk, wv, wo, w1, w2, g1, c1, g2, c2)

        def step(carry, items):
            xg, seg, tree, par = items
            return (carry, group_layer(xg, seg, tree, par, weights))
        _, result = lax.scan(step, jnp.zeros((), jnp.float32), (x, segments, trees, parents))
        return result
    floats = (inputs.astype(jnp.float32), w_query.astype(jnp.float32), w_key.astype(jnp.float32), w_value.astype(jnp.float32), w_out.astype(jnp.float32), w_hidden.astype(jnp.float32), w_proj.astype(jnp.float32), norm1_gain.astype(jnp.float32), norm1_bias.astype(jnp.float32), norm2_gain.astype(jnp.float32), norm2_bias.astype(jnp.float32))
    result, pullback = jax.vjp(forward, *floats)
    grads = pullback(cotangent.astype(jnp.float32))
    return (result.astype(jnp.bfloat16), grads[0], grads[1], grads[2], grads[3], grads[4], grads[5], grads[6], grads[7], grads[8], grads[9], grads[10])
```

```python
import functools

import jax
import jax.numpy as jnp
from jax import lax
from jax.experimental import pallas as pl
from jax.experimental.pallas import tpu as pltpu
from jax.sharding import PartitionSpec as P

HEADS = 8
HEAD = 64
BLOCK = 128
PAIR = 2 * BLOCK
TRUNK = 8
BRANCHES = 4
LEAVES = 8
TREE_BLOCKS = TRUNK + BRANCHES + LEAVES
TREE_TOK = TREE_BLOCKS * BLOCK
SINGLE = jnp.float32
HALF = jnp.bfloat16
NN = (((1,), (0,)), ((), ()))
NT = (((1,), (1,)), ((), ()))
LOG2E = 1.4426950408889634
SCALE = 0.125 * LOG2E
VMEM_LIMIT = 58 << 20


def dot(left, right, dims=NN):
    return lax.dot_general(left, right, dims, preferred_element_type=SINGLE)


def row_mean(values):
    return jnp.mean(values, axis=-1, keepdims=True)


def block_order(segments, trees, parents, rows, me):
    seg = segments.reshape(-1, BLOCK)[:, 0]
    tree = trees.reshape(-1, BLOCK)[:, 0]
    count = seg.shape[0]
    table = parents.reshape(-1)
    slot = tree * parents.shape[1] + seg
    parent = jnp.sum(
        jnp.where(slot[:, None] == jnp.arange(table.shape[0])[None, :], table[None, :], 0), axis=1
    )
    place = jnp.arange(count, dtype=jnp.int32)
    kind = jnp.where(seg == 0, 0, jnp.where(seg <= BRANCHES, seg, 16 * parent + seg))
    key = (tree * 256 + kind) * 64 + place
    rank = jnp.sum((key[None, :] < key[:, None]).astype(jnp.int32), axis=1)
    per = rows // BLOCK
    near = ((place // per) ^ me) * per + place % per
    order = jnp.sum(jnp.where(rank[None, :] == place[:, None], near[None, :], 0), axis=1)
    return order.astype(jnp.int32)


def tile_list():
    out = []
    trunk = TRUNK * BLOCK
    for start in range(0, trunk, PAIR):
        keys = [(0, start, None)] if start else []
        out.append((start, keys + [(start, PAIR, "causal")]))
    for pair in range(BRANCHES // 2):
        start = trunk + pair * PAIR
        out.append((start, [(0, trunk, None), (start, PAIR, "own")]))
    for branch in range(BRANCHES):
        start = trunk + BRANCHES * BLOCK + branch * PAIR
        out.append(
            (
                start,
                [(0, trunk, None), (trunk + branch * BLOCK, BLOCK, None), (start, PAIR, "own")],
            )
        )
    return out


def mask_of(kind):
    key = lax.broadcasted_iota(jnp.int32, (PAIR, PAIR), 0)
    query = lax.broadcasted_iota(jnp.int32, (PAIR, PAIR), 1)
    mask = key <= query
    if kind == "own":
        mask = mask & ((key >= BLOCK) == (query >= BLOCK))
    return mask


def pair_rows(order_ref, tree, start):
    first = tree * TREE_BLOCKS + start // BLOCK
    return [pl.ds(pl.multiple_of(order_ref[first + i] * BLOCK, BLOCK), BLOCK) for i in range(2)]


def attend_kernel(
    heads, order_ref, x_ref, w_ref, ctx_ref, q_ref, k_ref, v_ref, kt_ref, ot_ref, lse_ref, vt_ref
):
    trees = q_ref.shape[0] // heads
    wide = heads * HEAD

    def project(step, _):
        tree = step // (TREE_BLOCKS // 2)
        start = pl.multiple_of((step % (TREE_BLOCKS // 2)) * PAIR, PAIR)
        rows = [
            pl.ds(pl.multiple_of(order_ref[2 * step + i] * BLOCK, BLOCK), BLOCK) for i in range(2)
        ]
        x = jnp.concatenate([x_ref[r, :] for r in rows], axis=0)
        out = dot(x, w_ref[...]).astype(HALF)
        here = pl.ds(start, PAIR)
        kt = out[:, wide : 2 * wide].T
        vt = out[:, 2 * wide :].T
        for h in range(heads):
            at = tree * heads + h
            cols = slice(h * HEAD, (h + 1) * HEAD)
            q_ref[at, here, :] = out[:, cols]
            k_ref[at, here, :] = out[:, wide:][:, cols]
            v_ref[at, here, :] = out[:, 2 * wide :][:, cols]
            kt_ref[at, :, here] = kt[cols]
            vt_ref[at, :, here] = vt[cols]
        return 0

    lax.fori_loop(0, trees * TREE_BLOCKS // 2, project, 0)

    def tree_step(tree, _):
        for start, keys in tile_list():
            outs = []
            for h in range(heads):
                at = tree * heads + h
                q = q_ref[at, start : start + PAIR, :]
                scores = []
                for off, size, kind in keys:
                    s = dot(k_ref[at, off : off + size, :], q, NT)
                    if kind:
                        s = jnp.where(mask_of(kind), s, -1e30)
                    scores.append(s)
                top = functools.reduce(
                    jnp.maximum, [jnp.max(s, axis=0, keepdims=True) for s in scores]
                )
                top = top * SCALE
                mass = 0.0
                acc = 0.0
                for (off, size, _), s in zip(keys, scores):
                    e = jnp.exp2(s * SCALE - top)
                    mass = mass + jnp.sum(e, axis=0, keepdims=True)
                    acc = acc + dot(vt_ref[at, :, off : off + size], e.astype(HALF))
                outs.append(acc * (1.0 / mass))
                lse_ref[at, :, start : start + PAIR] = top + jnp.log2(mass)
            out = jnp.concatenate(outs, axis=0) if heads > 1 else outs[0]
            ot_ref[tree, :, start : start + PAIR] = out
            ctx = out.T.astype(HALF)
            for i, r in enumerate(pair_rows(order_ref, tree, start)):
                ctx_ref[r, :] = ctx[i * BLOCK : (i + 1) * BLOCK]
        return 0

    lax.fori_loop(0, trees, tree_step, 0)


def vmem(count):
    return [pl.BlockSpec(memory_space=pltpu.VMEM)] * count


def shape(dims, dtype):
    return jax.ShapeDtypeStruct(dims, dtype)


def attend(order, x, w, heads):
    total = x.shape[0]
    trees = total // TREE_TOK
    n = trees * heads
    return pl.pallas_call(
        functools.partial(attend_kernel, heads),
        out_shape=[
            shape((total, heads * HEAD), HALF),
            shape((n, TREE_TOK, HEAD), HALF),
            shape((n, TREE_TOK, HEAD), HALF),
            shape((n, TREE_TOK, HEAD), HALF),
            shape((n, HEAD, TREE_TOK), HALF),
            shape((trees, heads * HEAD, TREE_TOK), SINGLE),
            shape((n, 1, TREE_TOK), SINGLE),
        ],
        in_specs=[pl.BlockSpec(memory_space=pltpu.SMEM)] + vmem(2),
        out_specs=vmem(7),
        scratch_shapes=[pltpu.VMEM((n, HEAD, TREE_TOK), HALF)],
        compiler_params=pltpu.CompilerParams(vmem_limit_bytes=VMEM_LIMIT),
        cost_estimate=pl.CostEstimate(
            flops=10 * 10**9, bytes_accessed=20 * 10**6, transcendentals=11 * 10**6
        ),
        name="attend",
    )(order, x, w)


def pack_grads(me, parts, ao, ah, ap, pack_ref):
    width = ao.shape[1]
    depth = ao.shape[0] // parts
    inner = ah.shape[1]
    cols = inner // parts
    for c in range(parts):
        to = c ^ me
        pack_ref[to, 0:depth, :] = ao[c * depth : (c + 1) * depth, :].astype(HALF)
        for j in range(inner // width):
            pack_ref[to, depth * (j + 1) : depth * (j + 2), :] = ah[
                c * depth : (c + 1) * depth, j * width : (j + 1) * width
            ].astype(HALF)
        base = depth * (1 + inner // width)
        piece = ap[:, c * cols : (c + 1) * cols].astype(HALF)
        for j in range(width // cols):
            pack_ref[to, base : base + cols, j * cols : (j + 1) * cols] = piece[
                j * cols : (j + 1) * cols
            ]


def forward_back_kernel(
    chunk,
    me_ref,
    x_ref,
    ctx_ref,
    dy_ref,
    wo_ref,
    wh_ref,
    wp_ref,
    vec_ref,
    out_ref,
    dh1_ref,
    dctx_ref,
    pack_ref,
    norm_ref,
    ao,
    ah,
    ap,
    g_s,
    d_s,
):
    step = pl.program_id(0)
    me = me_ref[0]
    parts = ctx_ref.shape[0]
    inner = wh_ref.shape[1]
    gain1, bias1 = vec_ref[0:1, :], vec_ref[1:2, :]
    gain2, bias2 = vec_ref[2:3, :], vec_ref[3:4, :]

    @pl.when(step == 0)
    def _():
        for ref in (ao, ah, ap, norm_ref):
            ref[...] = jnp.zeros_like(ref)

    ctx = jnp.concatenate([ctx_ref[c ^ me] for c in range(parts)], axis=-1)
    h1 = x_ref[...].astype(SINGLE) + dot(ctx, wo_ref[...])
    c1 = h1 - row_mean(h1)
    r1 = lax.rsqrt(row_mean(c1 * c1) + 1e-5)
    n1 = c1 * r1
    y1 = n1 * gain1 + bias1
    u = y1.astype(HALF)
    branch = 0.0
    for j in range(0, inner, chunk):
        s = slice(j, j + chunk)
        z = dot(u, wh_ref[:, s])
        cdf = 0.5 * (1.0 + lax.erf(z * 0.7071067811865476))
        pdf = jnp.exp2(z * z * (-0.5 * LOG2E)) * 0.3989422804014327
        g = (z * cdf).astype(HALF)
        g_s[:, s] = g
        d_s[:, s] = cdf + z * pdf
        branch = branch + dot(g, wp_ref[s, :])
    h2 = y1 + branch
    c2 = h2 - row_mean(h2)
    r2 = lax.rsqrt(row_mean(c2 * c2) + 1e-5)
    n2 = c2 * r2
    out_ref[...] = (n2 * gain2 + bias2).astype(HALF)
    dy = dy_ref[...].astype(SINGLE)
    norm_ref[2:3, :] += jnp.sum(dy * n2, axis=0, keepdims=True)
    norm_ref[3:4, :] += jnp.sum(dy, axis=0, keepdims=True)
    dn2 = dy * gain2
    dh2 = r2 * (dn2 - row_mean(dn2) - n2 * row_mean(dn2 * n2))
    df = dh2.astype(HALF)
    df_t = df.T
    u_t = u.T
    back = 0.0
    for j in range(0, inner, chunk):
        s = slice(j, j + chunk)
        dz = (dot(df, wp_ref[s, :], NT) * d_s[:, s]).astype(HALF)
        back = back + dot(dz, wh_ref[:, s], NT)
        ap[:, s] += dot(df_t, g_s[:, s])
        ah[:, s] += dot(u_t, dz)
    dy1 = dh2 + back
    norm_ref[0:1, :] += jnp.sum(dy1 * n1, axis=0, keepdims=True)
    norm_ref[1:2, :] += jnp.sum(dy1, axis=0, keepdims=True)
    dn1 = dy1 * gain1
    dh1 = r1 * (dn1 - row_mean(dn1) - n1 * row_mean(dn1 * n1))
    dh1_ref[...] = dh1
    da = dh1.astype(HALF)
    ao[...] += dot(ctx.T, da)
    dctx = dot(da, wo_ref[...], NT).astype(HALF)
    wide = dctx.shape[1] // parts
    for c in range(parts):
        dctx_ref[c ^ me] = dctx[:, c * wide : (c + 1) * wide]

    @pl.when(step == pl.num_programs(0) - 1)
    def _():
        pack_grads(me, parts, ao, ah, ap, pack_ref)


def forward_back(me, x, ctx, dy, wo, wh, wp, vec):
    rows, width = x.shape
    parts, _, wide = ctx.shape
    inner = wh.shape[1]
    tile = PAIR if rows % PAIR == 0 else BLOCK
    packed = (width // parts) * (1 + inner // width) + inner // parts
    row = lambda w: pl.BlockSpec((tile, w), lambda i: (i, 0))
    tok = pl.BlockSpec((parts, tile, wide), lambda i: (0, i, 0))
    once = lambda a, b: pl.BlockSpec((a, b), lambda i: (0, 0), pipeline_mode=pl.Buffered(1))
    return pl.pallas_call(
        functools.partial(forward_back_kernel, 512),
        grid=(rows // tile,),
        in_specs=[
            pl.BlockSpec(memory_space=pltpu.SMEM),
            row(width),
            tok,
            row(width),
            once(width, width),
            once(width, inner),
            once(inner, width),
            once(4, width),
        ],
        out_specs=[
            row(width),
            row(width),
            tok,
            pl.BlockSpec((parts, packed, width), lambda i: (0, 0, 0)),
            pl.BlockSpec((4, width), lambda i: (0, 0)),
        ],
        out_shape=[
            shape((rows, width), HALF),
            shape((rows, width), SINGLE),
            shape((parts, rows, wide), HALF),
            shape((parts, packed, width), HALF),
            shape((4, width), SINGLE),
        ],
        scratch_shapes=[
            pltpu.VMEM((width, width), SINGLE),
            pltpu.VMEM((width, inner), SINGLE),
            pltpu.VMEM((width, inner), SINGLE),
            pltpu.VMEM((tile, inner), HALF),
            pltpu.VMEM((tile, inner), SINGLE),
        ],
        compiler_params=pltpu.CompilerParams(vmem_limit_bytes=VMEM_LIMIT),
        cost_estimate=pl.CostEstimate(
            flops=18 * 10**9, bytes_accessed=20 * 10**6, transcendentals=5 * 10**6
        ),
        name="forward_back",
    )(me, x, ctx, dy, wo, wh, wp, vec)


def attend_back_kernel(
    heads,
    order_ref,
    x_ref,
    q_ref,
    k_ref,
    v_ref,
    kt_ref,
    ot_ref,
    lse_ref,
    do_ref,
    g_ref,
    dw_ref,
    dk_s,
    dv_s,
    dw_s,
):
    trees = q_ref.shape[0] // heads
    wide = heads * HEAD

    def tree_step(tree, _):
        dk_s[...] = jnp.zeros_like(dk_s)
        dv_s[...] = jnp.zeros_like(dv_s)
        for start, keys in tile_list():
            here = slice(start, start + PAIR)
            rows = pair_rows(order_ref, tree, start)
            grad = jnp.concatenate([do_ref[r, :] for r in rows], axis=0)
            prod = grad.T.astype(SINGLE) * ot_ref[tree, :, here]
            grads = []
            for h in range(heads):
                at = tree * heads + h
                cols = slice(h * HEAD, (h + 1) * HEAD)
                q = q_ref[at, here, :]
                do = grad[:, cols]
                lse = lse_ref[at, :, here]
                delta = jnp.sum(prod[cols], axis=0, keepdims=True)
                dq = 0.0
                for off, size, kind in keys:
                    span = slice(off, off + size)
                    p = jnp.exp2(dot(k_ref[at, span, :], q, NT) * SCALE - lse)
                    if kind:
                        p = jnp.where(mask_of(kind), p, 0.0)
                    dp = dot(v_ref[at, span, :], do, NT)
                    ds = (p * (dp - delta)).astype(HALF)
                    dv_s[h, span, :] += dot(p.astype(HALF), do)
                    dk_s[h, span, :] += dot(ds, q)
                    dq = dq + dot(kt_ref[at, :, span], ds)
                grads.append(dq * 0.125)
            dq = (jnp.concatenate(grads, axis=0) if heads > 1 else grads[0]).T.astype(HALF)
            for i, r in enumerate(rows):
                g_ref[r, 0:wide] = dq[i * BLOCK : (i + 1) * BLOCK]
        for start in range(0, TREE_TOK, PAIR):
            here = slice(start, start + PAIR)
            dk = [dk_s[h, here, :] * 0.125 for h in range(heads)]
            dv = [dv_s[h, here, :] for h in range(heads)]
            both = jnp.concatenate(dk + dv, axis=-1).astype(HALF)
            for i, r in enumerate(pair_rows(order_ref, tree, start)):
                g_ref[r, wide : 3 * wide] = both[i * BLOCK : (i + 1) * BLOCK]
        return 0

    lax.fori_loop(0, trees, tree_step, 0)
    dw_s[...] = jnp.zeros_like(dw_s)
    step = 4 * BLOCK

    def weight_step(i, _):
        r = pl.ds(pl.multiple_of(i * step, step), step)
        dw_s[...] += dot(g_ref[r, :].T, x_ref[r, :])
        return 0

    lax.fori_loop(0, x_ref.shape[0] // step, weight_step, 0)
    dw_ref[...] = dw_s[...].astype(HALF)


def attend_back(order, x, saved, do, heads):
    total, width = x.shape
    wide = heads * HEAD
    return pl.pallas_call(
        functools.partial(attend_back_kernel, heads),
        out_shape=[shape((total, 3 * wide), HALF), shape((3 * wide, width), HALF)],
        in_specs=[pl.BlockSpec(memory_space=pltpu.SMEM)] + vmem(8),
        out_specs=vmem(2),
        scratch_shapes=[
            pltpu.VMEM((heads, TREE_TOK, HEAD), SINGLE),
            pltpu.VMEM((heads, TREE_TOK, HEAD), SINGLE),
            pltpu.VMEM((3 * wide, width), SINGLE),
        ],
        compiler_params=pltpu.CompilerParams(vmem_limit_bytes=VMEM_LIMIT),
        cost_estimate=pl.CostEstimate(
            flops=25 * 10**9, bytes_accessed=30 * 10**6, transcendentals=11 * 10**6
        ),
        name="attend_back",
    )(order, x, *saved, do)


def input_kernel(me_ref, base_ref, g_ref, w_ref, out_ref):
    me = me_ref[0]
    total = base_ref[...]
    for r in range(g_ref.shape[0]):
        total = total + dot(g_ref[r], w_ref[r ^ me], NT)
    out_ref[...] = total


def input_gradient(me, base, grads, weights):
    rows, width = base.shape
    parts, _, wide = grads.shape
    tile = PAIR if rows % PAIR == 0 else BLOCK
    row = pl.BlockSpec((tile, width), lambda i: (i, 0))
    return pl.pallas_call(
        input_kernel,
        grid=(rows // tile,),
        in_specs=[
            pl.BlockSpec(memory_space=pltpu.SMEM),
            row,
            pl.BlockSpec((parts, tile, wide), lambda i: (0, i, 0)),
            pl.BlockSpec(
                (parts, width, wide), lambda i: (0, 0, 0), pipeline_mode=pl.Buffered(1)
            ),
        ],
        out_specs=row,
        out_shape=shape((rows, width), SINGLE),
        compiler_params=pltpu.CompilerParams(vmem_limit_bytes=VMEM_LIMIT),
        cost_estimate=pl.CostEstimate(
            flops=2 * 10**9, bytes_accessed=11 * 10**6, transcendentals=0
        ),
        name="input_gradient",
    )(me, base, grads, weights)


def swap(value, axis, size, bit):
    return lax.ppermute(value, axis, [(i, i ^ bit) for i in range(size)])


def gather_near(value, parts):
    if parts != 4:
        return [value] + [swap(value, "fsdp", parts, r) for r in range(1, parts)]
    half = value.shape[0] // 2
    first = swap(value, "fsdp", parts, 1)
    second = swap(value, "fsdp", parts, 2)
    upper = swap(first[:half], "fsdp", parts, 2)
    lower = swap(second[half:], "fsdp", parts, 1)
    return [value, first, second, jnp.concatenate([upper, lower], axis=0)]


def exchange(value, parts):
    return jnp.stack([value[0]] + [swap(value[r], "fsdp", parts, r) for r in range(1, parts)])


def to_absolute(value, me):
    bit = 1
    while bit < value.shape[0]:
        flipped = value.reshape((-1, 2, bit) + value.shape[1:])[:, ::-1].reshape(value.shape)
        value = jnp.where((me & bit) != 0, flipped, value)
        bit *= 2
    return value


def shards(
    parts,
    inputs,
    cotangent,
    segments,
    trees,
    parents,
    w_query,
    w_key,
    w_value,
    w_out,
    w_hidden,
    w_proj,
    norm1_gain,
    norm1_bias,
    norm2_gain,
    norm2_bias,
):
    x = inputs[0]
    rows, width = x.shape
    inner = w_hidden.shape[1]
    heads = HEADS // parts
    wide = heads * HEAD
    depth = width // parts
    me = lax.axis_index("fsdp")
    me_arg = me.astype(jnp.int32).reshape(1)
    order = block_order(segments[0], trees[0], parents[0], rows, me)

    small = jnp.concatenate([w_query, w_key, w_value, w_out], axis=1)
    small_all = lax.all_gather(small, "fsdp", axis=0, tiled=True)
    near = jnp.concatenate(gather_near(x, parts), axis=0)
    full_h = lax.all_gather(w_hidden, "fsdp", axis=0, tiled=True)
    full_p = lax.all_gather(w_proj, "fsdp", axis=0, tiled=True)
    full_o = small_all[:, 3 * width :]
    by_device = small_all[:, : 3 * width].reshape(width, 3, parts, wide)
    by_device = by_device.transpose(2, 0, 1, 3).reshape(parts, width, 3 * wide)
    own = lax.dynamic_index_in_dim(by_device, me, 0, keepdims=False)

    ctx, *saved = attend(order, near, own, heads)
    ctx = exchange(ctx.reshape(parts, rows, wide), parts)
    vec = jnp.stack([norm1_gain, norm1_bias, norm2_gain, norm2_bias])
    output, dh1, dctx, pack, norms = forward_back(
        me_arg, x, ctx, cotangent[0], full_o, full_h, full_p, vec
    )
    do = exchange(dctx, parts).reshape(parts * rows, wide)
    grads, dw = attend_back(order, near, saved, do, heads)
    grads = exchange(grads.reshape(parts, rows, 3 * wide), parts)
    input_grad = input_gradient(me_arg, dh1, grads, by_device)

    pack = exchange(pack, parts).astype(SINGLE).sum(axis=0).astype(HALF)
    pack = lax.psum(pack, "rep").astype(SINGLE)
    grad_out = pack[:depth]
    base = depth * (1 + inner // width)
    grad_hidden = (
        pack[depth:base].reshape(inner // width, depth, width).transpose(1, 0, 2)
    ).reshape(depth, inner)
    cols = inner // parts
    grad_proj = pack[base:].reshape(cols, width // cols, cols).transpose(2, 1, 0)
    grad_proj = grad_proj.reshape(cols, width)

    dw = lax.psum(dw, "rep")
    dw = dw.reshape(3 * wide, parts, depth).transpose(1, 0, 2)
    dw = to_absolute(exchange(to_absolute(dw, me), parts), me).astype(SINGLE)
    dw = dw.reshape(parts, 3, wide, depth).transpose(1, 3, 0, 2).reshape(3, depth, width)
    norms = lax.psum(norms, ("fsdp", "rep"))
    return (
        output[None],
        input_grad[None],
        dw[0],
        dw[1],
        dw[2],
        grad_out,
        grad_hidden,
        grad_proj,
        norms[0],
        norms[1],
        norms[2],
        norms[3],
    )


def solution(mesh):
    token = P("rep", "fsdp", None)
    weight = P("fsdp", None)
    placed = (token, token, P("rep", None), P("rep", None), P("rep", None, None))
    return jax.shard_map(
        functools.partial(shards, mesh.shape["fsdp"]),
        mesh=mesh,
        in_specs=placed + (weight,) * 6 + (P(),) * 4,
        out_specs=(token, token) + (weight,) * 6 + (P(),) * 4,
        check_vma=False,
    )
```

```python
import functools

import jax
import jax.numpy as jnp
from jax import lax
from jax.experimental import pallas as pl
from jax.experimental.pallas import tpu as pltpu
from jax.sharding import PartitionSpec as P

HEADS = 8
HEAD = 64
BLOCK = 128
PAIR = 2 * BLOCK
TRUNK = 8
BRANCHES = 4
LEAVES = 8
TREE_BLOCKS = TRUNK + BRANCHES + LEAVES
TREE_TOK = TREE_BLOCKS * BLOCK
SINGLE = jnp.float32
HALF = jnp.bfloat16
NN = (((1,), (0,)), ((), ()))
NT = (((1,), (1,)), ((), ()))
LOG2E = 1.4426950408889634
SCALE = 0.125 * LOG2E
VMEM_LIMIT = 58 << 20
MESH = pl.DeviceIdType.MESH
SLICES = 8
LAYERS = 4


def dot(left, right, dims=NN):
    return lax.dot_general(left, right, dims, preferred_element_type=SINGLE)


def row_mean(values):
    return jnp.mean(values, axis=-1, keepdims=True)


def block_order(segments, trees, parents, rows, me):
    seg = segments.reshape(-1, BLOCK)[:, 0]
    tree = trees.reshape(-1, BLOCK)[:, 0]
    count = seg.shape[0]
    table = parents.reshape(-1)
    slot = tree * parents.shape[1] + seg
    parent = jnp.sum(
        jnp.where(slot[:, None] == jnp.arange(table.shape[0])[None, :], table[None, :], 0), axis=1
    )
    place = jnp.arange(count, dtype=jnp.int32)
    kind = jnp.where(seg == 0, 0, jnp.where(seg <= BRANCHES, seg, 16 * parent + seg))
    key = (tree * 256 + kind) * 64 + place
    rank = jnp.sum((key[None, :] < key[:, None]).astype(jnp.int32), axis=1)
    per = rows // BLOCK
    near = ((place // per) ^ me) * per + place % per
    order = jnp.sum(jnp.where(rank[None, :] == place[:, None], near[None, :], 0), axis=1)
    back = jnp.sum(jnp.where(near[None, :] == place[:, None], rank[None, :], 0), axis=1)
    return jnp.concatenate([order, back]).astype(jnp.int32)


def tile_list():
    out = []
    trunk = TRUNK * BLOCK
    for start in range(0, trunk, PAIR):
        keys = [(0, start, None)] if start else []
        out.append((start, keys + [(start, PAIR, "causal")]))
    for pair in range(BRANCHES // 2):
        start = trunk + pair * PAIR
        out.append((start, [(0, trunk, None), (start, PAIR, "own")]))
    for branch in range(BRANCHES):
        start = trunk + BRANCHES * BLOCK + branch * PAIR
        out.append(
            (
                start,
                [(0, trunk, None), (trunk + branch * BLOCK, BLOCK, None), (start, PAIR, "own")],
            )
        )
    return out


def mask_of(kind):
    key = lax.broadcasted_iota(jnp.int32, (PAIR, PAIR), 0)
    query = lax.broadcasted_iota(jnp.int32, (PAIR, PAIR), 1)
    mask = key <= query
    if kind == "own":
        mask = mask & ((key >= BLOCK) == (query >= BLOCK))
    return mask


def flip(value, bits):
    bit = 1
    while bit <= bits:
        if bits & bit:
            value = value + bit - 2 * bit * lax.rem(lax.div(value, bit), 2)
        bit *= 2
    return value


class Wire:
    def __init__(self, local_sem, send_sem, recv_sem):
        self.local_sem, self.send_sem, self.recv_sem = local_sem, send_sem, recv_sem
        self.locals = self.remotes = 0
        self.open = []

    def keep(self, source, target):
        copy = pltpu.make_async_copy(source, target, self.local_sem.at[self.locals])
        self.locals += 1
        copy.start()
        return copy

    def send(self, source, target, axis, peer):
        copy = pltpu.make_async_remote_copy(
            source,
            target,
            self.send_sem.at[self.remotes],
            self.recv_sem.at[self.remotes],
            device_id={axis: peer},
            device_id_type=MESH,
        )
        self.remotes += 1
        copy.start()
        self.open.append(copy)
        return copy

    def finish(self):
        for copy in self.open:
            copy.wait_send()


def greet(peers):
    barrier = pltpu.get_barrier_semaphore()
    for axis, peer in peers:
        pl.semaphore_signal(barrier, inc=1, device_id={axis: peer}, device_id_type=MESH)
    pl.semaphore_wait(barrier, len(peers))


def places(parts, copies):
    me = lax.axis_index("fsdp")
    rep = lax.axis_index("rep")
    near = [(r, ("fsdp", flip(me, r))) for r in range(1, parts)]
    core = ("rep", flip(rep, 1))
    layers = [(j, ("rep", flip(rep, 2 * j))) for j in range(1, LAYERS)]
    far = []
    bit = 2 * LAYERS
    while bit < copies:
        far.append(("rep", flip(rep, bit)))
        bit *= 2
    return me, rep, near, core, layers, far


def attend_head(head, trees, q_ref, k_ref, vt_ref, ot_ref, lse_ref, flat_ref):
    for start, keys in tile_list():
        here = slice(start, start + PAIR)
        for tree in range(trees):
            at = head * trees + tree
            q = q_ref[at, here, :]
            scores = []
            for off, size, kind in keys:
                s = dot(k_ref[at, off : off + size, :], q, NT)
                if kind:
                    s = jnp.where(mask_of(kind), s, -1e30)
                scores.append(s)
            top = functools.reduce(
                jnp.maximum, [jnp.max(s, axis=0, keepdims=True) for s in scores]
            )
            top = top * SCALE
            mass = 0.0
            acc = 0.0
            for (off, size, _), s in zip(keys, scores):
                e = jnp.exp2(s * SCALE - top)
                mass = mass + jnp.sum(e, axis=0, keepdims=True)
                acc = acc + dot(vt_ref[at, :, off : off + size], e.astype(HALF))
            out = acc * (1.0 / mass)
            lse_ref[at, :, here] = top + jnp.log2(mass)
            ot_ref[at, :, here] = out
            place = tree * TREE_BLOCKS + start // BLOCK
            flat_ref[place : place + 2] = out.T.astype(HALF).reshape(2, BLOCK, HEAD)


def fold(block):
    return jnp.concatenate([block[: BLOCK // 2], block[BLOCK // 2 :]], axis=1)


def unfold(packed):
    parts = []
    for i in range(packed.shape[0] // (BLOCK // 2)):
        piece = packed[i * (BLOCK // 2) : (i + 1) * (BLOCK // 2)]
        parts += [piece[:, :HEAD], piece[:, HEAD:]]
    return jnp.concatenate(parts, axis=0)


def block_at(index):
    return pl.ds(pl.multiple_of(index * BLOCK, BLOCK), BLOCK)


def start_kernel(
    parts,
    copies,
    heads,
    order_ref,
    x_hbm,
    by_hbm,
    sa_hbm,
    sb_hbm,
    near_hbm,
    q_hbm,
    k_hbm,
    v_hbm,
    kt_hbm,
    ot_hbm,
    lse_hbm,
    ctx_hbm,
    wa_hbm,
    wb_hbm,
    near_ref,
    own_ref,
    q_ref,
    k_ref,
    v_ref,
    kt_ref,
    vt_ref,
    ot_ref,
    lse_ref,
    flat_ref,
    ctx_ref,
    local_sem,
    send_sem,
    recv_sem,
):
    wire = Wire(local_sem, send_sem, recv_sem)
    me, rep, near, core, layers, far = places(parts, copies)
    per = x_hbm.shape[0]
    blocks = parts * per
    trees = blocks // TREE_BLOCKS
    wide = heads * HEAD
    greet([p for _, p in near] + [core] + [p for _, p in layers])

    side = lax.rem(rep, 2)
    layer = lax.rem(lax.div(rep, 2), LAYERS)
    mine = side * LAYERS + layer
    kept = [
        wire.keep(by_hbm.at[me], own_ref.at[me]),
        wire.keep(x_hbm, near_ref.at[pl.ds(0, per)]),
    ]
    own_copies = [wire.send(by_hbm.at[p[1]], own_ref.at[me], *p) for _, p in near]
    first = []
    for r, p in near:
        first.append(wire.send(sa_hbm.at[mine], wa_hbm.at[me, mine], *p))
        first.append(wire.send(sb_hbm.at[mine], wb_hbm.at[me, mine], *p))
    late = [wire.keep(sa_hbm, wa_hbm.at[me]), wire.keep(sb_hbm, wb_hbm.at[me])]

    def second():
        for copy in first:
            copy.wait_recv()
        out = []
        for _, p in layers:
            for r in range(1, parts):
                c = flip(me, r)
                out.append(wire.send(wa_hbm.at[c, mine], wa_hbm.at[c, mine], *p))
                out.append(wire.send(wb_hbm.at[c, mine], wb_hbm.at[c, mine], *p))
        return out

    def third(copies_in):
        for copy in copies_in:
            copy.wait_recv()
        out = []
        half = pl.ds(side * LAYERS, LAYERS)
        for r in range(1, parts):
            c = flip(me, r)
            out.append(wire.send(wa_hbm.at[c, half], wa_hbm.at[c, half], *core))
            out.append(wire.send(wb_hbm.at[c, half], wb_hbm.at[c, half], *core))
        return out

    if parts == 4:
        cuts = [i * per // 4 for i in range(5)]

        def part(chunk, i):
            return pl.ds(chunk * per + cuts[i], cuts[i + 1] - cuts[i])

        (_, px), (_, py), _ = near
        one, two = {}, {}
        for a, b in zip((0, 1, 2, 3), (2, 3, 0, 1)):
            one[a] = wire.send(x_hbm.at[part(0, a)], near_ref.at[part(1, a)], *px)
            two[b] = wire.send(x_hbm.at[part(0, b)], near_ref.at[part(2, b)], *py)
        three = []
        for a, b in ((0, 2), (1, 3)):
            one[a].wait_recv()
            three.append(wire.send(near_ref.at[part(1, a)], near_ref.at[part(3, a)], *py))
            two[b].wait_recv()
            three.append(wire.send(near_ref.at[part(2, b)], near_ref.at[part(3, b)], *px))
            if a == 0:
                layered = second()
        waits = [one[2], one[3], two[0], two[1]] + three
    else:
        waits = [wire.send(x_hbm, near_ref.at[pl.ds(r * per, per)], *p) for r, p in near]
        layered = second()
    for copy in own_copies + waits:
        copy.wait_recv()
    for copy in kept:
        copy.wait()
    saves = [wire.keep(near_ref, near_hbm)]
    weight = own_ref[...].reshape(parts * own_ref.shape[1], 3 * wide)
    half = TREE_BLOCKS // 2

    def project(step, _):
        tree = lax.div(step, half)
        start = pl.multiple_of(lax.rem(step, half) * PAIR, PAIR)
        x = jnp.concatenate(
            [near_ref[order_ref[2 * step + i]] for i in range(2)], axis=0
        )
        out = dot(x, weight).astype(HALF)
        here = pl.ds(start, PAIR)
        kt = out[:, wide : 2 * wide].T
        vt = out[:, 2 * wide :].T
        for h in range(heads):
            at = h * trees + tree
            cols = slice(h * HEAD, (h + 1) * HEAD)
            q_ref[at, here, :] = out[:, cols]
            k_ref[at, here, :] = out[:, wide:][:, cols]
            v_ref[at, here, :] = out[:, 2 * wide :][:, cols]
            kt_ref[at, :, here] = kt[cols]
            vt_ref[at, :, here] = vt[cols]
        return 0

    lax.fori_loop(0, blocks // 2, project, 0)
    cored = third(layered)
    saves += [
        wire.keep(a, b)
        for a, b in ((q_ref, q_hbm), (k_ref, k_hbm), (v_ref, v_hbm), (kt_ref, kt_hbm))
    ]
    context = []
    for h in range(heads):
        attend_head(h, trees, q_ref, k_ref, vt_ref, ot_ref, lse_ref, flat_ref)
        for r in range(parts):

            def unsort(j, _):
                block = flat_ref[order_ref[blocks + r * per + j]]
                at = pl.ds(pl.multiple_of(j * (BLOCK // 2), BLOCK // 2), BLOCK // 2)
                ctx_ref[h, r, at, :] = fold(block)
                return 0

            lax.fori_loop(0, per, unsort, 0)
            if r:
                context.append(wire.send(ctx_ref.at[h, r], ctx_hbm.at[h, r], *near[r - 1][1]))
            else:
                saves.append(wire.keep(ctx_ref.at[h, 0], ctx_hbm.at[h, 0]))
        some = pl.ds(h * trees, trees)
        saves.append(wire.keep(ot_ref.at[some], ot_hbm.at[some]))
        saves.append(wire.keep(lse_ref.at[some], lse_hbm.at[some]))
    for copy in cored + context:
        copy.wait_recv()
    for copy in saves + late:
        copy.wait()
    wire.finish()


def anywhere(count):
    return [pl.BlockSpec(memory_space=pl.ANY)] * count


def vmem(count):
    return [pl.BlockSpec(memory_space=pltpu.VMEM)] * count


def smem():
    return pl.BlockSpec(memory_space=pltpu.SMEM)


def shape(dims, dtype):
    return jax.ShapeDtypeStruct(dims, dtype)


def copies_of(count_local, count_remote):
    return [
        pltpu.SemaphoreType.DMA((count_local,)),
        pltpu.SemaphoreType.DMA((count_remote,)),
        pltpu.SemaphoreType.DMA((count_remote,)),
    ]


def params(number):
    return pltpu.CompilerParams(
        vmem_limit_bytes=VMEM_LIMIT, collective_id=number, has_side_effects=True
    )


def start(parts, copies, heads, order, x, by, sa, sb):
    rows, width = x.shape
    total = parts * rows
    trees = total // TREE_TOK
    n = trees * heads
    tok = ((n, TREE_TOK, HEAD), HALF)
    turned = ((n, HEAD, TREE_TOK), HALF)
    near = ((total // BLOCK, BLOCK, width), HALF)
    ot = ((n, HEAD, TREE_TOK), SINGLE)
    lse = ((n, 1, TREE_TOK), SINGLE)
    ctx = ((heads, parts, rows // 2, 2 * HEAD), HALF)
    outs = [near, tok, tok, tok, turned, ot, lse, ctx]
    outs += [((parts,) + sa.shape, HALF), ((parts,) + sb.shape, HALF)]
    scratch = [near, (by.shape, HALF), tok, tok, tok, turned, turned, ot, lse]
    scratch += [((total // BLOCK, BLOCK, HEAD), HALF), ctx]
    return pl.pallas_call(
        functools.partial(start_kernel, parts, copies, heads),
        out_shape=[shape(*o) for o in outs],
        in_specs=[smem()] + anywhere(4),
        out_specs=anywhere(len(outs)),
        scratch_shapes=[pltpu.VMEM(*s) for s in scratch]
        + copies_of(9 + 3 * heads, 64 + (parts - 1) * 16),
        compiler_params=params(0),
        name="start",
    )(order, x.reshape(rows // BLOCK, BLOCK, width), by, sa, sb)


def middle_kernel(
    parts,
    copies,
    heads,
    tile,
    x_hbm,
    dy_hbm,
    ctx_hbm,
    wa_hbm,
    wb_hbm,
    vec_ref,
    out_hbm,
    dh1_hbm,
    do_hbm,
    pack_hbm,
    go_hbm,
    norm_ref,
    x_ref,
    dy_ref,
    ctx_ref,
    wo_ref,
    wh_ref,
    wp_ref,
    out_ref,
    dh1_ref,
    do_ref,
    pack_ref,
    go_ref,
    cat_ref,
    u_ref,
    df_ref,
    da_ref,
    g_ref,
    dz_ref,
    d_s,
    local_sem,
    send_sem,
    recv_sem,
    tile_sem,
    out_sem,
):
    wire = Wire(local_sem, send_sem, recv_sem)
    me, rep, near, core, layers, far = places(parts, copies)
    rows, width = x_ref.shape
    inner = wh_ref.shape[1]
    wide = heads * HEAD
    chunk = 512
    count = rows // tile
    loads = [
        wire.keep(ctx_hbm, ctx_ref),
        wire.keep(wa_hbm.at[:, pl.ds(3 * width, width)], wo_ref),
        wire.keep(x_hbm, x_ref),
        wire.keep(wa_hbm.at[:, pl.ds(4 * width, inner)], wh_ref),
        wire.keep(wb_hbm, wp_ref),
        wire.keep(dy_hbm, dy_ref),
    ]
    greet([p for _, p in near])
    gain1, bias1 = vec_ref[0:1, :], vec_ref[1:2, :]
    gain2, bias2 = vec_ref[2:3, :], vec_ref[3:4, :]
    norm_ref[...] = jnp.zeros_like(norm_ref)
    for copy in loads:
        copy.wait()

    def rows_out(i, at):
        return [
            pltpu.make_async_copy(out_ref.at[at], out_hbm.at[at], out_sem.at[2 * i]),
            pltpu.make_async_copy(dh1_ref.at[at], dh1_hbm.at[at], out_sem.at[2 * i + 1]),
        ]

    def rows_sent(i, at):
        return [
            pltpu.make_async_remote_copy(
                do_ref.at[r, at],
                do_hbm.at[r, at],
                tile_sem.at[0, i * parts + r],
                tile_sem.at[1, i * parts + r],
                device_id={p[0]: p[1]},
                device_id_type=MESH,
            )
            for r, p in near
        ] + [
            pltpu.make_async_copy(do_ref.at[0, at], do_hbm.at[0, at], tile_sem.at[0, i * parts])
        ]

    def tile_rows(i):
        return pl.ds(pl.multiple_of(i * tile, tile), tile)

    def tile_step(i, _):
        at = tile_rows(i)
        packed = pl.ds(pl.multiple_of(i * (tile // 2), tile // 2), tile // 2)
        ctx = jnp.concatenate(
            [
                unfold(ctx_ref[h, flip(me, c), packed, :])
                for c in range(parts)
                for h in range(heads)
            ],
            axis=-1,
        )
        cat_ref[at, :] = ctx
        h1 = x_ref[at, :].astype(SINGLE) + dot(ctx, wo_ref[...])
        c1 = h1 - row_mean(h1)
        r1 = lax.rsqrt(row_mean(c1 * c1) + 1e-5)
        n1 = c1 * r1
        y1 = n1 * gain1 + bias1
        u = y1.astype(HALF)
        u_ref[at, :] = u
        branch = 0.0
        for j in range(0, inner, chunk):
            s = slice(j, j + chunk)
            z = dot(u, wh_ref[:, s])
            cdf = 0.5 * (1.0 + lax.erf(z * 0.7071067811865476))
            pdf = jnp.exp2(z * z * (-0.5 * LOG2E)) * 0.3989422804014327
            g = (z * cdf).astype(HALF)
            g_ref[at, s] = g
            d_s[:, s] = cdf + z * pdf
            branch = branch + dot(g, wp_ref[s, :])
        h2 = y1 + branch
        c2 = h2 - row_mean(h2)
        r2 = lax.rsqrt(row_mean(c2 * c2) + 1e-5)
        n2 = c2 * r2
        out_ref[at, :] = (n2 * gain2 + bias2).astype(HALF)
        dy = dy_ref[at, :].astype(SINGLE)
        norm_ref[2:3, :] += jnp.sum(dy * n2, axis=0, keepdims=True)
        norm_ref[3:4, :] += jnp.sum(dy, axis=0, keepdims=True)
        dn2 = dy * gain2
        dh2 = r2 * (dn2 - row_mean(dn2) - n2 * row_mean(dn2 * n2))
        df = dh2.astype(HALF)
        df_ref[at, :] = df
        back = 0.0
        for j in range(0, inner, chunk):
            s = slice(j, j + chunk)
            dz = (dot(df, wp_ref[s, :], NT) * d_s[:, s]).astype(HALF)
            dz_ref[at, s] = dz
            back = back + dot(dz, wh_ref[:, s], NT)
        dy1 = dh2 + back
        norm_ref[0:1, :] += jnp.sum(dy1 * n1, axis=0, keepdims=True)
        norm_ref[1:2, :] += jnp.sum(dy1, axis=0, keepdims=True)
        dn1 = dy1 * gain1
        dh1 = r1 * (dn1 - row_mean(dn1) - n1 * row_mean(dn1 * n1))
        dh1_ref[at, :] = dh1
        da = dh1.astype(HALF)
        da_ref[at, :] = da
        dctx = dot(da, wo_ref[...], NT).astype(HALF)
        for c in range(parts):
            do_ref[flip(me, c), at, :] = dctx[:, c * wide : (c + 1) * wide]
        for copy in rows_out(i, at) + rows_sent(i, at):
            copy.start()
        return 0

    lax.fori_loop(0, count, tile_step, 0)
    depth = width // parts
    cols = inner // parts
    df_t = df_ref[...].T
    for j in range(parts):
        s = slice(j * cols, (j + 1) * cols)
        grad = dot(df_t, g_ref[:, s]).astype(HALF)
        unit = width // LAYERS
        for z in range(LAYERS):
            piece = grad[z * unit : (z + 1) * unit]
            if cols < width:
                piece = jnp.concatenate([piece[:depth], piece[depth:]], axis=1)
            pack_ref[1, flip(me, j), z] = piece
    u_t = u_ref[...].T
    for j in range(inner // width):
        s = slice(j * width, (j + 1) * width)
        grad = dot(u_t, dz_ref[:, s]).astype(HALF)
        for c in range(parts):
            pack_ref[0, flip(me, c), j] = grad[c * depth : (c + 1) * depth]
    saves = [wire.keep(pack_ref, pack_hbm)]
    grad = dot(cat_ref[...].T, da_ref[...]).astype(HALF)
    for c in range(parts):
        go_ref[flip(me, c)] = grad[c * depth : (c + 1) * depth]
    saves.append(wire.keep(go_ref, go_hbm))

    def tile_end(i, _):
        at = tile_rows(i)
        for copy in rows_out(i, at):
            copy.wait()
        sent = rows_sent(i, at)
        for copy in sent:
            copy.wait()
        return 0

    lax.fori_loop(0, count, tile_end, 0)
    for copy in saves:
        copy.wait()


def middle(parts, copies, heads, x, dy, ctx, wa, wb, vec):
    rows, width = x.shape
    inner = wb.shape[0]
    tile = PAIR if rows % PAIR == 0 else BLOCK
    depth = width // parts
    wide = heads * HEAD
    tok = ((rows, width), HALF)
    full = ((rows, width), SINGLE)
    do = ((parts, rows, wide), HALF)
    pack = ((2, parts, LAYERS, depth, width), HALF)
    go = ((parts, depth, width), HALF)
    big = ((rows, inner), HALF)
    outs = [tok, full, do, pack, go]
    scratch = [tok, tok, (ctx.shape, HALF), ((width, width), HALF), ((width, inner), HALF)]
    scratch += [((inner, width), HALF), tok, full, do, pack, go, tok, tok, tok, tok, big, big]
    scratch += [((tile, inner), SINGLE)]
    count = rows // tile
    return pl.pallas_call(
        functools.partial(middle_kernel, parts, copies, heads, tile),
        out_shape=[shape(*o) for o in outs] + [shape((4, width), SINGLE)],
        in_specs=anywhere(5) + vmem(1),
        out_specs=anywhere(len(outs)) + vmem(1),
        scratch_shapes=[pltpu.VMEM(*s) for s in scratch]
        + copies_of(8, 1)
        + [
            pltpu.SemaphoreType.DMA((2, count * parts)),
            pltpu.SemaphoreType.DMA((2 * count,)),
        ],
        compiler_params=params(1),
        name="middle",
    )(x, dy, ctx, wa, wb, vec)


def attend_back_tile(
    head, tree, trees, start, keys, order_ref, q_ref, k_ref, v_ref, kt_ref, ot_ref, lse_ref,
    do_ref, dq_s, dk_s, dv_s,
):
    here = slice(start, start + PAIR)
    base = tree * TREE_BLOCKS
    at = head * trees + tree
    grad = []
    for i in range(2):
        grad.append(do_ref[order_ref[tree * TREE_BLOCKS + start // BLOCK + i]])
    do = jnp.concatenate(grad, axis=0)[:, head * HEAD : (head + 1) * HEAD]
    delta = jnp.sum(do.astype(SINGLE).T * ot_ref[at, :, here], axis=0, keepdims=True)
    q = q_ref[at, here, :]
    lse = lse_ref[at, :, here]
    dq = 0.0
    for off, size, kind in keys:
        span = slice(off, off + size)
        out = slice(base + off // BLOCK, base + (off + size) // BLOCK)
        p = jnp.exp2(dot(k_ref[at, span, :], q, NT) * SCALE - lse)
        if kind:
            p = jnp.where(mask_of(kind), p, 0.0)
        dp = dot(v_ref[at, span, :], do, NT)
        ds = (p * (dp - delta)).astype(HALF)
        dv_s[out] += dot(p.astype(HALF), do).reshape(size // BLOCK, BLOCK, HEAD)
        dk_s[out] += dot(ds, q).reshape(size // BLOCK, BLOCK, HEAD)
        dq = dq + dot(kt_ref[at, :, span], ds)
    first = base + start // BLOCK
    dq_s[first : first + 2] = (dq * 0.125).T.reshape(2, BLOCK, HEAD)


def total_of(*refs):
    return functools.reduce(jnp.add, [r.astype(SINGLE) for r in refs])


def finish_kernel(
    parts,
    copies,
    heads,
    tile,
    order_ref,
    near_hbm,
    q_hbm,
    k_hbm,
    v_hbm,
    kt_hbm,
    ot_hbm,
    lse_hbm,
    do_hbm,
    dh1_hbm,
    wa_hbm,
    pack_hbm,
    go_hbm,
    norm_in,
    dx_hbm,
    gq_ref,
    gk_ref,
    gv_ref,
    go_out,
    gh_ref,
    gp_ref,
    norm_out,
    near_ref,
    q_ref,
    k_ref,
    v_ref,
    kt_ref,
    ot_ref,
    lse_ref,
    do_ref,
    dx_ref,
    wq_ref,
    dq_s,
    dk_s,
    dv_s,
    qk_ref,
    vv_ref,
    qk_in,
    vv_in,
    wqk_ref,
    wvv_ref,
    po_ref,
    pc_ref,
    fr_ref,
    fs_ref,
    zr_ref,
    fb_ref,
    far_ref,
    dws_ref,
    dwr_ref,
    dwc_ref,
    dwz_ref,
    dwf_ref,
    gor_ref,
    gos_ref,
    goc_ref,
    goz_ref,
    gof_ref,
    nsum_ref,
    nrecv_ref,
    local_sem,
    send_sem,
    recv_sem,
    out_sem,
):
    wire = Wire(local_sem, send_sem, recv_sem)
    me, rep, near, core, layers, far = places(parts, copies)
    blocks, _, width = near_ref.shape
    total = blocks * BLOCK
    rows = total // parts
    trees = total // TREE_TOK
    per = rows // BLOCK
    depth = width // parts
    side = lax.rem(rep, 2)
    layer = lax.rem(lax.div(rep, 2), LAYERS)
    other = 1 - side

    def load(source, target, head):
        some = pl.ds(head * trees, trees)
        return wire.keep(source.at[some], target.at[some])

    pairs = [
        (q_hbm, q_ref),
        (k_hbm, k_ref),
        (v_hbm, v_ref),
        (kt_hbm, kt_ref),
        (ot_hbm, ot_ref),
        (lse_hbm, lse_ref),
    ]
    loads = [[wire.keep(do_hbm, do_ref)] + [load(a, b, 0) for a, b in pairs]]
    greet([p for _, p in near] + [core] + [p for _, p in layers] + far)

    half_out = wire.send(pack_hbm.at[other], pc_ref, *core)
    half_own = wire.keep(pack_hbm.at[side], po_ref)
    go_own = wire.keep(go_hbm.at[0], gor_ref.at[0])
    go_sent = [wire.send(go_hbm.at[r], gor_ref.at[r], *p) for r, p in near]
    for h in range(1, heads):
        loads.append([load(a, b, h) for a, b in pairs])
    near_load = wire.keep(near_hbm, near_ref)
    weight_load = wire.keep(wa_hbm.at[:, pl.ds(0, 3 * width)], wq_ref)
    base_load = wire.keep(dh1_hbm, dx_ref)

    doubling = [core, layers[0][1], layers[1][1]] + far
    bit = 1
    while bit < parts:
        doubling.append(near[bit - 1][1])
        bit *= 2
    nsum_ref[0] = norm_in[...]
    state = {"step": 0, "copy": wire.send(nsum_ref.at[0], nrecv_ref.at[0], *doubling[0])}

    def norm_step():
        i = state["step"]
        if i == len(doubling):
            return
        state["copy"].wait_recv()
        nsum_ref[i + 1] = nsum_ref[i] + nrecv_ref[i]
        state["step"] = i = i + 1
        if i < len(doubling):
            state["copy"] = wire.send(nsum_ref.at[i], nrecv_ref.at[i], *doubling[i])

    def pack_group():
        half_out.wait_recv()
        half_own.wait()
        for r in range(parts):
            for z in range(LAYERS):
                po_ref[r, z] = total_of(po_ref[r, z], pc_ref[r, z]).astype(HALF)
        return [wire.send(po_ref.at[r], fr_ref.at[r - 1], *p) for r, p in near]

    def pack_scatter(waits):
        for copy in waits:
            copy.wait_recv()
        for z in range(LAYERS):
            fs_ref[z] = total_of(po_ref[0, z], *[fr_ref[r, z] for r in range(parts - 1)]).astype(
                HALF
            )
        return [wire.send(fs_ref.at[flip(layer, j)], zr_ref.at[j - 1], *p) for j, p in layers]

    def beyond(value, slot):
        for i, p in enumerate(far):
            send, recv = far_ref.at[slot, i, 0], far_ref.at[slot, i, 1]
            n, m = value.shape
            send[0:n, 0:m] = value.astype(HALF)
            copy = wire.send(send, recv, *p)
            copy.wait_recv()
            value = value.astype(HALF).astype(SINGLE) + recv[0:n, 0:m].astype(SINGLE)
        return value.astype(HALF)

    def pack_spread(waits):
        for copy in waits:
            copy.wait_recv()
        piece = total_of(fs_ref[layer], *[zr_ref[j] for j in range(LAYERS - 1)])
        fb_ref[side, layer] = beyond(piece, 0)
        return [
            wire.send(fb_ref.at[side, layer], fb_ref.at[side, layer], *p) for _, p in layers
        ]

    def pack_cores(waits):
        for copy in waits:
            copy.wait_recv()
        return [wire.send(fb_ref.at[side], fb_ref.at[side], *core)]

    def small_cores(waits):
        for copy in waits:
            copy.wait_recv()
        go_own.wait()
        piece = depth // SLICES
        go = total_of(*[gor_ref[r] for r in range(parts)]).astype(HALF)
        for i in range(SLICES):
            gos_ref[i] = go[i * piece : (i + 1) * piece]
        there = pl.ds(other * LAYERS, LAYERS)
        return [
            wire.send(dwr_ref.at[there], dwc_ref, *core),
            wire.send(gos_ref.at[there], goc_ref, *core),
        ]

    def small_scatter(waits):
        for copy in waits:
            copy.wait_recv()
        for z in range(LAYERS):
            p = side * LAYERS + z
            dwr_ref[p] = total_of(dwr_ref[p], dwc_ref[z]).astype(HALF)
            gos_ref[p] = total_of(gos_ref[p], goc_ref[z]).astype(HALF)
        out = []
        for j, p in layers:
            there = side * LAYERS + flip(layer, j)
            out.append(wire.send(dwr_ref.at[there], dwz_ref.at[j - 1], *p))
            out.append(wire.send(gos_ref.at[there], goz_ref.at[j - 1], *p))
        return out

    def small_spread(waits):
        for copy in waits:
            copy.wait_recv()
        p = side * LAYERS + layer
        dwf_ref[p] = beyond(total_of(dwr_ref[p], *[dwz_ref[j] for j in range(LAYERS - 1)]), 1)
        gof_ref[p] = beyond(total_of(gos_ref[p], *[goz_ref[j] for j in range(LAYERS - 1)]), 2)
        out = []
        for _, to in layers:
            out.append(wire.send(dwf_ref.at[p], dwf_ref.at[p], *to))
            out.append(wire.send(gof_ref.at[p], gof_ref.at[p], *to))
        return out

    def small_last(waits):
        for copy in waits:
            copy.wait_recv()
        here = pl.ds(side * LAYERS, LAYERS)
        return [
            wire.send(dwf_ref.at[here], dwf_ref.at[here], *core),
            wire.send(gof_ref.at[here], gof_ref.at[here], *core),
        ]

    def unsort(head):
        for r in range(parts):

            def one(j, _):
                place = order_ref[blocks + r * per + j]
                both = jnp.concatenate([dq_s[place], dk_s[place] * 0.125], axis=1)
                qk_ref[head, r, block_at(j), :] = both.astype(HALF)
                lower = pl.ds(pl.multiple_of(j * (BLOCK // 2), BLOCK // 2), BLOCK // 2)
                vv_ref[head, r, lower, :] = fold(dv_s[place]).astype(HALF)
                return 0

            lax.fori_loop(0, per, one, 0)
        out = []
        for r, p in near:
            out.append(wire.send(qk_ref.at[head, r], qk_in.at[head, r], *p))
            out.append(wire.send(vv_ref.at[head, r], vv_in.at[head, r], *p))
        return out

    def weight_grads(head):
        total_dw = 0.0
        for r in range(parts):
            grads = jnp.concatenate([qk_ref[head, r], unfold(vv_ref[head, r])], axis=1)
            total_dw = total_dw + dot(
                grads.T, near_ref[r * per : (r + 1) * per].reshape(rows, width)
            )
        dw = total_dw.astype(HALF)
        for c in range(parts):
            dws_ref[head * parts + flip(me, c)] = dw[:, c * depth : (c + 1) * depth]
        dwr_ref[head * parts] = dws_ref[head * parts]
        return [
            wire.send(dws_ref.at[head * parts + r], dwr_ref.at[head * parts + r], *p)
            for r, p in near
        ]

    def turn_weights():
        for h in range(heads):
            for c in range(parts):
                at = (c * heads + h) * HEAD
                wqk_ref[h, :, c * 2 * HEAD : (c + 1) * 2 * HEAD] = jnp.concatenate(
                    [wq_ref[:, at : at + HEAD], wq_ref[:, width + at : width + at + HEAD]], axis=1
                )
                wvv_ref[h, :, c * HEAD : (c + 1) * HEAD] = wq_ref[
                    :, 2 * width + at : 2 * width + at + HEAD
                ]

    def input_grad(head, last):
        def step(i, _):
            at = pl.ds(pl.multiple_of(i * tile, tile), tile)
            lower = pl.ds(pl.multiple_of(i * (tile // 2), tile // 2), tile // 2)
            qk = jnp.concatenate([pick(qk_in, c, at) for c in range(parts)], axis=1)
            vv = jnp.concatenate([unfold(pick(vv_in, c, lower)) for c in range(parts)], axis=1)
            dx_ref[at, :] += dot(qk, wqk_ref[head], NT) + dot(vv, wvv_ref[head], NT)
            if last:
                pltpu.make_async_copy(dx_ref.at[at], dx_hbm.at[at], out_sem.at[i]).start()
            return 0

        def pick(ref, c, at):
            return ref[head, flip(me, c), at, :]

        lax.fori_loop(0, rows // tile, step, 0)

    def keep_own(head):
        qk_in[head, 0] = qk_ref[head, 0]
        vv_in[head, 0] = vv_ref[head, 0]

    group = scatter = spread = cores = None
    grads, weights = [], []
    for h in range(heads):
        for copy in loads[h]:
            copy.wait()
        dk_s[...] = jnp.zeros_like(dk_s)
        dv_s[...] = jnp.zeros_like(dv_s)
        for number, (begin, keys) in enumerate(tile_list()):
            for tree in range(trees):
                attend_back_tile(
                    h, tree, trees, begin, keys, order_ref, q_ref, k_ref, v_ref, kt_ref, ot_ref,
                    lse_ref, do_ref, dq_s, dk_s, dv_s,
                )
            if h == 0 and number == 5:
                group = pack_group()
            elif h == 0 and number in (2, 4, 8) or h and number % 2 == 0:
                norm_step()
        grads.append(unsort(h))
        keep_own(h)
        if h == 0:
            near_load.wait()
        weights += weight_grads(h)
    while state["step"] < len(doubling):
        norm_step()
    scatter = pack_scatter(group)
    small = small_cores(weights + go_sent)
    weight_load.wait()
    base_load.wait()
    turn_weights()
    for copy in grads[0]:
        copy.wait_recv()
    small = small_scatter(small)
    if heads > 1:
        input_grad(0, False)
    spread = pack_spread(scatter)
    small = small_spread(small)
    for copy in grads[-1]:
        copy.wait_recv()
    input_grad(heads - 1, True)
    cores = pack_cores(spread)
    small = small_last(small)

    for copy in cores + small:
        copy.wait_recv()
    norm_out[...] = nsum_ref[len(doubling)]
    for j in range(LAYERS):
        gh_ref[:, j * width : (j + 1) * width] = fb_ref[0, j].astype(SINGLE)
        piece = fb_ref[1, j].astype(SINGLE)
        cols = gp_ref.shape[0]
        if cols < width:
            piece = jnp.concatenate([piece[:, :cols], piece[:, cols:]], axis=0)
        unit = width // LAYERS
        gp_ref[:, j * unit : (j + 1) * unit] = piece.T
    piece = depth // SLICES
    for i in range(SLICES):
        go_out[i * piece : (i + 1) * piece, :] = gof_ref[i].astype(SINGLE)
    for c in range(parts):
        for h in range(heads):
            turned = dwf_ref[h * parts + flip(me, c)].astype(SINGLE).T
            at = (c * heads + h) * HEAD
            for ref, k in ((gq_ref, 0), (gk_ref, 1), (gv_ref, 2)):
                ref[:, at : at + HEAD] = turned[:, k * HEAD : (k + 1) * HEAD]

    def end(i, _):
        at = pl.ds(pl.multiple_of(i * tile, tile), tile)
        pltpu.make_async_copy(dx_ref.at[at], dx_hbm.at[at], out_sem.at[i]).wait()
        return 0

    lax.fori_loop(0, rows // tile, end, 0)
    wire.finish()


def finish(parts, copies, heads, order, saved, do, dh1, wa, pack, go, norms):
    near, q, k, v, kt, ot, lse = saved
    blocks, _, width = near.shape
    total = blocks * BLOCK
    rows = total // parts
    depth = width // parts
    inner = wa.shape[1] - 4 * width
    tile = PAIR if rows % PAIR == 0 else BLOCK
    piece = depth // SLICES
    beyonds = max(copies // (2 * LAYERS), 2).bit_length() - 1
    stages = (copies * parts).bit_length()
    flat = ((blocks, BLOCK, HEAD), SINGLE)
    qk = ((heads, parts, rows, 2 * HEAD), HALF)
    vv = ((heads, parts, rows // 2, 2 * HEAD), HALF)
    units = ((parts, LAYERS, depth, width), HALF)
    dws = ((SLICES, 3 * HEAD, depth), HALF)
    gos = ((SLICES, piece, width), HALF)
    scratch = [(a.shape, a.dtype) for a in (near, q, k, v, kt, ot, lse, do)]
    scratch += [((rows, width), SINGLE), ((width, 3 * width), HALF), flat, flat, flat]
    scratch += [qk, vv, qk, vv]
    scratch += [((heads, width, 2 * HEAD * parts), HALF), ((heads, width, HEAD * parts), HALF)]
    scratch += [units, units, ((parts - 1,) + units[0][1:], HALF), (units[0][1:], HALF)]
    scratch += [((LAYERS - 1, depth, width), HALF), ((2, LAYERS, depth, width), HALF)]
    scratch += [((3, beyonds, 2, max(3 * HEAD, depth), width), HALF)]
    scratch += [dws, dws, ((LAYERS, 3 * HEAD, depth), HALF), ((LAYERS - 1, 3 * HEAD, depth), HALF)]
    scratch += [dws, (go.shape, HALF), gos, ((LAYERS, piece, width), HALF)]
    scratch += [((LAYERS - 1, piece, width), HALF), gos]
    scratch += [((stages, 4, width), SINGLE), ((stages, 4, width), SINGLE)]
    square = ((depth, width), SINGLE)
    outs = [square] * 4 + [((depth, inner), SINGLE), ((inner // parts, width), SINGLE)]
    outs += [((4, width), SINGLE)]
    return pl.pallas_call(
        functools.partial(finish_kernel, parts, copies, heads, tile),
        out_shape=[shape((rows, width), SINGLE)] + [shape(*o) for o in outs],
        in_specs=[smem()] + anywhere(12) + vmem(1),
        out_specs=anywhere(1) + vmem(len(outs)),
        scratch_shapes=[pltpu.VMEM(*s) for s in scratch]
        + copies_of(8 + 6 * heads, 48 + 12 * parts)
        + [pltpu.SemaphoreType.DMA((rows // tile,))],
        compiler_params=params(2),
        name="finish",
    )(order, near, q, k, v, kt, ot, lse, do, dh1, wa, pack, go, norms)


def shards(
    parts,
    copies,
    inputs,
    cotangent,
    segments,
    trees,
    parents,
    w_query,
    w_key,
    w_value,
    w_out,
    w_hidden,
    w_proj,
    norm1_gain,
    norm1_bias,
    norm2_gain,
    norm2_bias,
):
    x = inputs[0]
    rows, width = x.shape
    inner = w_hidden.shape[1]
    heads = HEADS // parts
    wide = heads * HEAD
    depth = width // parts
    me = lax.axis_index("fsdp")
    order = block_order(segments[0], trees[0], parents[0], rows, me)
    by = jnp.concatenate([w.reshape(depth, parts, wide) for w in (w_query, w_key, w_value)], axis=2)
    by = by.transpose(1, 0, 2)
    sa = jnp.concatenate([w_query, w_key, w_value, w_out, w_hidden], axis=1)
    sa = sa.reshape(SLICES, depth // SLICES, 4 * width + inner)
    sb = w_proj.reshape(SLICES, inner // parts // SLICES, width)
    near, q, k, v, kt, ot, lse, ctx, wa, wb = start(parts, copies, heads, order, x, by, sa, sb)
    wa = wa.reshape(width, 4 * width + inner)
    wb = wb.reshape(inner, width)
    vec = jnp.stack([norm1_gain, norm1_bias, norm2_gain, norm2_bias])
    output, dh1, do, pack, go, norms = middle(
        parts, copies, heads, x, cotangent[0], ctx, wa, wb, vec
    )
    saved = (near, q, k, v, kt, ot, lse)
    input_grad, gq, gk, gv, go, gh, gp, norms = finish(
        parts, copies, heads, order, saved, do.reshape(-1, BLOCK, wide), dh1, wa, pack, go, norms
    )
    return (
        output[None],
        input_grad[None],
        gq,
        gk,
        gv,
        go,
        gh,
        gp,
        norms[0],
        norms[1],
        norms[2],
        norms[3],
    )


def solution(mesh):
    token = P("rep", "fsdp", None)
    weight = P("fsdp", None)
    placed = (token, token, P("rep", None), P("rep", None), P("rep", None, None))
    return jax.shard_map(
        functools.partial(shards, mesh.shape["fsdp"], mesh.shape["rep"]),
        mesh=mesh,
        in_specs=placed + (weight,) * 6 + (P(),) * 4,
        out_specs=(token, token) + (weight,) * 6 + (P(),) * 4,
        check_vma=False,
    )
```

```python
import functools

import jax
import jax.numpy as jnp
from jax import lax
from jax.experimental import pallas as pl
from jax.experimental.pallas import tpu as pltpu
from jax.sharding import PartitionSpec as P

HEADS = 8
HEAD = 64
BLOCK = 128
PAIR = 2 * BLOCK
TRUNK = 8
BRANCHES = 4
LEAVES = 8
TREE_BLOCKS = TRUNK + BRANCHES + LEAVES
TREE_TOK = TREE_BLOCKS * BLOCK
SINGLE = jnp.float32
HALF = jnp.bfloat16
NN = (((1,), (0,)), ((), ()))
NT = (((1,), (1,)), ((), ()))
LOG2E = 1.4426950408889634
SCALE = 0.125 * LOG2E
VMEM_LIMIT = 58 << 20
MESH = pl.DeviceIdType.MESH
SLICES = 8
LAYERS = 4


def dot(left, right, dims=NN):
    return lax.dot_general(left, right, dims, preferred_element_type=SINGLE)


def row_mean(values):
    return jnp.mean(values, axis=-1, keepdims=True)


def block_order(segments, trees, parents, rows, me):
    seg = segments.reshape(-1, BLOCK)[:, 0]
    tree = trees.reshape(-1, BLOCK)[:, 0]
    count = seg.shape[0]
    table = parents.reshape(-1)
    slot = tree * parents.shape[1] + seg
    parent = jnp.sum(
        jnp.where(slot[:, None] == jnp.arange(table.shape[0])[None, :], table[None, :], 0), axis=1
    )
    place = jnp.arange(count, dtype=jnp.int32)
    kind = jnp.where(seg == 0, 0, jnp.where(seg <= BRANCHES, seg, 16 * parent + seg))
    key = (tree * 256 + kind) * 64 + place
    rank = jnp.sum((key[None, :] < key[:, None]).astype(jnp.int32), axis=1)
    per = rows // BLOCK
    near = ((place // per) ^ me) * per + place % per
    order = jnp.sum(jnp.where(rank[None, :] == place[:, None], near[None, :], 0), axis=1)
    back = jnp.sum(jnp.where(near[None, :] == place[:, None], rank[None, :], 0), axis=1)
    return jnp.concatenate([order, back]).astype(jnp.int32)


def tile_list():
    out = []
    trunk = TRUNK * BLOCK
    for start in range(0, trunk, PAIR):
        keys = [(0, start, None)] if start else []
        out.append((start, keys + [(start, PAIR, "causal")]))
    for pair in range(BRANCHES // 2):
        start = trunk + pair * PAIR
        out.append((start, [(0, trunk, None), (start, PAIR, "own")]))
    for branch in range(BRANCHES):
        start = trunk + BRANCHES * BLOCK + branch * PAIR
        out.append(
            (
                start,
                [(0, trunk, None), (trunk + branch * BLOCK, BLOCK, None), (start, PAIR, "own")],
            )
        )
    return out


def mask_of(kind):
    key = lax.broadcasted_iota(jnp.int32, (PAIR, PAIR), 0)
    query = lax.broadcasted_iota(jnp.int32, (PAIR, PAIR), 1)
    mask = key <= query
    if kind == "own":
        mask = mask & ((key >= BLOCK) == (query >= BLOCK))
    return mask


def flip(value, bits):
    bit = 1
    while bit <= bits:
        if bits & bit:
            value = value + bit - 2 * bit * lax.rem(lax.div(value, bit), 2)
        bit *= 2
    return value


def flip_two(one, two, size):
    out = 0
    bit = 1
    while bit < size:
        out = out + bit * lax.rem(lax.rem(lax.div(one, bit), 2) + lax.rem(lax.div(two, bit), 2), 2)
        bit *= 2
    return out


class Wire:
    def __init__(self, local_sem, send_sem, recv_sem):
        self.local_sem, self.send_sem, self.recv_sem = local_sem, send_sem, recv_sem
        self.locals = self.remotes = 0
        self.open = []

    def keep(self, source, target):
        copy = pltpu.make_async_copy(source, target, self.local_sem.at[self.locals])
        self.locals += 1
        copy.start()
        return copy

    def send(self, source, target, axis, peer):
        copy = pltpu.make_async_remote_copy(
            source,
            target,
            self.send_sem.at[self.remotes],
            self.recv_sem.at[self.remotes],
            device_id={axis: peer},
            device_id_type=MESH,
        )
        self.remotes += 1
        copy.start()
        self.open.append(copy)
        return copy

    def finish(self):
        for copy in self.open:
            copy.wait_send()


def greet(peers):
    barrier = pltpu.get_barrier_semaphore()
    for axis, peer in peers:
        pl.semaphore_signal(barrier, inc=1, device_id={axis: peer}, device_id_type=MESH)
    pl.semaphore_wait(barrier, len(peers))


def places(parts, copies):
    me = lax.axis_index("fsdp")
    rep = lax.axis_index("rep")
    near = [(r, ("fsdp", flip(me, r))) for r in range(1, parts)]
    core = ("rep", flip(rep, 1))
    layers = [(j, ("rep", flip(rep, 2 * j))) for j in range(1, LAYERS)]
    far = []
    bit = 2 * LAYERS
    while bit < copies:
        far.append(("rep", flip(rep, bit)))
        bit *= 2
    return me, rep, near, core, layers, far


def picks(order_ref, tree, start, size):
    first = tree * TREE_BLOCKS + start // BLOCK
    return [order_ref[first + i] for i in range(size // BLOCK)]


def stack(ref, head, chosen, axis):
    blocks = [ref[head][i] for i in chosen]
    return jnp.concatenate(blocks, axis=axis) if len(blocks) > 1 else blocks[0]


def attend_head(head, trees, order_ref, q_ref, k_ref, vt_ref, ot_ref, lse_ref, flat_ref):
    for start, keys in tile_list():
        here = slice(start, start + PAIR)
        for tree in range(trees):
            at = head * trees + tree
            q = stack(q_ref, head, picks(order_ref, tree, start, PAIR), 0)
            scores = []
            for off, size, kind in keys:
                s = dot(stack(k_ref, head, picks(order_ref, tree, off, size), 0), q, NT)
                if kind:
                    s = jnp.where(mask_of(kind), s, -1e30)
                scores.append(s)
            top = functools.reduce(
                jnp.maximum, [jnp.max(s, axis=0, keepdims=True) for s in scores]
            )
            top = top * SCALE
            mass = 0.0
            acc = 0.0
            for (off, size, _), s in zip(keys, scores):
                e = jnp.exp2(s * SCALE - top)
                mass = mass + jnp.sum(e, axis=0, keepdims=True)
                vt = stack(vt_ref, head, picks(order_ref, tree, off, size), 1)
                acc = acc + dot(vt, e.astype(HALF))
            out = acc * (1.0 / mass)
            lse_ref[at, :, here] = top + jnp.log2(mass)
            ot_ref[at, :, here] = out
            place = tree * TREE_BLOCKS + start // BLOCK
            flat_ref[place : place + 2] = out.T.astype(HALF).reshape(2, BLOCK, HEAD)


def fold(block):
    return jnp.concatenate([block[: BLOCK // 2], block[BLOCK // 2 :]], axis=1)


def unfold(packed):
    parts = []
    for i in range(packed.shape[0] // (BLOCK // 2)):
        piece = packed[i * (BLOCK // 2) : (i + 1) * (BLOCK // 2)]
        parts += [piece[:, :HEAD], piece[:, HEAD:]]
    return jnp.concatenate(parts, axis=0)


def block_at(index):
    return pl.ds(pl.multiple_of(index * BLOCK, BLOCK), BLOCK)


def start_kernel(
    parts,
    copies,
    heads,
    order_ref,
    x_hbm,
    by_hbm,
    sa_hbm,
    sb_hbm,
    near_hbm,
    q_hbm,
    k_hbm,
    v_hbm,
    kt_hbm,
    ot_hbm,
    lse_hbm,
    ctx_hbm,
    wa_hbm,
    wb_hbm,
    near_ref,
    own_ref,
    q_ref,
    k_ref,
    v_ref,
    kt_ref,
    vt_ref,
    ot_ref,
    lse_ref,
    flat_ref,
    ctx_ref,
    local_sem,
    send_sem,
    recv_sem,
):
    wire = Wire(local_sem, send_sem, recv_sem)
    me, rep, near, core, layers, far = places(parts, copies)
    per = x_hbm.shape[0]
    blocks = parts * per
    trees = blocks // TREE_BLOCKS
    wide = heads * HEAD
    greet([p for _, p in near] + [core] + [p for _, p in layers])

    side = lax.rem(rep, 2)
    layer = lax.rem(lax.div(rep, 2), LAYERS)
    mine = side * LAYERS + layer
    kept = [
        wire.keep(by_hbm.at[me], own_ref.at[me]),
        wire.keep(x_hbm, near_ref.at[pl.ds(0, per)]),
    ]
    own_copies = [wire.send(by_hbm.at[p[1]], own_ref.at[me], *p) for _, p in near]
    first = []
    for r, p in near:
        first.append(wire.send(sa_hbm.at[mine], wa_hbm.at[me, mine], *p))
        first.append(wire.send(sb_hbm.at[mine], wb_hbm.at[me, mine], *p))
    late = [wire.keep(sa_hbm, wa_hbm.at[me]), wire.keep(sb_hbm, wb_hbm.at[me])]

    def second():
        for copy in first:
            copy.wait_recv()
        out = []
        for _, p in layers:
            for r in range(1, parts):
                c = flip(me, r)
                out.append(wire.send(wa_hbm.at[c, mine], wa_hbm.at[c, mine], *p))
                out.append(wire.send(wb_hbm.at[c, mine], wb_hbm.at[c, mine], *p))
        return out

    def third(copies_in):
        for copy in copies_in:
            copy.wait_recv()
        out = []
        half = pl.ds(side * LAYERS, LAYERS)
        for r in range(1, parts):
            c = flip(me, r)
            out.append(wire.send(wa_hbm.at[c, half], wa_hbm.at[c, half], *core))
            out.append(wire.send(wb_hbm.at[c, half], wb_hbm.at[c, half], *core))
        return out

    def project(first, count):
        weight = own_ref[...].reshape(parts * own_ref.shape[1], 3 * wide)
        x = near_ref[first : first + count].reshape(count * BLOCK, near_ref.shape[2])
        out = dot(x, weight).astype(HALF)
        for i in range(count):
            block = out[i * BLOCK : (i + 1) * BLOCK]
            kt = block[:, wide : 2 * wide].T
            vt = block[:, 2 * wide :].T
            for h in range(heads):
                cols = slice(h * HEAD, (h + 1) * HEAD)
                q_ref[h, first + i] = block[:, cols]
                k_ref[h, first + i] = block[:, wide:][:, cols]
                v_ref[h, first + i] = block[:, 2 * wide :][:, cols]
                kt_ref[h, first + i] = kt[cols]
                vt_ref[h, first + i] = vt[cols]

    def wait_all(copies_in):
        for copy in copies_in:
            copy.wait_recv()

    if parts == 4:
        cuts = [i * per // 4 for i in range(5)]

        def part(chunk, i):
            return pl.ds(chunk * per + cuts[i], cuts[i + 1] - cuts[i])

        (_, px), (_, py), _ = near
        one, two = {}, {}
        for a, b in zip((0, 1, 2, 3), (2, 3, 0, 1)):
            one[a] = wire.send(x_hbm.at[part(0, a)], near_ref.at[part(1, a)], *px)
            two[b] = wire.send(x_hbm.at[part(0, b)], near_ref.at[part(2, b)], *py)
        three = {}
        for a, b in ((0, 2), (1, 3)):
            one[a].wait_recv()
            three[a] = wire.send(near_ref.at[part(1, a)], near_ref.at[part(3, a)], *py)
            two[b].wait_recv()
            three[b] = wire.send(near_ref.at[part(2, b)], near_ref.at[part(3, b)], *px)
            if a == 0:
                layered = second()
                for copy in kept:
                    copy.wait()
                wait_all(own_copies)
                project(0, per)
        wait_all([one[2], one[3]])
        project(per, per)
        wait_all([two[0], two[1]])
        project(2 * per, per)
        wait_all([three[0], three[2]])
        project(3 * per, cuts[1])
        project(3 * per + cuts[2], cuts[3] - cuts[2])
        wait_all([three[1], three[3]])
        project(3 * per + cuts[1], cuts[2] - cuts[1])
        project(3 * per + cuts[3], cuts[4] - cuts[3])
    else:
        waits = [wire.send(x_hbm, near_ref.at[pl.ds(r * per, per)], *p) for r, p in near]
        layered = second()
        for copy in kept:
            copy.wait()
        wait_all(own_copies + waits)
        for r in range(parts):
            project(r * per, per)
    saves = [wire.keep(near_ref, near_hbm)]
    cored = third(layered)
    saves += [
        wire.keep(a, b)
        for a, b in ((q_ref, q_hbm), (k_ref, k_hbm), (v_ref, v_hbm), (kt_ref, kt_hbm))
    ]
    context = []
    for h in range(heads):
        views = [[ref.at[i] for i in range(heads)] for ref in (q_ref, k_ref, vt_ref)]
        attend_head(h, trees, order_ref, *views, ot_ref, lse_ref, flat_ref)
        for r in range(parts):

            def unsort(j, _):
                block = flat_ref[order_ref[blocks + r * per + j]]
                at = pl.ds(pl.multiple_of(j * (BLOCK // 2), BLOCK // 2), BLOCK // 2)
                ctx_ref[h, r, at, :] = fold(block)
                return 0

            lax.fori_loop(0, per, unsort, 0)
            if r:
                context.append(wire.send(ctx_ref.at[h, r], ctx_hbm.at[h, r], *near[r - 1][1]))
            else:
                saves.append(wire.keep(ctx_ref.at[h, 0], ctx_hbm.at[h, 0]))
        some = pl.ds(h * trees, trees)
        saves.append(wire.keep(ot_ref.at[some], ot_hbm.at[some]))
        saves.append(wire.keep(lse_ref.at[some], lse_hbm.at[some]))
    for copy in cored + context:
        copy.wait_recv()
    for copy in saves + late:
        copy.wait()
    wire.finish()


def anywhere(count):
    return [pl.BlockSpec(memory_space=pl.ANY)] * count


def vmem(count):
    return [pl.BlockSpec(memory_space=pltpu.VMEM)] * count


def smem():
    return pl.BlockSpec(memory_space=pltpu.SMEM)


def shape(dims, dtype):
    return jax.ShapeDtypeStruct(dims, dtype)


def copies_of(count_local, count_remote):
    return [
        pltpu.SemaphoreType.DMA((count_local,)),
        pltpu.SemaphoreType.DMA((count_remote,)),
        pltpu.SemaphoreType.DMA((count_remote,)),
    ]


def params(number):
    return pltpu.CompilerParams(
        vmem_limit_bytes=VMEM_LIMIT, collective_id=number, has_side_effects=True
    )


def start(parts, copies, heads, order, x, by, sa, sb):
    rows, width = x.shape
    total = parts * rows
    trees = total // TREE_TOK
    n = trees * heads
    tok = ((heads, total // BLOCK, BLOCK, HEAD), HALF)
    turned = ((heads, total // BLOCK, HEAD, BLOCK), HALF)
    near = ((total // BLOCK, BLOCK, width), HALF)
    ot = ((n, HEAD, TREE_TOK), SINGLE)
    lse = ((n, 1, TREE_TOK), SINGLE)
    ctx = ((heads, parts, rows // 2, 2 * HEAD), HALF)
    outs = [near, tok, tok, tok, turned, ot, lse, ctx]
    outs += [((parts,) + sa.shape, HALF), ((parts,) + sb.shape, HALF)]
    scratch = [near, (by.shape, HALF), tok, tok, tok, turned, turned, ot, lse]
    scratch += [((total // BLOCK, BLOCK, HEAD), HALF), ctx]
    return pl.pallas_call(
        functools.partial(start_kernel, parts, copies, heads),
        out_shape=[shape(*o) for o in outs],
        in_specs=[smem()] + anywhere(4),
        out_specs=anywhere(len(outs)),
        scratch_shapes=[pltpu.VMEM(*s) for s in scratch]
        + copies_of(9 + 3 * heads, 64 + (parts - 1) * 16),
        compiler_params=params(0),
        name="start",
    )(order, x.reshape(rows // BLOCK, BLOCK, width), by, sa, sb)


def middle_kernel(
    parts,
    copies,
    heads,
    tile,
    x_hbm,
    dy_hbm,
    ctx_hbm,
    wa_hbm,
    wb_hbm,
    vec_ref,
    out_hbm,
    dh1_hbm,
    do_hbm,
    pa_hbm,
    pb_hbm,
    norm_ref,
    x_ref,
    dy_ref,
    ctx_ref,
    wo_ref,
    wh_ref,
    wp_ref,
    out_ref,
    dh1_ref,
    do_ref,
    pa_ref,
    pb_ref,
    cat_ref,
    u_ref,
    df_ref,
    da_ref,
    g_ref,
    dz_ref,
    d_s,
    local_sem,
    send_sem,
    recv_sem,
    tile_sem,
    out_sem,
):
    wire = Wire(local_sem, send_sem, recv_sem)
    me, rep, near, core, layers, far = places(parts, copies)
    rows, width = x_ref.shape
    inner = wh_ref.shape[1]
    wide = heads * HEAD
    chunk = 512
    count = rows // tile
    loads = [
        wire.keep(ctx_hbm, ctx_ref),
        wire.keep(wa_hbm.at[:, pl.ds(3 * width, width)], wo_ref),
        wire.keep(x_hbm, x_ref),
        wire.keep(wa_hbm.at[:, pl.ds(4 * width, inner)], wh_ref),
        wire.keep(wb_hbm, wp_ref),
        wire.keep(dy_hbm, dy_ref),
    ]
    greet([p for _, p in near])
    gain1, bias1 = vec_ref[0:1, :], vec_ref[1:2, :]
    gain2, bias2 = vec_ref[2:3, :], vec_ref[3:4, :]
    norm_ref[...] = jnp.zeros_like(norm_ref)
    for copy in loads:
        copy.wait()

    def rows_out(i, at):
        return [
            pltpu.make_async_copy(out_ref.at[at], out_hbm.at[at], out_sem.at[2 * i]),
            pltpu.make_async_copy(dh1_ref.at[at], dh1_hbm.at[at], out_sem.at[2 * i + 1]),
        ]

    def rows_sent(i, at):
        return [
            pltpu.make_async_remote_copy(
                do_ref.at[r, at],
                do_hbm.at[r, at],
                tile_sem.at[0, i * parts + r],
                tile_sem.at[1, i * parts + r],
                device_id={p[0]: p[1]},
                device_id_type=MESH,
            )
            for r, p in near
        ] + [
            pltpu.make_async_copy(do_ref.at[0, at], do_hbm.at[0, at], tile_sem.at[0, i * parts])
        ]

    def tile_rows(i):
        return pl.ds(pl.multiple_of(i * tile, tile), tile)

    def tile_step(i, _):
        at = tile_rows(i)
        packed = pl.ds(pl.multiple_of(i * (tile // 2), tile // 2), tile // 2)
        ctx = jnp.concatenate(
            [
                unfold(ctx_ref[h, flip(me, c), packed, :])
                for c in range(parts)
                for h in range(heads)
            ],
            axis=-1,
        )
        cat_ref[at, :] = ctx
        h1 = x_ref[at, :].astype(SINGLE) + dot(ctx, wo_ref[...])
        c1 = h1 - row_mean(h1)
        r1 = lax.rsqrt(row_mean(c1 * c1) + 1e-5)
        n1 = c1 * r1
        y1 = n1 * gain1 + bias1
        u = y1.astype(HALF)
        u_ref[at, :] = u
        branch = 0.0
        for j in range(0, inner, chunk):
            s = slice(j, j + chunk)
            z = dot(u, wh_ref[:, s])
            cdf = 0.5 * (1.0 + lax.erf(z * 0.7071067811865476))
            pdf = jnp.exp2(z * z * (-0.5 * LOG2E)) * 0.3989422804014327
            g = (z * cdf).astype(HALF)
            g_ref[at, s] = g
            d_s[:, s] = cdf + z * pdf
            branch = branch + dot(g, wp_ref[s, :])
        h2 = y1 + branch
        c2 = h2 - row_mean(h2)
        r2 = lax.rsqrt(row_mean(c2 * c2) + 1e-5)
        n2 = c2 * r2
        out_ref[at, :] = (n2 * gain2 + bias2).astype(HALF)
        dy = dy_ref[at, :].astype(SINGLE)
        norm_ref[2:3, :] += jnp.sum(dy * n2, axis=0, keepdims=True)
        norm_ref[3:4, :] += jnp.sum(dy, axis=0, keepdims=True)
        dn2 = dy * gain2
        dh2 = r2 * (dn2 - row_mean(dn2) - n2 * row_mean(dn2 * n2))
        df = dh2.astype(HALF)
        df_ref[at, :] = df
        back = 0.0
        for j in range(0, inner, chunk):
            s = slice(j, j + chunk)
            dz = (dot(df, wp_ref[s, :], NT) * d_s[:, s]).astype(HALF)
            dz_ref[at, s] = dz
            back = back + dot(dz, wh_ref[:, s], NT)
        dy1 = dh2 + back
        norm_ref[0:1, :] += jnp.sum(dy1 * n1, axis=0, keepdims=True)
        norm_ref[1:2, :] += jnp.sum(dy1, axis=0, keepdims=True)
        dn1 = dy1 * gain1
        dh1 = r1 * (dn1 - row_mean(dn1) - n1 * row_mean(dn1 * n1))
        dh1_ref[at, :] = dh1
        da = dh1.astype(HALF)
        da_ref[at, :] = da
        dctx = dot(da, wo_ref[...], NT).astype(HALF)
        for c in range(parts):
            do_ref[flip(me, c), at, :] = dctx[:, c * wide : (c + 1) * wide]
        for copy in rows_out(i, at) + rows_sent(i, at):
            copy.start()
        return 0

    lax.fori_loop(0, count, tile_step, 0)
    depth = width // parts
    cols = inner // parts
    low = depth // 2
    unit = width // LAYERS
    small = depth // SLICES

    def put(side, c, z, piece):
        to = flip(me, c)
        pa_ref[side, to, z, 0:low] = piece[:low]
        pb_ref[side, z, to] = piece[low:]

    df_t = df_ref[...].T
    for c in range(parts):
        grad = dot(df_t, g_ref[:, c * cols : (c + 1) * cols]).astype(HALF)
        for z in range(LAYERS):
            piece = grad[z * unit : (z + 1) * unit]
            if cols < width:
                piece = jnp.concatenate([piece[:depth], piece[depth:]], axis=1)
            put(1, c, z, piece)
    u_t = u_ref[...].T
    for z in range(LAYERS):
        grad = dot(u_t, dz_ref[:, z * width : (z + 1) * width]).astype(HALF)
        for c in range(parts):
            put(0, c, z, grad[c * depth : (c + 1) * depth])
    grad = dot(cat_ref[...].T, da_ref[...]).astype(HALF)
    for c in range(parts):
        for side in range(2):
            for z in range(LAYERS):
                at = c * depth + (side * LAYERS + z) * small
                pa_ref[side, flip(me, c), z, low : low + small] = grad[at : at + small]
    saves = [wire.keep(pa_ref, pa_hbm), wire.keep(pb_ref, pb_hbm)]

    def tile_end(i, _):
        at = tile_rows(i)
        for copy in rows_out(i, at):
            copy.wait()
        sent = rows_sent(i, at)
        for copy in sent:
            copy.wait()
        return 0

    lax.fori_loop(0, count, tile_end, 0)
    for copy in saves:
        copy.wait()


def middle(parts, copies, heads, x, dy, ctx, wa, wb, vec):
    rows, width = x.shape
    inner = wb.shape[0]
    tile = PAIR if rows % PAIR == 0 else BLOCK
    depth = width // parts
    wide = heads * HEAD
    tok = ((rows, width), HALF)
    full = ((rows, width), SINGLE)
    do = ((parts, rows, wide), HALF)
    pack = ((2, parts, LAYERS, depth // 2 + depth // SLICES, width), HALF)
    pack_b = ((2, LAYERS, parts, depth // 2, width), HALF)
    big = ((rows, inner), HALF)
    outs = [tok, full, do, pack, pack_b]
    scratch = [tok, tok, (ctx.shape, HALF), ((width, width), HALF), ((width, inner), HALF)]
    scratch += [((inner, width), HALF), tok, full, do, pack, pack_b, tok, tok, tok, tok, big, big]
    scratch += [((tile, inner), SINGLE)]
    count = rows // tile
    return pl.pallas_call(
        functools.partial(middle_kernel, parts, copies, heads, tile),
        out_shape=[shape(*o) for o in outs] + [shape((4, width), SINGLE)],
        in_specs=anywhere(5) + vmem(1),
        out_specs=anywhere(len(outs)) + vmem(1),
        scratch_shapes=[pltpu.VMEM(*s) for s in scratch]
        + copies_of(8, 1)
        + [
            pltpu.SemaphoreType.DMA((2, count * parts)),
            pltpu.SemaphoreType.DMA((2 * count,)),
        ],
        compiler_params=params(1),
        name="middle",
    )(x, dy, ctx, wa, wb, vec)


def attend_back_tile(
    head, tree, trees, start, keys, order_ref, q_ref, k_ref, v_ref, kt_ref, ot_ref, lse_ref,
    do_ref, dq_s, dk_s, dv_s,
):
    here = slice(start, start + PAIR)
    base = tree * TREE_BLOCKS
    at = head * trees + tree
    grad = []
    for i in range(2):
        grad.append(do_ref[order_ref[tree * TREE_BLOCKS + start // BLOCK + i]])
    do = jnp.concatenate(grad, axis=0)[:, head * HEAD : (head + 1) * HEAD]
    delta = jnp.sum(do.astype(SINGLE).T * ot_ref[at, :, here], axis=0, keepdims=True)
    q = stack(q_ref, head, picks(order_ref, tree, start, PAIR), 0)
    lse = lse_ref[at, :, here]
    dq = 0.0
    for off, size, kind in keys:
        chosen = picks(order_ref, tree, off, size)
        out = slice(base + off // BLOCK, base + (off + size) // BLOCK)
        p = jnp.exp2(dot(stack(k_ref, head, chosen, 0), q, NT) * SCALE - lse)
        if kind:
            p = jnp.where(mask_of(kind), p, 0.0)
        dp = dot(stack(v_ref, head, chosen, 0), do, NT)
        ds = (p * (dp - delta)).astype(HALF)
        dv_s[out] += dot(p.astype(HALF), do).reshape(size // BLOCK, BLOCK, HEAD)
        dk_s[out] += dot(ds, q).reshape(size // BLOCK, BLOCK, HEAD)
        dq = dq + dot(stack(kt_ref, head, chosen, 1), ds)
    first = base + start // BLOCK
    dq_s[first : first + 2] = (dq * 0.125).T.reshape(2, BLOCK, HEAD)


def total_of(*refs):
    return functools.reduce(jnp.add, [r.astype(SINGLE) for r in refs])


def finish_kernel(
    parts,
    copies,
    heads,
    tile,
    order_ref,
    near_hbm,
    q_hbm,
    k_hbm,
    v_hbm,
    kt_hbm,
    ot_hbm,
    lse_hbm,
    do_hbm,
    dh1_hbm,
    wa_hbm,
    pa_hbm,
    pb_hbm,
    norm_in,
    dx_hbm,
    gq_ref,
    gk_ref,
    gv_ref,
    go_out,
    gh_ref,
    gp_ref,
    norm_out,
    near_ref,
    q_ref,
    k_ref,
    v_ref,
    kt_ref,
    ot_ref,
    lse_ref,
    do_ref,
    dx_ref,
    wq_ref,
    dq_s,
    dk_s,
    dv_s,
    qk_ref,
    vv_ref,
    qk_in,
    vv_in,
    wqk_ref,
    wvv_ref,
    pa_ref,
    pac_ref,
    par_ref,
    pas_ref,
    paz_ref,
    fa_ref,
    pb_ref,
    pbc_ref,
    pbr_ref,
    pbs_ref,
    pbz_ref,
    fb_ref,
    far_ref,
    dws_ref,
    dwc_ref,
    dwz_ref,
    dwp_ref,
    dwf_ref,
    nsum_ref,
    nrecv_ref,
    local_sem,
    send_sem,
    recv_sem,
    out_sem,
    row_sem,
):
    wire = Wire(local_sem, send_sem, recv_sem)
    me, rep, near, core, layers, far = places(parts, copies)
    blocks, _, width = near_ref.shape
    total = blocks * BLOCK
    rows = total // parts
    trees = total // TREE_TOK
    per = rows // BLOCK
    depth = width // parts
    side = lax.rem(rep, 2)
    layer = lax.rem(lax.div(rep, 2), LAYERS)
    other = 1 - side
    split = 2 * LAYERS // parts

    def load(source, target, head):
        return wire.keep(source.at[head], target[head])

    def load_tree(source, target, head):
        some = pl.ds(head * trees, trees)
        return wire.keep(source.at[some], target.at[some])

    def load_head(head):
        return [
            load(q_hbm, q_ref, head),
            load(k_hbm, k_ref, head),
            load(v_hbm, v_ref, head),
            load(kt_hbm, kt_ref, head),
            load_tree(ot_hbm, ot_ref, head),
            load_tree(lse_hbm, lse_ref, head),
        ]

    def arrived(copies_in):
        for copy in copies_in:
            copy.wait_recv()

    loads = [[wire.keep(do_hbm, do_ref)] + load_head(0)]
    greet([p for _, p in near] + [core] + [p for _, p in layers] + far)

    halves_out = [
        wire.send(pa_hbm.at[other], pac_ref, *core),
        wire.send(pb_hbm.at[other], pbc_ref, *core),
    ]
    halves_own = [wire.keep(pa_hbm.at[side], pa_ref), wire.keep(pb_hbm.at[side], pb_ref)]
    for h in range(1, heads):
        loads.append(load_head(h))
    near_load = wire.keep(near_hbm, near_ref)
    weight_load = wire.keep(wa_hbm.at[:, pl.ds(0, 3 * width)], wq_ref)
    base_load = wire.keep(dh1_hbm, dx_ref)

    doubling = [core, layers[0][1], layers[1][1]] + far
    bit = 1
    while bit < parts:
        doubling.append(near[bit - 1][1])
        bit *= 2
    nsum_ref[0] = norm_in[...]
    state = {"step": 0, "copy": wire.send(nsum_ref.at[0], nrecv_ref.at[0], *doubling[0])}

    def norm_step():
        i = state["step"]
        if i == len(doubling):
            return
        state["copy"].wait_recv()
        nsum_ref[i + 1] = nsum_ref[i] + nrecv_ref[i]
        state["step"] = i = i + 1
        if i < len(doubling):
            state["copy"] = wire.send(nsum_ref.at[i], nrecv_ref.at[i], *doubling[i])

    def beyond(value, slot):
        for i, p in enumerate(far):
            send, recv = far_ref.at[slot, i, 0], far_ref.at[slot, i, 1]
            n, m = value.shape
            send[0:n, 0:m] = value.astype(HALF)
            copy = wire.send(send, recv, *p)
            copy.wait_recv()
            value = value.astype(HALF).astype(SINGLE) + recv[0:n, 0:m].astype(SINGLE)
        return value.astype(HALF)

    low = pb_ref.shape[2]

    def pack_split():
        arrived(halves_out)
        for copy in halves_own:
            copy.wait()
        for r in range(parts):
            for z in range(LAYERS):
                pa_ref[r, z] = total_of(pa_ref[r, z], pac_ref[r, z]).astype(HALF)
        out_a = [wire.send(pa_ref.at[r], par_ref.at[r - 1], *p) for r, p in near]
        for z in range(LAYERS):
            for r in range(parts):
                pb_ref[z, r] = total_of(pb_ref[z, r], pbc_ref[z, r]).astype(HALF)
        out_b = [wire.send(pb_ref.at[flip(layer, j)], pbr_ref.at[j - 1], *p) for j, p in layers]
        return out_a, out_b

    def pack_a_scatter(waits):
        arrived(waits)
        for z in range(LAYERS):
            pas_ref[z] = total_of(
                pa_ref[0, z], *[par_ref[r, z] for r in range(parts - 1)]
            ).astype(HALF)
        return [wire.send(pas_ref.at[flip(layer, j)], paz_ref.at[j - 1], *p) for j, p in layers]

    def pack_a_spread(waits):
        arrived(waits)
        piece = total_of(pas_ref[layer], *[paz_ref[j] for j in range(LAYERS - 1)])
        fa_ref[side, layer] = beyond(piece, 0)
        here = fa_ref.at[side, layer]
        return [wire.send(here, here, *p) for _, p in layers]

    def pack_b_scatter(waits):
        arrived(waits)
        for r in range(parts):
            piece = total_of(pb_ref[layer, r], *[pbr_ref[j, r] for j in range(LAYERS - 1)])
            pbs_ref[r] = beyond(piece, 3 + r)
        return [wire.send(pbs_ref.at[r], pbz_ref.at[r - 1], *p) for r, p in near]

    def pack_b_spread(waits):
        arrived(waits)
        piece = total_of(pbs_ref[0], *[pbz_ref[r] for r in range(parts - 1)])
        fb_ref[side, layer] = piece.astype(HALF)
        here = fb_ref.at[side, layer]
        return [wire.send(here, here, *p) for _, p in layers]

    def pack_cores(waits):
        arrived(waits)
        return [
            wire.send(fa_ref.at[side], fa_ref.at[side], *core),
            wire.send(fb_ref.at[side], fb_ref.at[side], *core),
        ]

    def weights_cores(head):
        return [wire.send(dws_ref.at[head, other], dwc_ref.at[head], *core)]

    def weights_scatter(head, waits):
        arrived(waits)
        for z in range(LAYERS):
            dws_ref[head, side, z] = total_of(dws_ref[head, side, z], dwc_ref[head, z]).astype(HALF)
        return [
            wire.send(dws_ref.at[head, side, flip(layer, j)], dwz_ref.at[head, j - 1], *p)
            for j, p in layers
        ]

    to_row = layer if split == 2 else side * LAYERS + layer

    def weights_send(head, waits):
        arrived(waits)
        piece = total_of(
            dws_ref[head, side, layer], *[dwz_ref[head, j] for j in range(LAYERS - 1)]
        )
        dwp_ref[head] = beyond(piece, 1 + head)

        @pl.when(to_row == 0)
        def _():
            dwf_ref[head, side, layer] = dwp_ref[head]

        copy = pltpu.make_async_remote_copy(
            dwp_ref.at[head],
            dwf_ref.at[head, side, layer],
            row_sem.at[0, head],
            row_sem.at[1, head],
            device_id={"fsdp": flip_two(me, to_row, parts)},
            device_id_type=MESH,
        )

        @pl.when(to_row != 0)
        def _():
            copy.start()

        return copy

    def weights_spread(head, copy):
        @pl.when(to_row != 0)
        def _():
            copy.wait()

        here = dwf_ref.at[head, side, layer]
        return [wire.send(here, here, *p) for _, p in layers]

    def weights_last(head, waits):
        arrived(waits)
        return [wire.send(dwf_ref.at[head, side], dwf_ref.at[head, side], *core)]

    def unsort(head):
        for r in range(parts):

            def one(j, _):
                place = order_ref[blocks + r * per + j]
                both = jnp.concatenate([dq_s[place], dk_s[place] * 0.125], axis=1)
                qk_ref[head, r, block_at(j), :] = both.astype(HALF)
                lower = pl.ds(pl.multiple_of(j * (BLOCK // 2), BLOCK // 2), BLOCK // 2)
                vv_ref[head, r, lower, :] = fold(dv_s[place]).astype(HALF)
                return 0

            lax.fori_loop(0, per, one, 0)
        return [wire.send(qk_ref.at[head, r], qk_in.at[head, r], *p) for r, p in near]

    def send_values(head):
        return [wire.send(vv_ref.at[head, r], vv_in.at[head, r], *p) for r, p in near]

    def weight_grads(head):
        total_dw = 0.0
        for r in range(parts):
            grads = jnp.concatenate([qk_ref[head, r], unfold(vv_ref[head, r])], axis=1)
            total_dw = total_dw + dot(
                grads.T, near_ref[r * per : (r + 1) * per].reshape(rows, width)
            )
        dw = total_dw.astype(HALF)
        for c in range(parts):
            to = flip(me, c)
            piece = dw[:, c * depth : (c + 1) * depth]
            if split == 2:
                dws_ref[head, 0, to] = piece[: piece.shape[0] // 2]
                dws_ref[head, 1, to] = piece[piece.shape[0] // 2 :]
            else:
                dws_ref[head, lax.div(to, LAYERS), lax.rem(to, LAYERS)] = piece

    def turn_weights():
        for h in range(heads):
            for c in range(parts):
                at = (c * heads + h) * HEAD
                wqk_ref[h, :, c * 2 * HEAD : (c + 1) * 2 * HEAD] = jnp.concatenate(
                    [wq_ref[:, at : at + HEAD], wq_ref[:, width + at : width + at + HEAD]], axis=1
                )
                wvv_ref[h, :, c * HEAD : (c + 1) * HEAD] = wq_ref[
                    :, 2 * width + at : 2 * width + at + HEAD
                ]

    def input_grad(head, first, last):
        def pick(ref, c, at):
            return ref[head, flip(me, c), at, :]

        def step(i, _):
            at = pl.ds(pl.multiple_of(i * tile, tile), tile)
            lower = pl.ds(pl.multiple_of(i * (tile // 2), tile // 2), tile // 2)
            total_dx = dx_ref[at, :]
            if first:
                qk = jnp.concatenate([pick(qk_in, c, at) for c in range(parts)], axis=1)
                total_dx = total_dx + dot(qk, wqk_ref[head], NT)
            if last:
                vv = jnp.concatenate([unfold(pick(vv_in, c, lower)) for c in range(parts)], axis=1)
                total_dx = total_dx + dot(vv, wvv_ref[head], NT)
            dx_ref[at, :] = total_dx
            if last and head == heads - 1:
                pltpu.make_async_copy(dx_ref.at[at], dx_hbm.at[at], out_sem.at[i]).start()
            return 0

        lax.fori_loop(0, rows // tile, step, 0)

    def keep_own(head):
        qk_in[head, 0] = qk_ref[head, 0]
        vv_in[head, 0] = vv_ref[head, 0]

    sent, values, chains = [], [], {}
    for h in range(heads):
        for copy in loads[h]:
            copy.wait()
        dk_s[...] = jnp.zeros_like(dk_s)
        dv_s[...] = jnp.zeros_like(dv_s)
        for number, (begin, keys) in enumerate(tile_list()):
            for tree in range(trees):
                attend_back_tile(
                    h, tree, trees, begin, keys, order_ref, q_ref, k_ref, v_ref, kt_ref, ot_ref,
                    lse_ref, do_ref, dq_s, dk_s, dv_s,
                )
            event = (h, number)
            if event == (0, 4):
                pack_a, pack_b = pack_split()
            elif event == (0, 6) or event == (0, 8):
                norm_step()
            elif event == (1, 1):
                chains[0] = weights_scatter(0, chains[0])
            elif event == (1, 2):
                norm_step()
            elif event == (1, 4):
                pack_a = pack_a_scatter(pack_a)
            elif event == (1, 5):
                chains[0] = weights_send(0, chains[0])
            elif event == (1, 7):
                pack_b = pack_b_scatter(pack_b)
            elif event == (1, 8):
                norm_step()
        sent.append(unsort(h))
        keep_own(h)
        if h == 0:
            near_load.wait()
        if h < heads - 1:
            values.append(send_values(h))
            weight_grads(h)
            chains[h] = weights_cores(h)
    end_head = heads - 1
    if heads == 1:
        pack_a = pack_a_scatter(pack_a)
        pack_b = pack_b_scatter(pack_b)
    weight_grads(end_head)
    chains[end_head] = weights_cores(end_head)
    pack_a = pack_a_spread(pack_a)
    weight_load.wait()
    base_load.wait()
    turn_weights()
    chains[end_head] = weights_scatter(end_head, chains[end_head])
    if heads > 1:
        arrived(sent[0] + values[0])
        input_grad(0, True, True)
    chains[end_head] = weights_send(end_head, chains[end_head])
    values.append(send_values(end_head))
    pack_b = pack_b_spread(pack_b)
    while state["step"] < len(doubling):
        norm_step()
    if heads > 1:
        chains[0] = weights_spread(0, chains[0])
    arrived(sent[end_head])
    input_grad(end_head, True, False)
    last = pack_cores(pack_a + pack_b)
    chains[end_head] = weights_spread(end_head, chains[end_head])
    arrived(values[end_head])
    input_grad(end_head, False, True)
    for h in range(heads):
        last += weights_last(h, chains[h])
    arrived(last)

    norm_out[...] = nsum_ref[len(doubling)]
    small = depth // SLICES
    cols = gp_ref.shape[0]
    unit = width // LAYERS
    for z in range(LAYERS):
        here = slice(z * width, (z + 1) * width)
        gh_ref[0:low, here] = fa_ref[0, z, 0:low].astype(SINGLE)
        gh_ref[low:depth, here] = fb_ref[0, z].astype(SINGLE)
        piece = jnp.concatenate([fa_ref[1, z, 0:low], fb_ref[1, z]], axis=0).astype(SINGLE)
        if cols < width:
            piece = jnp.concatenate([piece[:, :cols], piece[:, cols:]], axis=0)
        gp_ref[:, z * unit : (z + 1) * unit] = piece.T
        for i in range(2):
            at = (i * LAYERS + z) * small
            go_out[at : at + small, :] = fa_ref[i, z, low : low + small].astype(SINGLE)
    for c in range(parts):
        for h in range(heads):
            r = flip(me, c)
            if split == 2:
                piece = jnp.concatenate([dwf_ref[h, 0, r], dwf_ref[h, 1, r]], axis=0)
            else:
                piece = dwf_ref[h, lax.div(r, LAYERS), lax.rem(r, LAYERS)]
            turned = piece.astype(SINGLE).T
            at = (c * heads + h) * HEAD
            for ref, k in ((gq_ref, 0), (gk_ref, 1), (gv_ref, 2)):
                ref[:, at : at + HEAD] = turned[:, k * HEAD : (k + 1) * HEAD]

    def end(i, _):
        at = pl.ds(pl.multiple_of(i * tile, tile), tile)
        pltpu.make_async_copy(dx_ref.at[at], dx_hbm.at[at], out_sem.at[i]).wait()
        return 0

    lax.fori_loop(0, rows // tile, end, 0)
    wire.finish()


def finish(parts, copies, heads, order, saved, do, dh1, wa, pa, pb, norms):
    near, q, k, v, kt, ot, lse = saved
    blocks, _, width = near.shape
    total = blocks * BLOCK
    rows = total // parts
    depth = width // parts
    inner = wa.shape[1] - 4 * width
    tile = PAIR if rows % PAIR == 0 else BLOCK
    split = 2 * LAYERS // parts
    beyonds = max(copies // (2 * LAYERS), 2).bit_length() - 1
    stages = (copies * parts).bit_length()
    flat = ((blocks, BLOCK, HEAD), SINGLE)
    qk = ((heads, parts, rows, 2 * HEAD), HALF)
    vv = ((heads, parts, rows // 2, 2 * HEAD), HALF)
    a, b = pa.shape[1:], pb.shape[1:]
    dws = (LAYERS, 3 * HEAD // split, depth)
    each = lambda r: [pltpu.VMEM(r.shape[1:], r.dtype)] * heads
    scratch = [(r.shape, r.dtype) for r in (ot, lse, do)]
    scratch += [((rows, width), SINGLE), ((width, 3 * width), HALF), flat, flat, flat]
    scratch += [qk, vv, qk, vv]
    scratch += [((heads, width, 2 * HEAD * parts), HALF), ((heads, width, HEAD * parts), HALF)]
    scratch += [(n, HALF) for n in (a, a, (parts - 1,) + a[1:], a[1:])]
    scratch += [((LAYERS - 1,) + a[2:], HALF), ((2, LAYERS) + a[2:], HALF)]
    scratch += [(n, HALF) for n in (b, b, (LAYERS - 1,) + b[1:], b[1:])]
    scratch += [((parts - 1,) + b[2:], HALF), ((2, LAYERS) + b[2:], HALF)]
    scratch += [((3 + parts, beyonds, 2, max(3 * HEAD, depth), width), HALF)]
    if copies == 2 * LAYERS:
        scratch[-1] = ((1, 1, 2, 16, width), HALF)
    scratch += [((heads, 2) + dws, HALF), ((heads,) + dws, HALF)]
    scratch += [((heads, LAYERS - 1) + dws[1:], HALF), ((heads,) + dws[1:], HALF)]
    scratch += [((heads, 2) + dws, HALF)]
    scratch += [((stages, 4, width), SINGLE), ((stages, 4, width), SINGLE)]
    square = ((depth, width), SINGLE)
    outs = [square] * 4 + [((depth, inner), SINGLE), ((inner // parts, width), SINGLE)]
    outs += [((4, width), SINGLE)]
    return pl.pallas_call(
        functools.partial(finish_kernel, parts, copies, heads, tile),
        out_shape=[shape((rows, width), SINGLE)] + [shape(*o) for o in outs],
        in_specs=[smem()] + anywhere(12) + vmem(1),
        out_specs=anywhere(1) + vmem(len(outs)),
        scratch_shapes=[pltpu.VMEM(near.shape, HALF)]
        + [each(r) for r in (q, k, v, kt)]
        + [pltpu.VMEM(*s) for s in scratch]
        + copies_of(8 + 6 * heads, 48 + 12 * parts)
        + [pltpu.SemaphoreType.DMA((rows // tile,)), pltpu.SemaphoreType.DMA((2, heads))],
        compiler_params=params(2),
        name="finish",
    )(order, near, q, k, v, kt, ot, lse, do, dh1, wa, pa, pb, norms)


def shards(
    parts,
    copies,
    inputs,
    cotangent,
    segments,
    trees,
    parents,
    w_query,
    w_key,
    w_value,
    w_out,
    w_hidden,
    w_proj,
    norm1_gain,
    norm1_bias,
    norm2_gain,
    norm2_bias,
):
    x = inputs[0]
    rows, width = x.shape
    inner = w_hidden.shape[1]
    heads = HEADS // parts
    wide = heads * HEAD
    depth = width // parts
    me = lax.axis_index("fsdp")
    order = block_order(segments[0], trees[0], parents[0], rows, me)
    by = jnp.concatenate([w.reshape(depth, parts, wide) for w in (w_query, w_key, w_value)], axis=2)
    by = by.transpose(1, 0, 2)
    sa = jnp.concatenate([w_query, w_key, w_value, w_out, w_hidden], axis=1)
    sa = sa.reshape(SLICES, depth // SLICES, 4 * width + inner)
    sb = w_proj.reshape(SLICES, inner // parts // SLICES, width)
    near, q, k, v, kt, ot, lse, ctx, wa, wb = start(parts, copies, heads, order, x, by, sa, sb)
    wa = wa.reshape(width, 4 * width + inner)
    wb = wb.reshape(inner, width)
    vec = jnp.stack([norm1_gain, norm1_bias, norm2_gain, norm2_bias])
    output, dh1, do, pa, pb, norms = middle(
        parts, copies, heads, x, cotangent[0], ctx, wa, wb, vec
    )
    saved = (near, q, k, v, kt, ot, lse)
    input_grad, gq, gk, gv, go, gh, gp, norms = finish(
        parts, copies, heads, order, saved, do.reshape(-1, BLOCK, wide), dh1, wa, pa, pb, norms
    )
    return (
        output[None],
        input_grad[None],
        gq,
        gk,
        gv,
        go,
        gh,
        gp,
        norms[0],
        norms[1],
        norms[2],
        norms[3],
    )


def solution(mesh):
    token = P("rep", "fsdp", None)
    weight = P("fsdp", None)
    placed = (token, token, P("rep", None), P("rep", None), P("rep", None, None))
    return jax.shard_map(
        functools.partial(shards, mesh.shape["fsdp"], mesh.shape["rep"]),
        mesh=mesh,
        in_specs=placed + (weight,) * 6 + (P(),) * 4,
        out_specs=(token, token) + (weight,) * 6 + (P(),) * 4,
        check_vma=False,
    )
```

```python
import functools

import jax
import jax.numpy as jnp
from jax import lax
from jax.experimental import pallas as pl
from jax.experimental.pallas import tpu as pltpu
from jax.sharding import PartitionSpec as P

HEADS = 8
HEAD = 64
BLOCK = 128
PAIR = 2 * BLOCK
TRUNK = 8
BRANCHES = 4
LEAVES = 8
TREE_BLOCKS = TRUNK + BRANCHES + LEAVES
TREE_TOK = TREE_BLOCKS * BLOCK
SINGLE = jnp.float32
HALF = jnp.bfloat16
NN = (((1,), (0,)), ((), ()))
NT = (((1,), (1,)), ((), ()))
LOG2E = 1.4426950408889634
SCALE = 0.125 * LOG2E
VMEM_LIMIT = 58 << 20
MESH = pl.DeviceIdType.MESH
SLICES = 8
LAYERS = 4


def dot(left, right, dims=NN):
    return lax.dot_general(left, right, dims, preferred_element_type=SINGLE)


def row_mean(values):
    return jnp.mean(values, axis=-1, keepdims=True)


def block_order(segments, trees, parents, rows, me):
    seg = segments.reshape(-1, BLOCK)[:, 0]
    tree = trees.reshape(-1, BLOCK)[:, 0]
    count = seg.shape[0]
    table = parents.reshape(-1)
    slot = tree * parents.shape[1] + seg
    parent = jnp.sum(
        jnp.where(slot[:, None] == jnp.arange(table.shape[0])[None, :], table[None, :], 0), axis=1
    )
    place = jnp.arange(count, dtype=jnp.int32)
    kind = jnp.where(seg == 0, 0, jnp.where(seg <= BRANCHES, seg, 16 * parent + seg))
    key = (tree * 256 + kind) * 64 + place
    rank = jnp.sum((key[None, :] < key[:, None]).astype(jnp.int32), axis=1)
    per = rows // BLOCK
    near = ((place // per) ^ me) * per + place % per
    order = jnp.sum(jnp.where(rank[None, :] == place[:, None], near[None, :], 0), axis=1)
    back = jnp.sum(jnp.where(near[None, :] == place[:, None], rank[None, :], 0), axis=1)
    return jnp.concatenate([order, back]).astype(jnp.int32)


def tile_list():
    out = []
    trunk = TRUNK * BLOCK
    for start in range(0, trunk, PAIR):
        keys = [(0, start, None)] if start else []
        out.append((start, keys + [(start, PAIR, "causal")]))
    for pair in range(BRANCHES // 2):
        start = trunk + pair * PAIR
        out.append((start, [(0, trunk, None), (start, PAIR, "own")]))
    for branch in range(BRANCHES):
        start = trunk + BRANCHES * BLOCK + branch * PAIR
        out.append(
            (
                start,
                [(0, trunk, None), (trunk + branch * BLOCK, BLOCK, None), (start, PAIR, "own")],
            )
        )
    return out


def mask_of(kind):
    key = lax.broadcasted_iota(jnp.int32, (PAIR, PAIR), 0)
    query = lax.broadcasted_iota(jnp.int32, (PAIR, PAIR), 1)
    mask = key <= query
    if kind == "own":
        mask = mask & ((key >= BLOCK) == (query >= BLOCK))
    return mask


def flip(value, bits):
    bit = 1
    while bit <= bits:
        if bits & bit:
            value = value + bit - 2 * bit * lax.rem(lax.div(value, bit), 2)
        bit *= 2
    return value


def flip_two(one, two, size):
    out = 0
    bit = 1
    while bit < size:
        out = out + bit * lax.rem(lax.rem(lax.div(one, bit), 2) + lax.rem(lax.div(two, bit), 2), 2)
        bit *= 2
    return out


class Wire:
    def __init__(self, local_sem, send_sem, recv_sem):
        self.local_sem, self.send_sem, self.recv_sem = local_sem, send_sem, recv_sem
        self.locals = self.remotes = 0
        self.open = []

    def keep(self, source, target):
        copy = pltpu.make_async_copy(source, target, self.local_sem.at[self.locals])
        self.locals += 1
        copy.start()
        return copy

    def plan(self, source, target, axis, peer):
        copy = pltpu.make_async_remote_copy(
            source,
            target,
            self.send_sem.at[self.remotes],
            self.recv_sem.at[self.remotes],
            device_id={axis: peer},
            device_id_type=MESH,
        )
        self.remotes += 1
        self.open.append(copy)
        return copy

    def send(self, *route):
        copy = self.plan(*route)
        copy.start()
        return copy

    def finish(self):
        for copy in self.open:
            copy.wait_send()


def greet(peers):
    barrier = pltpu.get_barrier_semaphore()
    for axis, peer in peers:
        pl.semaphore_signal(barrier, inc=1, device_id={axis: peer}, device_id_type=MESH)
    pl.semaphore_wait(barrier, len(peers))


def places(parts, copies):
    me = lax.axis_index("fsdp")
    rep = lax.axis_index("rep")
    near = [(r, ("fsdp", flip(me, r))) for r in range(1, parts)]
    core = ("rep", flip(rep, 1))
    layers = [(j, ("rep", flip(rep, 2 * j))) for j in range(1, LAYERS)]
    far = []
    bit = 2 * LAYERS
    while bit < copies:
        far.append(("rep", flip(rep, bit)))
        bit *= 2
    return me, rep, near, core, layers, far


class Gather:
    def __init__(self, wire, spots, shards_in, full):
        self.wire, self.spots, self.shards_in, self.full = wire, spots, shards_in, full
        me, rep, near, core, layers, far = spots
        self.side = lax.rem(rep, 2)
        mine = self.side * LAYERS + lax.rem(lax.div(rep, 2), LAYERS)
        half = pl.ds(self.side * LAYERS, LAYERS)
        others = [flip(me, r) for r, _ in near]
        pairs = list(zip(shards_in, full))
        self.own = []
        self.stages = [
            [wire.plan(a.at[mine], b.at[me, mine], *p) for _, p in near for a, b in pairs],
            [
                wire.plan(b.at[c, mine], b.at[c, mine], *p)
                for _, p in layers
                for c in others
                for b in full
            ],
            [wire.plan(b.at[c, half], b.at[c, half], *core) for c in others for b in full],
        ]

    def start(self):
        for copy in self.stages[0]:
            copy.start()
        me = self.spots[0]
        self.own = [self.wire.keep(a, b.at[me]) for a, b in zip(self.shards_in, self.full)]

    def step(self, i):
        for copy in self.stages[i - 1]:
            copy.wait_recv()
        for copy in self.stages[i]:
            copy.start()

    def end(self):
        for copy in self.stages[2]:
            copy.wait_recv()
        for copy in self.own:
            copy.wait()


def picks(order_ref, tree, start, size):
    first = tree * TREE_BLOCKS + start // BLOCK
    return [order_ref[first + i] for i in range(size // BLOCK)]


def stack(ref, head, chosen, axis):
    blocks = [ref[head][i] for i in chosen]
    return jnp.concatenate(blocks, axis=axis) if len(blocks) > 1 else blocks[0]


def attend_head(head, trees, order_ref, q_ref, k_ref, vt_ref, ot_ref, lse_ref, flat_ref):
    for start, keys in tile_list():
        here = slice(start, start + PAIR)
        for tree in range(trees):
            at = head * trees + tree
            q = stack(q_ref, head, picks(order_ref, tree, start, PAIR), 0)
            scores = []
            for off, size, kind in keys:
                s = dot(stack(k_ref, head, picks(order_ref, tree, off, size), 0), q, NT)
                if kind:
                    s = jnp.where(mask_of(kind), s, -1e30)
                scores.append(s)
            top = functools.reduce(
                jnp.maximum, [jnp.max(s, axis=0, keepdims=True) for s in scores]
            )
            top = top * SCALE
            mass = 0.0
            acc = 0.0
            for (off, size, _), s in zip(keys, scores):
                e = jnp.exp2(s * SCALE - top)
                mass = mass + jnp.sum(e, axis=0, keepdims=True)
                vt = stack(vt_ref, head, picks(order_ref, tree, off, size), 1)
                acc = acc + dot(vt, e.astype(HALF))
            out = acc * (1.0 / mass)
            lse_ref[at, :, here] = top + jnp.log2(mass)
            ot_ref[at, :, here] = out
            place = tree * TREE_BLOCKS + start // BLOCK
            flat_ref[place : place + 2] = out.T.astype(HALF).reshape(2, BLOCK, HEAD)


def fold(block):
    return jnp.concatenate([block[: BLOCK // 2], block[BLOCK // 2 :]], axis=1)


def unfold(packed):
    parts = []
    for i in range(packed.shape[0] // (BLOCK // 2)):
        piece = packed[i * (BLOCK // 2) : (i + 1) * (BLOCK // 2)]
        parts += [piece[:, :HEAD], piece[:, HEAD:]]
    return jnp.concatenate(parts, axis=0)


def block_at(index):
    return pl.ds(pl.multiple_of(index * BLOCK, BLOCK), BLOCK)


def start_kernel(
    parts,
    copies,
    heads,
    order_ref,
    x_hbm,
    by_hbm,
    so_hbm,
    sh_hbm,
    sp_hbm,
    near_hbm,
    q_hbm,
    k_hbm,
    v_hbm,
    kt_hbm,
    ot_hbm,
    lse_hbm,
    ctx_hbm,
    wo_hbm,
    wh_hbm,
    wp_hbm,
    near_ref,
    own_ref,
    q_ref,
    k_ref,
    v_ref,
    kt_ref,
    vt_ref,
    ot_ref,
    lse_ref,
    flat_ref,
    ctx_ref,
    local_sem,
    send_sem,
    recv_sem,
):
    wire = Wire(local_sem, send_sem, recv_sem)
    spots = places(parts, copies)
    me, rep, near, core, layers, far = spots
    per = x_hbm.shape[0]
    blocks = parts * per
    trees = blocks // TREE_BLOCKS
    wide = heads * HEAD
    greet([p for _, p in near] + [core] + [p for _, p in layers])

    def own_piece(device):
        if len(by_hbm) == 1:
            return [(by_hbm[0].at[device], own_ref.at[me])]
        at = pl.ds(pl.multiple_of(device * wide, wide), wide)
        return [
            (w.at[:, at], own_ref.at[me, :, pl.ds(i * wide, wide)]) for i, w in enumerate(by_hbm)
        ]

    kept = [wire.keep(*pair) for pair in own_piece(me)]
    kept.append(wire.keep(x_hbm, near_ref.at[pl.ds(0, per)]))
    own_copies = [wire.send(*pair, *p) for _, p in near for pair in own_piece(p[1])]
    gather = Gather(wire, spots, (so_hbm, sh_hbm, sp_hbm), (wo_hbm, wh_hbm, wp_hbm))
    gather.start()

    def project(first, count):
        weight = own_ref[...].reshape(parts * own_ref.shape[1], 3 * wide)
        x = near_ref[first : first + count].reshape(count * BLOCK, near_ref.shape[2])
        out = dot(x, weight).astype(HALF)
        for i in range(count):
            block = out[i * BLOCK : (i + 1) * BLOCK]
            kt = block[:, wide : 2 * wide].T
            vt = block[:, 2 * wide :].T
            for h in range(heads):
                cols = slice(h * HEAD, (h + 1) * HEAD)
                q_ref[h, first + i] = block[:, cols]
                k_ref[h, first + i] = block[:, wide:][:, cols]
                v_ref[h, first + i] = block[:, 2 * wide :][:, cols]
                kt_ref[h, first + i] = kt[cols]
                vt_ref[h, first + i] = vt[cols]

    def wait_all(copies_in):
        for copy in copies_in:
            copy.wait_recv()

    if parts == 4:
        cuts = [i * per // 4 for i in range(5)]

        def part(chunk, i):
            return pl.ds(chunk * per + cuts[i], cuts[i + 1] - cuts[i])

        (_, px), (_, py), _ = near
        one, two = {}, {}
        for a, b in zip((0, 1, 2, 3), (2, 3, 0, 1)):
            one[a] = wire.send(x_hbm.at[part(0, a)], near_ref.at[part(1, a)], *px)
            two[b] = wire.send(x_hbm.at[part(0, b)], near_ref.at[part(2, b)], *py)
        three = {}
        for a, b in ((0, 2), (1, 3)):
            one[a].wait_recv()
            three[a] = wire.send(near_ref.at[part(1, a)], near_ref.at[part(3, a)], *py)
            two[b].wait_recv()
            three[b] = wire.send(near_ref.at[part(2, b)], near_ref.at[part(3, b)], *px)
            if a == 0:
                gather.step(1)
                for copy in kept:
                    copy.wait()
                wait_all(own_copies)
                project(0, per)
        wait_all([one[2], one[3]])
        project(per, per)
        wait_all([two[0], two[1]])
        project(2 * per, per)
        wait_all([three[0], three[2]])
        project(3 * per, cuts[1])
        project(3 * per + cuts[2], cuts[3] - cuts[2])
        wait_all([three[1], three[3]])
        project(3 * per + cuts[1], cuts[2] - cuts[1])
        project(3 * per + cuts[3], cuts[4] - cuts[3])
    else:
        waits = [wire.send(x_hbm, near_ref.at[pl.ds(r * per, per)], *p) for r, p in near]
        gather.step(1)
        for copy in kept:
            copy.wait()
        wait_all(own_copies + waits)
        for r in range(parts):
            project(r * per, per)
    saves = [wire.keep(near_ref, near_hbm)]
    saves += [
        wire.keep(a, b)
        for a, b in ((q_ref, q_hbm), (k_ref, k_hbm), (v_ref, v_hbm), (kt_ref, kt_hbm))
    ]
    context = []
    for h in range(heads):
        if h == heads - 1:
            gather.step(2)
        views = [[ref.at[i] for i in range(heads)] for ref in (q_ref, k_ref, vt_ref)]
        attend_head(h, trees, order_ref, *views, ot_ref, lse_ref, flat_ref)
        for r in range(parts):

            def unsort(j, _):
                block = flat_ref[order_ref[blocks + r * per + j]]
                at = pl.ds(pl.multiple_of(j * (BLOCK // 2), BLOCK // 2), BLOCK // 2)
                ctx_ref[h, r, at, :] = fold(block)
                return 0

            lax.fori_loop(0, per, unsort, 0)
            if r:
                context.append(wire.send(ctx_ref.at[h, r], ctx_hbm.at[h, r], *near[r - 1][1]))
            else:
                saves.append(wire.keep(ctx_ref.at[h, 0], ctx_hbm.at[h, 0]))
        some = pl.ds(h * trees, trees)
        saves.append(wire.keep(ot_ref.at[some], ot_hbm.at[some]))
        saves.append(wire.keep(lse_ref.at[some], lse_hbm.at[some]))
    wait_all(context)
    gather.end()
    for copy in saves:
        copy.wait()
    wire.finish()


def anywhere(count):
    return [pl.BlockSpec(memory_space=pl.ANY)] * count


def vmem(count):
    return [pl.BlockSpec(memory_space=pltpu.VMEM)] * count


def smem():
    return pl.BlockSpec(memory_space=pltpu.SMEM)


def shape(dims, dtype):
    return jax.ShapeDtypeStruct(dims, dtype)


def copies_of(count_local, count_remote):
    return [
        pltpu.SemaphoreType.DMA((count_local,)),
        pltpu.SemaphoreType.DMA((count_remote,)),
        pltpu.SemaphoreType.DMA((count_remote,)),
    ]


def params(number):
    return pltpu.CompilerParams(
        vmem_limit_bytes=VMEM_LIMIT, collective_id=number, has_side_effects=True
    )


def start(parts, copies, heads, order, x, by, slices):
    rows, width = x.shape
    total = parts * rows
    trees = total // TREE_TOK
    n = trees * heads
    tok = ((heads, total // BLOCK, BLOCK, HEAD), HALF)
    turned = ((heads, total // BLOCK, HEAD, BLOCK), HALF)
    near = ((total // BLOCK, BLOCK, width), HALF)
    ot = ((n, HEAD, TREE_TOK), SINGLE)
    lse = ((n, 1, TREE_TOK), SINGLE)
    ctx = ((heads, parts, rows // 2, 2 * HEAD), HALF)
    outs = [near, tok, tok, tok, turned, ot, lse, ctx]
    outs += [((parts,) + w.shape, HALF) for w in slices]
    scratch = [near, ((parts, width // parts, 3 * heads * HEAD), HALF), tok, tok, tok, turned, turned, ot, lse]
    scratch += [((total // BLOCK, BLOCK, HEAD), HALF), ctx]
    return pl.pallas_call(
        functools.partial(start_kernel, parts, copies, heads),
        out_shape=[shape(*o) for o in outs],
        in_specs=[smem(), *anywhere(1), anywhere(len(by)), *anywhere(3)],
        out_specs=anywhere(len(outs)),
        scratch_shapes=[pltpu.VMEM(*s) for s in scratch]
        + copies_of(12 + 3 * heads, 32 + (parts - 1) * 24),
        compiler_params=params(0),
        name="start",
    )(order, x.reshape(rows // BLOCK, BLOCK, width), by, *slices)


def middle_kernel(
    parts,
    copies,
    heads,
    tile,
    x_hbm,
    dy_hbm,
    ctx_hbm,
    wo_hbm,
    wh_hbm,
    wp_hbm,
    sq_hbm,
    sk_hbm,
    sv_hbm,
    vec_refs,
    out_hbm,
    dh1_hbm,
    do_hbm,
    pa_hbm,
    pb_hbm,
    wq_hbm,
    wk_hbm,
    wv_hbm,
    norm_ref,
    x_ref,
    dy_ref,
    ctx_ref,
    wo_ref,
    wh_ref,
    wp_ref,
    out_ref,
    dh1_ref,
    do_ref,
    pa_ref,
    pb_ref,
    cat_ref,
    u_ref,
    df_ref,
    da_ref,
    g_ref,
    dz_ref,
    d_s,
    local_sem,
    send_sem,
    recv_sem,
    tile_sem,
    out_sem,
):
    wire = Wire(local_sem, send_sem, recv_sem)
    spots = places(parts, copies)
    me, rep, near, core, layers, far = spots
    rows, width = x_ref.shape
    inner = wh_ref.shape[1]
    wide = heads * HEAD
    chunk = 512
    count = rows // tile
    loads = [
        wire.keep(ctx_hbm, ctx_ref),
        wire.keep(wo_hbm, wo_ref),
        wire.keep(x_hbm, x_ref),
        wire.keep(wh_hbm, wh_ref),
        wire.keep(wp_hbm, wp_ref),
        wire.keep(dy_hbm, dy_ref),
    ]
    greet([p for _, p in near] + [core] + [p for _, p in layers])
    gather = Gather(wire, spots, (sq_hbm, sk_hbm, sv_hbm), (wq_hbm, wk_hbm, wv_hbm))
    gather.start()
    gain1, bias1, gain2, bias2 = [ref[...] for ref in vec_refs]
    norm_ref[...] = jnp.zeros_like(norm_ref)
    for copy in loads:
        copy.wait()

    def rows_out(i, at):
        return [
            pltpu.make_async_copy(out_ref.at[at], out_hbm.at[at], out_sem.at[2 * i]),
            pltpu.make_async_copy(dh1_ref.at[at], dh1_hbm.at[at], out_sem.at[2 * i + 1]),
        ]

    def rows_sent(i, at):
        return [
            pltpu.make_async_remote_copy(
                do_ref.at[r, at],
                do_hbm.at[r, at],
                tile_sem.at[0, i * parts + r],
                tile_sem.at[1, i * parts + r],
                device_id={p[0]: p[1]},
                device_id_type=MESH,
            )
            for r, p in near
        ] + [
            pltpu.make_async_copy(do_ref.at[0, at], do_hbm.at[0, at], tile_sem.at[0, i * parts])
        ]

    def tile_rows(i):
        return pl.ds(pl.multiple_of(i * tile, tile), tile)

    def tile_step(i, _):
        at = tile_rows(i)
        packed = pl.ds(pl.multiple_of(i * (tile // 2), tile // 2), tile // 2)
        ctx = jnp.concatenate(
            [
                unfold(ctx_ref[h, flip(me, c), packed, :])
                for c in range(parts)
                for h in range(heads)
            ],
            axis=-1,
        )
        cat_ref[at, :] = ctx
        h1 = x_ref[at, :].astype(SINGLE) + dot(ctx, wo_ref[...])
        c1 = h1 - row_mean(h1)
        r1 = lax.rsqrt(row_mean(c1 * c1) + 1e-5)
        n1 = c1 * r1
        y1 = n1 * gain1 + bias1
        u = y1.astype(HALF)
        u_ref[at, :] = u
        branch = 0.0
        for j in range(0, inner, chunk):
            s = slice(j, j + chunk)
            z = dot(u, wh_ref[:, s])
            cdf = 0.5 * (1.0 + lax.erf(z * 0.7071067811865476))
            pdf = jnp.exp2(z * z * (-0.5 * LOG2E)) * 0.3989422804014327
            g = (z * cdf).astype(HALF)
            g_ref[at, s] = g
            d_s[:, s] = cdf + z * pdf
            branch = branch + dot(g, wp_ref[s, :])
        h2 = y1 + branch
        c2 = h2 - row_mean(h2)
        r2 = lax.rsqrt(row_mean(c2 * c2) + 1e-5)
        n2 = c2 * r2
        out_ref[at, :] = (n2 * gain2 + bias2).astype(HALF)
        dy = dy_ref[at, :].astype(SINGLE)
        norm_ref[2:3, :] += jnp.sum(dy * n2, axis=0, keepdims=True)
        norm_ref[3:4, :] += jnp.sum(dy, axis=0, keepdims=True)
        dn2 = dy * gain2
        dh2 = r2 * (dn2 - row_mean(dn2) - n2 * row_mean(dn2 * n2))
        df = dh2.astype(HALF)
        df_ref[at, :] = df
        back = 0.0
        for j in range(0, inner, chunk):
            s = slice(j, j + chunk)
            dz = (dot(df, wp_ref[s, :], NT) * d_s[:, s]).astype(HALF)
            dz_ref[at, s] = dz
            back = back + dot(dz, wh_ref[:, s], NT)
        dy1 = dh2 + back
        norm_ref[0:1, :] += jnp.sum(dy1 * n1, axis=0, keepdims=True)
        norm_ref[1:2, :] += jnp.sum(dy1, axis=0, keepdims=True)
        dn1 = dy1 * gain1
        dh1 = r1 * (dn1 - row_mean(dn1) - n1 * row_mean(dn1 * n1))
        dh1_ref[at, :] = dh1
        da = dh1.astype(HALF)
        da_ref[at, :] = da
        dctx = dot(da, wo_ref[...], NT).astype(HALF)
        for c in range(parts):
            do_ref[flip(me, c), at, :] = dctx[:, c * wide : (c + 1) * wide]
        for copy in rows_out(i, at) + rows_sent(i, at):
            copy.start()
        for stage in (1, 2):

            @pl.when(i == 2 * (stage - 1))
            def _():
                gather.step(stage)

        return 0

    lax.fori_loop(0, count, tile_step, 0)
    depth = width // parts
    cols = inner // parts
    low = depth // 2
    unit = width // LAYERS
    small = depth // SLICES

    def put(side, c, z, piece):
        to = flip(me, c)
        pa_ref[side, to, z, 0:low] = piece[:low]
        pb_ref[side, z, to] = piece[low:]

    df_t = df_ref[...].T
    for c in range(parts):
        grad = dot(df_t, g_ref[:, c * cols : (c + 1) * cols]).astype(HALF)
        for z in range(LAYERS):
            piece = grad[z * unit : (z + 1) * unit]
            if cols < width:
                piece = jnp.concatenate([piece[:depth], piece[depth:]], axis=1)
            put(1, c, z, piece)
    u_t = u_ref[...].T
    for z in range(LAYERS):
        grad = dot(u_t, dz_ref[:, z * width : (z + 1) * width]).astype(HALF)
        for c in range(parts):
            put(0, c, z, grad[c * depth : (c + 1) * depth])
    grad = dot(cat_ref[...].T, da_ref[...]).astype(HALF)
    for c in range(parts):
        for side in range(2):
            for z in range(LAYERS):
                at = c * depth + (side * LAYERS + z) * small
                pa_ref[side, flip(me, c), z, low : low + small] = grad[at : at + small]
    saves = [wire.keep(pa_ref, pa_hbm), wire.keep(pb_ref, pb_hbm)]

    def tile_end(i, _):
        at = tile_rows(i)
        for copy in rows_out(i, at):
            copy.wait()
        sent = rows_sent(i, at)
        for copy in sent:
            copy.wait()
        return 0

    lax.fori_loop(0, count, tile_end, 0)
    for copy in saves:
        copy.wait()
    gather.end()
    wire.finish()


def middle(parts, copies, heads, x, dy, ctx, wo, wh, wp, slices, vecs):
    rows, width = x.shape
    inner = wp.shape[0]
    tile = PAIR if rows % PAIR == 0 else BLOCK
    depth = width // parts
    wide = heads * HEAD
    tok = ((rows, width), HALF)
    full = ((rows, width), SINGLE)
    do = ((parts, rows, wide), HALF)
    pack = ((2, parts, LAYERS, depth // 2 + depth // SLICES, width), HALF)
    pack_b = ((2, LAYERS, parts, depth // 2, width), HALF)
    big = ((rows, inner), HALF)
    outs = [tok, full, do, pack, pack_b] + [((parts,) + w.shape, HALF) for w in slices]
    scratch = [tok, tok, (ctx.shape, HALF), ((width, width), HALF), ((width, inner), HALF)]
    scratch += [((inner, width), HALF), tok, full, do, pack, pack_b, tok, tok, tok, tok, big, big]
    scratch += [((tile, inner), SINGLE)]
    count = rows // tile
    return pl.pallas_call(
        functools.partial(middle_kernel, parts, copies, heads, tile),
        out_shape=[shape(*o) for o in outs] + [shape((4, width), SINGLE)],
        in_specs=[*anywhere(9), vmem(4)],
        out_specs=anywhere(len(outs)) + vmem(1),
        scratch_shapes=[pltpu.VMEM(*s) for s in scratch]
        + copies_of(12, 24 * (parts - 1))
        + [
            pltpu.SemaphoreType.DMA((2, count * parts)),
            pltpu.SemaphoreType.DMA((2 * count,)),
        ],
        compiler_params=params(1),
        name="middle",
    )(x, dy, ctx, wo, wh, wp, *slices, vecs)


def attend_back_tile(
    head, tree, trees, start, keys, order_ref, q_ref, k_ref, v_ref, kt_ref, ot_ref, lse_ref,
    do_ref, dq_s, dk_s, dv_s,
):
    here = slice(start, start + PAIR)
    base = tree * TREE_BLOCKS
    at = head * trees + tree
    grad = []
    for i in range(2):
        grad.append(do_ref[order_ref[tree * TREE_BLOCKS + start // BLOCK + i]])
    do = jnp.concatenate(grad, axis=0)[:, head * HEAD : (head + 1) * HEAD]
    delta = jnp.sum(do.astype(SINGLE).T * ot_ref[at, :, here], axis=0, keepdims=True)
    q = stack(q_ref, head, picks(order_ref, tree, start, PAIR), 0)
    lse = lse_ref[at, :, here]
    dq = 0.0
    for off, size, kind in keys:
        chosen = picks(order_ref, tree, off, size)
        out = slice(base + off // BLOCK, base + (off + size) // BLOCK)
        p = jnp.exp2(dot(stack(k_ref, head, chosen, 0), q, NT) * SCALE - lse)
        if kind:
            p = jnp.where(mask_of(kind), p, 0.0)
        dp = dot(stack(v_ref, head, chosen, 0), do, NT)
        ds = (p * (dp - delta)).astype(HALF)
        dv_s[out] += dot(p.astype(HALF), do).reshape(size // BLOCK, BLOCK, HEAD)
        dk_s[out] += dot(ds, q).reshape(size // BLOCK, BLOCK, HEAD)
        dq = dq + dot(stack(kt_ref, head, chosen, 1), ds)
    first = base + start // BLOCK
    dq_s[first : first + 2] = (dq * 0.125).T.reshape(2, BLOCK, HEAD)


def total_of(*refs):
    return functools.reduce(jnp.add, [r.astype(SINGLE) for r in refs])


def finish_kernel(
    parts,
    copies,
    heads,
    tile,
    order_ref,
    near_hbm,
    q_hbm,
    k_hbm,
    v_hbm,
    kt_hbm,
    ot_hbm,
    lse_hbm,
    do_hbm,
    dh1_hbm,
    wq_hbm,
    wk_hbm,
    wv_hbm,
    pa_hbm,
    pb_hbm,
    norm_in,
    dx_hbm,
    qk_hbm,
    vv_hbm,
    wqk_hbm,
    wvv_hbm,
    fa_ref,
    fb_ref,
    dwf_ref,
    norm_out,
    near_ref,
    q_ref,
    k_ref,
    v_ref,
    kt_ref,
    ot_ref,
    lse_ref,
    do_ref,
    dx_ref,
    wq_ref,
    dq_s,
    dk_s,
    dv_s,
    qk_ref,
    vv_ref,
    qk_in,
    vv_in,
    wqk_ref,
    wvv_ref,
    pa_ref,
    pac_ref,
    par_ref,
    pas_ref,
    paz_ref,
    pb_ref,
    pbc_ref,
    pbr_ref,
    pbs_ref,
    pbz_ref,
    far_ref,
    dws_ref,
    dwc_ref,
    dwz_ref,
    dwp_ref,
    nsum_ref,
    nrecv_ref,
    local_sem,
    send_sem,
    recv_sem,
    row_sem,
):
    wire = Wire(local_sem, send_sem, recv_sem)
    me, rep, near, core, layers, far = places(parts, copies)
    blocks, _, width = near_ref.shape
    total = blocks * BLOCK
    rows = total // parts
    trees = total // TREE_TOK
    per = rows // BLOCK
    depth = width // parts
    side = lax.rem(rep, 2)
    layer = lax.rem(lax.div(rep, 2), LAYERS)
    other = 1 - side
    split = 2 * LAYERS // parts

    def load(source, target, head):
        return wire.keep(source.at[head], target[head])

    def load_tree(source, target, head):
        some = pl.ds(head * trees, trees)
        return wire.keep(source.at[some], target.at[some])

    def load_head(head):
        return [
            load(q_hbm, q_ref, head),
            load(k_hbm, k_ref, head),
            load(v_hbm, v_ref, head),
            load(kt_hbm, kt_ref, head),
            load_tree(ot_hbm, ot_ref, head),
            load_tree(lse_hbm, lse_ref, head),
        ]

    def arrived(copies_in):
        for copy in copies_in:
            copy.wait_recv()

    loads = [[wire.keep(do_hbm, do_ref)] + load_head(0)]
    greet([p for _, p in near] + [core] + [p for _, p in layers] + far)

    halves_out = [
        wire.send(pa_hbm.at[other], pac_ref, *core),
        wire.send(pb_hbm.at[other], pbc_ref, *core),
    ]
    halves_own = [wire.keep(pa_hbm.at[side], pa_ref), wire.keep(pb_hbm.at[side], pb_ref)]
    for h in range(1, heads):
        loads.append(load_head(h))
    near_load = wire.keep(near_hbm, near_ref)
    weight_load = [
        wire.keep(w, wq_ref.at[:, pl.ds(i * width, width)])
        for i, w in enumerate((wq_hbm, wk_hbm, wv_hbm))
    ]
    base_load = wire.keep(dh1_hbm, dx_ref)

    doubling = [core, layers[0][1], layers[1][1]] + far
    bit = 1
    while bit < parts:
        doubling.append(near[bit - 1][1])
        bit *= 2
    nsum_ref[0] = norm_in[...]
    state = {"step": 0, "copy": wire.send(nsum_ref.at[0], nrecv_ref.at[0], *doubling[0])}

    def norm_step():
        i = state["step"]
        if i == len(doubling):
            return
        state["copy"].wait_recv()
        nsum_ref[i + 1] = nsum_ref[i] + nrecv_ref[i]
        state["step"] = i = i + 1
        if i < len(doubling):
            state["copy"] = wire.send(nsum_ref.at[i], nrecv_ref.at[i], *doubling[i])

    def beyond(value, slot):
        for i, p in enumerate(far):
            send, recv = far_ref.at[slot, i, 0], far_ref.at[slot, i, 1]
            n, m = value.shape
            send[0:n, 0:m] = value.astype(HALF)
            copy = wire.send(send, recv, *p)
            copy.wait_recv()
            value = value.astype(HALF).astype(SINGLE) + recv[0:n, 0:m].astype(SINGLE)
        return value.astype(HALF)

    low = pb_ref.shape[2]

    def pack_split():
        arrived(halves_out)
        for copy in halves_own:
            copy.wait()
        for r in range(parts):
            for z in range(LAYERS):
                pa_ref[r, z] = total_of(pa_ref[r, z], pac_ref[r, z]).astype(HALF)
        out_a = [wire.send(pa_ref.at[r], par_ref.at[r - 1], *p) for r, p in near]
        for z in range(LAYERS):
            for r in range(parts):
                pb_ref[z, r] = total_of(pb_ref[z, r], pbc_ref[z, r]).astype(HALF)
        out_b = [wire.send(pb_ref.at[flip(layer, j)], pbr_ref.at[j - 1], *p) for j, p in layers]
        return out_a, out_b

    def pack_a_scatter(waits):
        arrived(waits)
        for z in range(LAYERS):
            pas_ref[z] = total_of(
                pa_ref[0, z], *[par_ref[r, z] for r in range(parts - 1)]
            ).astype(HALF)
        return [wire.send(pas_ref.at[flip(layer, j)], paz_ref.at[j - 1], *p) for j, p in layers]

    def pack_a_spread(waits):
        arrived(waits)
        piece = total_of(pas_ref[layer], *[paz_ref[j] for j in range(LAYERS - 1)])
        fa_ref[side, layer] = beyond(piece, 0)
        here = fa_ref.at[side, layer]
        return [wire.send(here, here, *p) for _, p in layers]

    def pack_b_scatter(waits):
        arrived(waits)
        for r in range(parts):
            piece = total_of(pb_ref[layer, r], *[pbr_ref[j, r] for j in range(LAYERS - 1)])
            pbs_ref[r] = beyond(piece, 3 + r)
        return [wire.send(pbs_ref.at[r], pbz_ref.at[r - 1], *p) for r, p in near]

    def pack_b_spread(waits):
        arrived(waits)
        piece = total_of(pbs_ref[0], *[pbz_ref[r] for r in range(parts - 1)])
        fb_ref[side, layer] = piece.astype(HALF)
        here = fb_ref.at[side, layer]
        return [wire.send(here, here, *p) for _, p in layers]

    def pack_cores(waits):
        arrived(waits)
        return [
            wire.send(fa_ref.at[side], fa_ref.at[side], *core),
            wire.send(fb_ref.at[side], fb_ref.at[side], *core),
        ]

    def weights_cores(head):
        return [wire.send(dws_ref.at[head, other], dwc_ref.at[head], *core)]

    def weights_scatter(head, waits):
        arrived(waits)
        for z in range(LAYERS):
            dws_ref[head, side, z] = total_of(dws_ref[head, side, z], dwc_ref[head, z]).astype(HALF)
        return [
            wire.send(dws_ref.at[head, side, flip(layer, j)], dwz_ref.at[head, j - 1], *p)
            for j, p in layers
        ]

    to_row = layer if split == 2 else side * LAYERS + layer

    def weights_send(head, waits):
        arrived(waits)
        piece = total_of(
            dws_ref[head, side, layer], *[dwz_ref[head, j] for j in range(LAYERS - 1)]
        )
        dwp_ref[head] = beyond(piece, 1 + head)

        @pl.when(to_row == 0)
        def _():
            dwf_ref[head, side, layer] = dwp_ref[head]

        copy = pltpu.make_async_remote_copy(
            dwp_ref.at[head],
            dwf_ref.at[head, side, layer],
            row_sem.at[0, head],
            row_sem.at[1, head],
            device_id={"fsdp": flip_two(me, to_row, parts)},
            device_id_type=MESH,
        )

        @pl.when(to_row != 0)
        def _():
            copy.start()

        return copy

    def weights_spread(head, copy):
        @pl.when(to_row != 0)
        def _():
            copy.wait()

        here = dwf_ref.at[head, side, layer]
        return [wire.send(here, here, *p) for _, p in layers]

    def weights_last(head, waits):
        arrived(waits)
        return [wire.send(dwf_ref.at[head, side], dwf_ref.at[head, side], *core)]

    def unsort(head):
        for r in range(parts):

            def one(j, _):
                place = order_ref[blocks + r * per + j]
                both = jnp.concatenate([dq_s[place], dk_s[place] * 0.125], axis=1)
                qk_ref[head, r, block_at(j), :] = both.astype(HALF)
                lower = pl.ds(pl.multiple_of(j * (BLOCK // 2), BLOCK // 2), BLOCK // 2)
                vv_ref[head, r, lower, :] = fold(dv_s[place]).astype(HALF)
                return 0

            lax.fori_loop(0, per, one, 0)
        if head == heads - 1:
            kept.append(wire.keep(qk_ref.at[head, 0], qk_hbm.at[0]))
            kept.append(wire.keep(vv_ref.at[head, 0], vv_hbm.at[0]))
            return [wire.send(qk_ref.at[head, r], qk_hbm.at[r], *p) for r, p in near]
        qk_in[head, 0] = qk_ref[head, 0]
        vv_in[head, 0] = vv_ref[head, 0]
        return [wire.send(qk_ref.at[head, r], qk_in.at[head, r], *p) for r, p in near]

    def send_values(head):
        if head == heads - 1:
            return [wire.send(vv_ref.at[head, r], vv_hbm.at[r], *p) for r, p in near]
        return [wire.send(vv_ref.at[head, r], vv_in.at[head, r], *p) for r, p in near]

    def weight_grads(head):
        total_dw = 0.0
        for r in range(parts):
            grads = jnp.concatenate([qk_ref[head, r], unfold(vv_ref[head, r])], axis=1)
            total_dw = total_dw + dot(
                grads.T, near_ref[r * per : (r + 1) * per].reshape(rows, width)
            )
        dw = total_dw.astype(HALF)
        for c in range(parts):
            to = flip(me, c)
            piece = dw[:, c * depth : (c + 1) * depth]
            if split == 2:
                dws_ref[head, 0, to] = piece[: piece.shape[0] // 2]
                dws_ref[head, 1, to] = piece[piece.shape[0] // 2 :]
            else:
                dws_ref[head, lax.div(to, LAYERS), lax.rem(to, LAYERS)] = piece

    def turn_weights():
        for h in range(heads):
            for c in range(parts):
                at = (c * heads + h) * HEAD
                wqk_ref[h, :, c * 2 * HEAD : (c + 1) * 2 * HEAD] = jnp.concatenate(
                    [wq_ref[:, at : at + HEAD], wq_ref[:, width + at : width + at + HEAD]], axis=1
                )
                wvv_ref[h, :, c * HEAD : (c + 1) * HEAD] = wq_ref[
                    :, 2 * width + at : 2 * width + at + HEAD
                ]

    def input_grad(head):
        def pick(ref, c, at):
            return ref[head, flip(me, c), at, :]

        def step(i, _):
            at = pl.ds(pl.multiple_of(i * tile, tile), tile)
            lower = pl.ds(pl.multiple_of(i * (tile // 2), tile // 2), tile // 2)
            qk = jnp.concatenate([pick(qk_in, c, at) for c in range(parts)], axis=1)
            vv = jnp.concatenate([unfold(pick(vv_in, c, lower)) for c in range(parts)], axis=1)
            dx_ref[at, :] += dot(qk, wqk_ref[head], NT) + dot(vv, wvv_ref[head], NT)
            return 0

        lax.fori_loop(0, rows // tile, step, 0)

    kept = []
    sent, values, chains = [], [], {}
    for h in range(heads):
        for copy in loads[h]:
            copy.wait()
        dk_s[...] = jnp.zeros_like(dk_s)
        dv_s[...] = jnp.zeros_like(dv_s)
        for number, (begin, keys) in enumerate(tile_list()):
            for tree in range(trees):
                attend_back_tile(
                    h, tree, trees, begin, keys, order_ref, q_ref, k_ref, v_ref, kt_ref, ot_ref,
                    lse_ref, do_ref, dq_s, dk_s, dv_s,
                )
            event = (h, number)
            if event == (0, 4):
                pack_a, pack_b = pack_split()
            elif event == (0, 6) or event == (0, 8):
                norm_step()
            elif event == (1, 1):
                chains[0] = weights_scatter(0, chains[0])
            elif event == (1, 2):
                norm_step()
            elif event == (1, 4):
                pack_a = pack_a_scatter(pack_a)
            elif event == (1, 5):
                chains[0] = weights_send(0, chains[0])
            elif event == (1, 7):
                pack_b = pack_b_scatter(pack_b)
            elif event == (1, 8):
                norm_step()
        sent.append(unsort(h))
        if h == 0:
            near_load.wait()
        if h < heads - 1:
            values.append(send_values(h))
            weight_grads(h)
            chains[h] = weights_cores(h)
    end_head = heads - 1
    if heads == 1:
        pack_a = pack_a_scatter(pack_a)
        pack_b = pack_b_scatter(pack_b)
    weight_grads(end_head)
    chains[end_head] = weights_cores(end_head)
    pack_a = pack_a_spread(pack_a)
    for copy in weight_load + [base_load]:
        copy.wait()
    turn_weights()
    kept.append(wire.keep(wqk_ref.at[end_head], wqk_hbm))
    kept.append(wire.keep(wvv_ref.at[end_head], wvv_hbm))
    chains[end_head] = weights_scatter(end_head, chains[end_head])
    if heads > 1:
        arrived(sent[0] + values[0])
        input_grad(0)
    kept.append(wire.keep(dx_ref, dx_hbm))
    chains[end_head] = weights_send(end_head, chains[end_head])
    values.append(send_values(end_head))
    pack_b = pack_b_spread(pack_b)
    while state["step"] < len(doubling):
        norm_step()
    if heads > 1:
        chains[0] = weights_spread(0, chains[0])
    last = pack_cores(pack_a + pack_b)
    chains[end_head] = weights_spread(end_head, chains[end_head])
    for h in range(heads):
        last += weights_last(h, chains[h])
    norm_out[...] = nsum_ref[len(doubling)]
    arrived(last + sent[end_head] + values[end_head])
    for copy in kept:
        copy.wait()
    wire.finish()


def finish(parts, copies, heads, order, saved, do, dh1, wq, wk, wv, pa, pb, norms):
    near, q, k, v, kt, ot, lse = saved
    blocks, _, width = near.shape
    total = blocks * BLOCK
    rows = total // parts
    depth = width // parts
    tile = PAIR if rows % PAIR == 0 else BLOCK
    split = 2 * LAYERS // parts
    beyonds = max(copies // (2 * LAYERS), 2).bit_length() - 1
    stages = (copies * parts).bit_length()
    flat = ((blocks, BLOCK, HEAD), SINGLE)
    qk = ((heads, parts, rows, 2 * HEAD), HALF)
    vv = ((heads, parts, rows // 2, 2 * HEAD), HALF)
    a, b = pa.shape[1:], pb.shape[1:]
    dws = (LAYERS, 3 * HEAD // split, depth)
    each = lambda r: [pltpu.VMEM(r.shape[1:], r.dtype)] * heads
    scratch = [(r.shape, r.dtype) for r in (ot, lse, do)]
    scratch += [((rows, width), SINGLE), ((width, 3 * width), HALF), flat, flat, flat]
    scratch += [qk, vv, qk, vv]
    scratch += [((heads, width, 2 * HEAD * parts), HALF), ((heads, width, HEAD * parts), HALF)]
    scratch += [(n, HALF) for n in (a, a, (parts - 1,) + a[1:], a[1:])]
    scratch += [((LAYERS - 1,) + a[2:], HALF)]
    scratch += [(n, HALF) for n in (b, b, (LAYERS - 1,) + b[1:], b[1:])]
    scratch += [((parts - 1,) + b[2:], HALF)]
    scratch += [((3 + parts, beyonds, 2, max(3 * HEAD, depth), width), HALF)]
    if copies == 2 * LAYERS:
        scratch[-1] = ((1, 1, 2, 16, width), HALF)
    scratch += [((heads, 2) + dws, HALF), ((heads,) + dws, HALF)]
    scratch += [((heads, LAYERS - 1) + dws[1:], HALF), ((heads,) + dws[1:], HALF)]
    scratch += [((stages, 4, width), SINGLE), ((stages, 4, width), SINGLE)]
    outs = [((rows, width), SINGLE), (qk[0][1:], HALF), (vv[0][1:], HALF)]
    outs += [((width, 2 * HEAD * parts), HALF), ((width, HEAD * parts), HALF)]
    small = [((2, LAYERS) + a[2:], HALF), ((2, LAYERS) + b[2:], HALF), ((heads, 2) + dws, HALF)]
    small += [((4, width), SINGLE)]
    return pl.pallas_call(
        functools.partial(finish_kernel, parts, copies, heads, tile),
        out_shape=[shape(*o) for o in outs + small],
        in_specs=[smem()] + anywhere(14) + vmem(1),
        out_specs=anywhere(len(outs)) + vmem(len(small)),
        scratch_shapes=[pltpu.VMEM(near.shape, HALF)]
        + [each(r) for r in (q, k, v, kt)]
        + [pltpu.VMEM(*s) for s in scratch]
        + copies_of(16 + 6 * heads, 48 + 12 * parts)
        + [pltpu.SemaphoreType.DMA((2, heads))],
        compiler_params=params(2),
        name="finish",
    )(order, near, q, k, v, kt, ot, lse, do, dh1, wq, wk, wv, pa, pb, norms)


def close_kernel(
    parts,
    heads,
    base_ref,
    qk_ref,
    vv_ref,
    out_in,
    wqk_ref,
    wvv_ref,
    fa_ref,
    fb_ref,
    dwf_ref,
    norm_in,
    out_ref,
    dx_ref,
    gq_ref,
    gk_ref,
    gv_ref,
    go_ref,
    gh_ref,
    gp_ref,
    *norm_refs,
):
    me = lax.axis_index("fsdp")
    width = base_ref.shape[1]
    depth = width // parts
    split = 2 * LAYERS // parts
    qk = jnp.concatenate([qk_ref[flip(me, c)] for c in range(parts)], axis=1)
    vv = jnp.concatenate([unfold(vv_ref[flip(me, c)]) for c in range(parts)], axis=1)
    dx_ref[...] = base_ref[...] + dot(qk, wqk_ref[...], NT) + dot(vv, wvv_ref[...], NT)
    out_ref[...] = out_in[...]

    @pl.when(pl.program_id(0) == 0)
    def _():
        for i, ref in enumerate(norm_refs):
            ref[...] = norm_in[i : i + 1, :]
        low = fb_ref.shape[2]
        small = depth // SLICES
        cols = gp_ref.shape[0]
        unit = width // LAYERS
        for z in range(LAYERS):
            here = slice(z * width, (z + 1) * width)
            gh_ref[0:low, here] = fa_ref[0, z, 0:low].astype(SINGLE)
            gh_ref[low:depth, here] = fb_ref[0, z].astype(SINGLE)
            piece = jnp.concatenate([fa_ref[1, z, 0:low], fb_ref[1, z]], axis=0).astype(SINGLE)
            if cols < width:
                piece = jnp.concatenate([piece[:, :cols], piece[:, cols:]], axis=0)
            gp_ref[:, z * unit : (z + 1) * unit] = piece.T
            for i in range(2):
                at = (i * LAYERS + z) * small
                go_ref[at : at + small, :] = fa_ref[i, z, low : low + small].astype(SINGLE)
        for c in range(parts):
            for h in range(heads):
                r = flip(me, c)
                if split == 2:
                    piece = jnp.concatenate([dwf_ref[h, 0, r], dwf_ref[h, 1, r]], axis=0)
                else:
                    piece = dwf_ref[h, lax.div(r, LAYERS), lax.rem(r, LAYERS)]
                turned = piece.astype(SINGLE).T
                at = (c * heads + h) * HEAD
                for ref, k in ((gq_ref, 0), (gk_ref, 1), (gv_ref, 2)):
                    ref[:, at : at + HEAD] = turned[:, k * HEAD : (k + 1) * HEAD]


def close(parts, heads, output, base, qk, vv, wqk, wvv, fa, fb, dwf, norms, inner):
    rows, width = base.shape
    tile = PAIR if rows % PAIR == 0 else BLOCK
    depth = width // parts
    row = pl.BlockSpec((tile, width), lambda i: (i, 0))
    once = lambda a: pl.BlockSpec(a, lambda i: (0,) * len(a), pipeline_mode=pl.Buffered(1))
    last = lambda a: pl.BlockSpec(a, lambda i: (0,) * len(a))
    grads = [(depth, width)] * 4 + [(depth, inner), (inner // parts, width)] + [(1, width)] * 4
    return pl.pallas_call(
        functools.partial(close_kernel, parts, heads),
        grid=(rows // tile,),
        in_specs=[
            row,
            pl.BlockSpec((parts, tile, 2 * HEAD), lambda i: (0, i, 0)),
            pl.BlockSpec((parts, tile // 2, 2 * HEAD), lambda i: (0, i, 0)),
            row,
        ]
        + [once(a.shape) for a in (wqk, wvv, fa, fb, dwf, norms)],
        out_specs=[row, row] + [last(g) for g in grads],
        out_shape=[shape((rows, width), HALF), shape((rows, width), SINGLE)]
        + [shape(g, SINGLE) for g in grads],
        compiler_params=pltpu.CompilerParams(vmem_limit_bytes=VMEM_LIMIT),
        name="close",
    )(base, qk, vv, output, wqk, wvv, fa, fb, dwf, norms)


def shards(
    parts,
    copies,
    inputs,
    cotangent,
    segments,
    trees,
    parents,
    w_query,
    w_key,
    w_value,
    w_out,
    w_hidden,
    w_proj,
    norm1_gain,
    norm1_bias,
    norm2_gain,
    norm2_bias,
):
    x = inputs[0]
    rows, width = x.shape
    inner = w_hidden.shape[1]
    heads = HEADS // parts
    wide = heads * HEAD
    depth = width // parts
    me = lax.axis_index("fsdp")
    order = block_order(segments[0], trees[0], parents[0], rows, me)
    by = [w_query, w_key, w_value]
    if wide % BLOCK:
        by = jnp.concatenate([w.reshape(depth, parts, wide) for w in by], axis=2)
        by = [by.transpose(1, 0, 2)]
    cut = lambda w: w.reshape(SLICES, w.shape[0] // SLICES, w.shape[1])
    whole = lambda w: w.reshape(-1, w.shape[-1])
    slices = [cut(w) for w in (w_out, w_hidden, w_proj)]
    near, q, k, v, kt, ot, lse, ctx, *gathered = start(parts, copies, heads, order, x, by, slices)
    vecs = [n.reshape(1, width) for n in (norm1_gain, norm1_bias, norm2_gain, norm2_bias)]
    output, dh1, do, pa, pb, wq, wk, wv, norms = middle(
        parts,
        copies,
        heads,
        x,
        cotangent[0],
        ctx,
        *[whole(w) for w in gathered],
        [cut(w) for w in (w_query, w_key, w_value)],
        vecs,
    )
    saved = (near, q, k, v, kt, ot, lse)
    do = do.reshape(-1, BLOCK, wide)
    weights = [whole(w) for w in (wq, wk, wv)]
    left = finish(parts, copies, heads, order, saved, do, dh1, *weights, pa, pb, norms)
    output, input_grad, *grads = close(parts, heads, output, *left, inner)
    return (output[None], input_grad[None], *grads[:6], *[n.reshape(width) for n in grads[6:]])


def solution(mesh):
    token = P("rep", "fsdp", None)
    weight = P("fsdp", None)
    placed = (token, token, P("rep", None), P("rep", None), P("rep", None, None))
    return jax.shard_map(
        functools.partial(shards, mesh.shape["fsdp"], mesh.shape["rep"]),
        mesh=mesh,
        in_specs=placed + (weight,) * 6 + (P(),) * 4,
        out_specs=(token, token) + (weight,) * 6 + (P(),) * 4,
        check_vma=False,
    )
```

```python
import functools

import jax
import jax.numpy as jnp
from jax import lax
from jax.experimental import pallas as pl
from jax.experimental.pallas import tpu as pltpu
from jax.sharding import PartitionSpec as P

HEADS = 8
HEAD = 64
BLOCK = 128
PAIR = 2 * BLOCK
TRUNK = 8
BRANCHES = 4
LEAVES = 8
TREE_BLOCKS = TRUNK + BRANCHES + LEAVES
TREE_TOK = TREE_BLOCKS * BLOCK
SINGLE = jnp.float32
HALF = jnp.bfloat16
NN = (((1,), (0,)), ((), ()))
NT = (((1,), (1,)), ((), ()))
LOG2E = 1.4426950408889634
SCALE = 0.125 * LOG2E
VMEM_LIMIT = 58 << 20
MESH = pl.DeviceIdType.MESH
SLICES = 8
LAYERS = 4


def dot(left, right, dims=NN):
    return lax.dot_general(left, right, dims, preferred_element_type=SINGLE)


def row_mean(values):
    return jnp.mean(values, axis=-1, keepdims=True)


def block_order(segments, trees, parents, rows, me):
    seg = segments.reshape(-1, BLOCK)[:, 0]
    tree = trees.reshape(-1, BLOCK)[:, 0]
    count = seg.shape[0]
    table = parents.reshape(-1)
    slot = tree * parents.shape[1] + seg
    parent = jnp.sum(
        jnp.where(slot[:, None] == jnp.arange(table.shape[0])[None, :], table[None, :], 0), axis=1
    )
    place = jnp.arange(count, dtype=jnp.int32)
    kind = jnp.where(seg == 0, 0, jnp.where(seg <= BRANCHES, seg, 16 * parent + seg))
    key = (tree * 256 + kind) * 64 + place
    rank = jnp.sum((key[None, :] < key[:, None]).astype(jnp.int32), axis=1)
    per = rows // BLOCK
    near = ((place // per) ^ me) * per + place % per
    order = jnp.sum(jnp.where(rank[None, :] == place[:, None], near[None, :], 0), axis=1)
    back = jnp.sum(jnp.where(near[None, :] == place[:, None], rank[None, :], 0), axis=1)
    return jnp.concatenate([order, back]).astype(jnp.int32)


def tile_list():
    out = []
    trunk = TRUNK * BLOCK
    for start in range(0, trunk, PAIR):
        keys = [(0, start, None)] if start else []
        out.append((start, keys + [(start, PAIR, "causal")]))
    for pair in range(BRANCHES // 2):
        start = trunk + pair * PAIR
        out.append((start, [(0, trunk, None), (start, PAIR, "own")]))
    for branch in range(BRANCHES):
        start = trunk + BRANCHES * BLOCK + branch * PAIR
        out.append(
            (
                start,
                [(0, trunk, None), (trunk + branch * BLOCK, BLOCK, None), (start, PAIR, "own")],
            )
        )
    return out


def mask_of(kind):
    key = lax.broadcasted_iota(jnp.int32, (PAIR, PAIR), 0)
    query = lax.broadcasted_iota(jnp.int32, (PAIR, PAIR), 1)
    mask = key <= query
    if kind == "own":
        mask = mask & ((key >= BLOCK) == (query >= BLOCK))
    return mask


def flip(value, bits):
    bit = 1
    while bit <= bits:
        if bits & bit:
            value = value + bit - 2 * bit * lax.rem(lax.div(value, bit), 2)
        bit *= 2
    return value


def flip_two(one, two, size):
    out = 0
    bit = 1
    while bit < size:
        out = out + bit * lax.rem(lax.rem(lax.div(one, bit), 2) + lax.rem(lax.div(two, bit), 2), 2)
        bit *= 2
    return out


class Wire:
    def __init__(self, local_sem, send_sem, recv_sem):
        self.local_sem, self.send_sem, self.recv_sem = local_sem, send_sem, recv_sem
        self.locals = self.remotes = 0
        self.open = []

    def keep(self, source, target):
        copy = pltpu.make_async_copy(source, target, self.local_sem.at[self.locals])
        self.locals += 1
        copy.start()
        return copy

    def plan(self, source, target, axis, peer):
        copy = pltpu.make_async_remote_copy(
            source,
            target,
            self.send_sem.at[self.remotes],
            self.recv_sem.at[self.remotes],
            device_id={axis: peer},
            device_id_type=MESH,
        )
        self.remotes += 1
        self.open.append(copy)
        return copy

    def send(self, *route):
        copy = self.plan(*route)
        copy.start()
        return copy

    def finish(self):
        for copy in self.open:
            copy.wait_send()


def greet(peers):
    barrier = pltpu.get_barrier_semaphore()
    for axis, peer in peers:
        pl.semaphore_signal(barrier, inc=1, device_id={axis: peer}, device_id_type=MESH)
    pl.semaphore_wait(barrier, len(peers))


def places(parts, copies):
    me = lax.axis_index("fsdp")
    rep = lax.axis_index("rep")
    near = [(r, ("fsdp", flip(me, r))) for r in range(1, parts)]
    core = ("rep", flip(rep, 1))
    layers = [(j, ("rep", flip(rep, 2 * j))) for j in range(1, LAYERS)]
    far = []
    bit = 2 * LAYERS
    while bit < copies:
        far.append(("rep", flip(rep, bit)))
        bit *= 2
    return me, rep, near, core, layers, far


class Gather:
    def __init__(self, wire, spots, shards_in, full):
        self.wire, self.spots, self.shards_in, self.full = wire, spots, shards_in, full
        me, rep, near, core, layers, far = spots
        self.side = lax.rem(rep, 2)
        mine = self.side * LAYERS + lax.rem(lax.div(rep, 2), LAYERS)
        half = pl.ds(self.side * LAYERS, LAYERS)
        others = [flip(me, r) for r, _ in near]
        pairs = list(zip(shards_in, full))
        self.own = []
        self.stages = [
            [wire.plan(a.at[mine], b.at[me, mine], *p) for _, p in near for a, b in pairs],
            [
                wire.plan(b.at[c, mine], b.at[c, mine], *p)
                for _, p in layers
                for c in others
                for b in full
            ],
            [wire.plan(b.at[c, half], b.at[c, half], *core) for c in others for b in full],
        ]

    def start(self):
        for copy in self.stages[0]:
            copy.start()
        me = self.spots[0]
        self.own = [self.wire.keep(a, b.at[me]) for a, b in zip(self.shards_in, self.full)]

    def step(self, i):
        for copy in self.stages[i - 1]:
            copy.wait_recv()
        for copy in self.stages[i]:
            copy.start()

    def end(self):
        for copy in self.stages[2]:
            copy.wait_recv()
        for copy in self.own:
            copy.wait()


def picks(order_ref, tree, start, size):
    first = tree * TREE_BLOCKS + start // BLOCK
    return [order_ref[first + i] for i in range(size // BLOCK)]


def stack(ref, head, chosen, axis):
    blocks = [ref[head][i] for i in chosen]
    return jnp.concatenate(blocks, axis=axis) if len(blocks) > 1 else blocks[0]


def attend_head(head, trees, order_ref, q_ref, k_ref, vt_ref, ot_ref, lse_ref, flat_ref):
    def scores_of(tree, start, keys):
        q = stack(q_ref, head, picks(order_ref, tree, start, PAIR), 0)
        scores = []
        for off, size, kind in keys:
            s = dot(stack(k_ref, head, picks(order_ref, tree, off, size), 0), q, NT)
            if kind:
                s = jnp.where(mask_of(kind), s, -1e30)
            scores.append(s)
        return scores

    def finish_tile(tree, start, keys, scores):
        here = slice(start, start + PAIR)
        at = head * trees + tree
        top = functools.reduce(jnp.maximum, [jnp.max(s, axis=0, keepdims=True) for s in scores])
        top = top * SCALE
        mass = 0.0
        acc = 0.0
        for (off, size, _), s in zip(keys, scores):
            e = jnp.exp2(s * SCALE - top)
            mass = mass + jnp.sum(e, axis=0, keepdims=True)
            vt = stack(vt_ref, head, picks(order_ref, tree, off, size), 1)
            acc = acc + dot(vt, e.astype(HALF))
        out = acc * (1.0 / mass)
        lse_ref[at, :, here] = top + jnp.log2(mass)
        ot_ref[at, :, here] = out
        place = tree * TREE_BLOCKS + start // BLOCK
        flat_ref[place : place + 2] = out.T.astype(HALF).reshape(2, BLOCK, HEAD)

    held = []
    for start, keys in tile_list():
        for tree in range(trees):
            held.append((tree, start, keys, scores_of(tree, start, keys)))
            if len(held) > 2:
                finish_tile(*held.pop(0))
    for tile in held:
        finish_tile(*tile)


def fold(block):
    return jnp.concatenate([block[: BLOCK // 2], block[BLOCK // 2 :]], axis=1)


def unfold(packed):
    parts = []
    for i in range(packed.shape[0] // (BLOCK // 2)):
        piece = packed[i * (BLOCK // 2) : (i + 1) * (BLOCK // 2)]
        parts += [piece[:, :HEAD], piece[:, HEAD:]]
    return jnp.concatenate(parts, axis=0)


def block_at(index):
    return pl.ds(pl.multiple_of(index * BLOCK, BLOCK), BLOCK)


def start_kernel(
    parts,
    copies,
    heads,
    order_ref,
    x_hbm,
    by_hbm,
    so_hbm,
    sh_hbm,
    sp_hbm,
    near_hbm,
    q_hbm,
    k_hbm,
    v_hbm,
    kt_hbm,
    ot_hbm,
    lse_hbm,
    ctx_hbm,
    wo_hbm,
    wh_hbm,
    wp_hbm,
    near_ref,
    own_ref,
    q_ref,
    k_ref,
    v_ref,
    kt_ref,
    vt_ref,
    ot_ref,
    lse_ref,
    flat_ref,
    ctx_ref,
    local_sem,
    send_sem,
    recv_sem,
):
    wire = Wire(local_sem, send_sem, recv_sem)
    spots = places(parts, copies)
    me, rep, near, core, layers, far = spots
    per = x_hbm.shape[0]
    blocks = parts * per
    trees = blocks // TREE_BLOCKS
    wide = heads * HEAD
    greet([p for _, p in near] + [core] + [p for _, p in layers])

    def own_piece(device):
        if len(by_hbm) == 1:
            return [(by_hbm[0].at[device], own_ref.at[me])]
        at = pl.ds(pl.multiple_of(device * wide, wide), wide)
        return [
            (w.at[:, at], own_ref.at[me, :, pl.ds(i * wide, wide)]) for i, w in enumerate(by_hbm)
        ]

    kept = [wire.keep(*pair) for pair in own_piece(me)]
    kept.append(wire.keep(x_hbm, near_ref.at[pl.ds(0, per)]))
    own_copies = [wire.send(*pair, *p) for _, p in near for pair in own_piece(p[1])]
    gather = Gather(wire, spots, (so_hbm, sh_hbm, sp_hbm), (wo_hbm, wh_hbm, wp_hbm))
    gather.start()

    def project(first, count):
        weight = own_ref[...].reshape(parts * own_ref.shape[1], 3 * wide)
        x = near_ref[first : first + count].reshape(count * BLOCK, near_ref.shape[2])
        out = dot(x, weight).astype(HALF)
        for i in range(count):
            block = out[i * BLOCK : (i + 1) * BLOCK]
            kt = block[:, wide : 2 * wide].T
            vt = block[:, 2 * wide :].T
            for h in range(heads):
                cols = slice(h * HEAD, (h + 1) * HEAD)
                q_ref[h, first + i] = block[:, cols]
                k_ref[h, first + i] = block[:, wide:][:, cols]
                v_ref[h, first + i] = block[:, 2 * wide :][:, cols]
                kt_ref[h, first + i] = kt[cols]
                vt_ref[h, first + i] = vt[cols]

    def wait_all(copies_in):
        for copy in copies_in:
            copy.wait_recv()

    if parts == 4:
        cuts = [i * per // 4 for i in range(5)]

        def part(chunk, i):
            return pl.ds(chunk * per + cuts[i], cuts[i + 1] - cuts[i])

        (_, px), (_, py), _ = near
        one, two = {}, {}
        for a, b in zip((0, 1, 2, 3), (2, 3, 0, 1)):
            one[a] = wire.send(x_hbm.at[part(0, a)], near_ref.at[part(1, a)], *px)
            two[b] = wire.send(x_hbm.at[part(0, b)], near_ref.at[part(2, b)], *py)
        three = {}
        for a, b in ((0, 2), (1, 3)):
            one[a].wait_recv()
            three[a] = wire.send(near_ref.at[part(1, a)], near_ref.at[part(3, a)], *py)
            two[b].wait_recv()
            three[b] = wire.send(near_ref.at[part(2, b)], near_ref.at[part(3, b)], *px)
            if a == 0:
                gather.step(1)
                for copy in kept:
                    copy.wait()
                wait_all(own_copies)
                project(0, per)
        wait_all([one[2], one[3]])
        project(per, per)
        wait_all([two[0], two[1]])
        project(2 * per, per)
        wait_all([three[0], three[2]])
        project(3 * per, cuts[1])
        project(3 * per + cuts[2], cuts[3] - cuts[2])
        wait_all([three[1], three[3]])
        project(3 * per + cuts[1], cuts[2] - cuts[1])
        project(3 * per + cuts[3], cuts[4] - cuts[3])
    else:
        waits = [wire.send(x_hbm, near_ref.at[pl.ds(r * per, per)], *p) for r, p in near]
        gather.step(1)
        for copy in kept:
            copy.wait()
        wait_all(own_copies + waits)
        for r in range(parts):
            project(r * per, per)
    saves = [wire.keep(near_ref, near_hbm)]
    saves += [
        wire.keep(a, b)
        for a, b in ((q_ref, q_hbm), (k_ref, k_hbm), (v_ref, v_hbm), (kt_ref, kt_hbm))
    ]
    context = []
    for h in range(heads):
        if h == heads - 1:
            gather.step(2)
        views = [[ref.at[i] for i in range(heads)] for ref in (q_ref, k_ref, vt_ref)]
        attend_head(h, trees, order_ref, *views, ot_ref, lse_ref, flat_ref)
        for r in range(parts):

            def unsort(j, _):
                block = flat_ref[order_ref[blocks + r * per + j]]
                at = pl.ds(pl.multiple_of(j * (BLOCK // 2), BLOCK // 2), BLOCK // 2)
                ctx_ref[h, r, at, :] = fold(block)
                return 0

            lax.fori_loop(0, per, unsort, 0)
            if r:
                context.append(wire.send(ctx_ref.at[h, r], ctx_hbm.at[h, r], *near[r - 1][1]))
            else:
                saves.append(wire.keep(ctx_ref.at[h, 0], ctx_hbm.at[h, 0]))
        some = pl.ds(h * trees, trees)
        saves.append(wire.keep(ot_ref.at[some], ot_hbm.at[some]))
        saves.append(wire.keep(lse_ref.at[some], lse_hbm.at[some]))
    wait_all(context)
    gather.end()
    for copy in saves:
        copy.wait()
    wire.finish()


def anywhere(count):
    return [pl.BlockSpec(memory_space=pl.ANY)] * count


def vmem(count):
    return [pl.BlockSpec(memory_space=pltpu.VMEM)] * count


def smem():
    return pl.BlockSpec(memory_space=pltpu.SMEM)


def shape(dims, dtype):
    return jax.ShapeDtypeStruct(dims, dtype)


def copies_of(count_local, count_remote):
    return [
        pltpu.SemaphoreType.DMA((count_local,)),
        pltpu.SemaphoreType.DMA((count_remote,)),
        pltpu.SemaphoreType.DMA((count_remote,)),
    ]


def params(number):
    return pltpu.CompilerParams(
        vmem_limit_bytes=VMEM_LIMIT, collective_id=number, has_side_effects=True
    )


def start(parts, copies, heads, order, x, by, slices):
    rows, width = x.shape
    total = parts * rows
    trees = total // TREE_TOK
    n = trees * heads
    tok = ((heads, total // BLOCK, BLOCK, HEAD), HALF)
    turned = ((heads, total // BLOCK, HEAD, BLOCK), HALF)
    near = ((total // BLOCK, BLOCK, width), HALF)
    ot = ((n, HEAD, TREE_TOK), SINGLE)
    lse = ((n, 1, TREE_TOK), SINGLE)
    ctx = ((heads, parts, rows // 2, 2 * HEAD), HALF)
    outs = [near, tok, tok, tok, turned, ot, lse, ctx]
    outs += [((parts,) + w.shape, HALF) for w in slices]
    scratch = [near, ((parts, width // parts, 3 * heads * HEAD), HALF), tok, tok, tok, turned, turned, ot, lse]
    scratch += [((total // BLOCK, BLOCK, HEAD), HALF), ctx]
    return pl.pallas_call(
        functools.partial(start_kernel, parts, copies, heads),
        out_shape=[shape(*o) for o in outs],
        in_specs=[smem(), *anywhere(1), anywhere(len(by)), *anywhere(3)],
        out_specs=anywhere(len(outs)),
        scratch_shapes=[pltpu.VMEM(*s) for s in scratch]
        + copies_of(12 + 3 * heads, 32 + (parts - 1) * 24),
        compiler_params=params(0),
        name="start",
    )(order, x.reshape(rows // BLOCK, BLOCK, width), by, *slices)


def middle_kernel(
    parts,
    copies,
    heads,
    tile,
    x_hbm,
    dy_hbm,
    ctx_hbm,
    wo_hbm,
    wh_hbm,
    wp_hbm,
    sq_hbm,
    sk_hbm,
    sv_hbm,
    vec_refs,
    out_hbm,
    dh1_hbm,
    do_hbm,
    pa_hbm,
    pb_hbm,
    wq_hbm,
    wk_hbm,
    wv_hbm,
    norm_out,
    norm_ref,
    norm_s,
    norm_r,
    x_ref,
    dy_ref,
    ctx_ref,
    wo_ref,
    wh_ref,
    wp_ref,
    out_ref,
    dh1_ref,
    do_ref,
    pa_ref,
    pb_ref,
    cat_ref,
    u_ref,
    df_ref,
    da_ref,
    g_ref,
    dz_ref,
    d_s,
    local_sem,
    send_sem,
    recv_sem,
    tile_sem,
    out_sem,
):
    wire = Wire(local_sem, send_sem, recv_sem)
    spots = places(parts, copies)
    me, rep, near, core, layers, far = spots
    rows, width = x_ref.shape
    inner = wh_ref.shape[1]
    wide = heads * HEAD
    chunk = 512
    count = rows // tile
    loads = [
        wire.keep(ctx_hbm, ctx_ref),
        wire.keep(wo_hbm, wo_ref),
        wire.keep(x_hbm, x_ref),
        wire.keep(wh_hbm, wh_ref),
        wire.keep(wp_hbm, wp_ref),
        wire.keep(dy_hbm, dy_ref),
    ]
    greet([p for _, p in near] + [core] + [p for _, p in layers] + far)
    gather = Gather(wire, spots, (sq_hbm, sk_hbm, sv_hbm), (wq_hbm, wk_hbm, wv_hbm))
    gather.start()
    gain1, bias1, gain2, bias2 = [ref[...] for ref in vec_refs]
    norm_ref[...] = jnp.zeros_like(norm_ref)
    for copy in loads:
        copy.wait()

    def rows_out(i, at):
        return [
            pltpu.make_async_copy(out_ref.at[at], out_hbm.at[at], out_sem.at[2 * i]),
            pltpu.make_async_copy(dh1_ref.at[at], dh1_hbm.at[at], out_sem.at[2 * i + 1]),
        ]

    def rows_sent(i, at):
        return [
            pltpu.make_async_remote_copy(
                do_ref.at[r, at],
                do_hbm.at[r, at],
                tile_sem.at[0, i * parts + r],
                tile_sem.at[1, i * parts + r],
                device_id={p[0]: p[1]},
                device_id_type=MESH,
            )
            for r, p in near
        ] + [
            pltpu.make_async_copy(do_ref.at[0, at], do_hbm.at[0, at], tile_sem.at[0, i * parts])
        ]

    def tile_rows(i):
        return pl.ds(pl.multiple_of(i * tile, tile), tile)

    def tile_step(i, _):
        at = tile_rows(i)
        packed = pl.ds(pl.multiple_of(i * (tile // 2), tile // 2), tile // 2)
        ctx = jnp.concatenate(
            [
                unfold(ctx_ref[h, flip(me, c), packed, :])
                for c in range(parts)
                for h in range(heads)
            ],
            axis=-1,
        )
        cat_ref[at, :] = ctx
        h1 = x_ref[at, :].astype(SINGLE) + dot(ctx, wo_ref[...])
        c1 = h1 - row_mean(h1)
        r1 = lax.rsqrt(row_mean(c1 * c1) + 1e-5)
        n1 = c1 * r1
        y1 = n1 * gain1 + bias1
        u = y1.astype(HALF)
        u_ref[at, :] = u
        branch = 0.0
        spans = [slice(j, j + chunk) for j in range(0, inner, chunk)]
        later = dot(u, wh_ref[:, spans[0]])
        for n, s in enumerate(spans):
            z = later
            if n + 1 < len(spans):
                later = dot(u, wh_ref[:, spans[n + 1]])
            cdf = 0.5 * (1.0 + lax.erf(z * 0.7071067811865476))
            pdf = jnp.exp2(z * z * (-0.5 * LOG2E)) * 0.3989422804014327
            g = (z * cdf).astype(HALF)
            g_ref[at, s] = g
            d_s[:, s] = cdf + z * pdf
            branch = branch + dot(g, wp_ref[s, :])
        h2 = y1 + branch
        c2 = h2 - row_mean(h2)
        r2 = lax.rsqrt(row_mean(c2 * c2) + 1e-5)
        n2 = c2 * r2
        out_ref[at, :] = (n2 * gain2 + bias2).astype(HALF)
        dy = dy_ref[at, :].astype(SINGLE)
        norm_ref[2:3, :] += jnp.sum(dy * n2, axis=0, keepdims=True)
        norm_ref[3:4, :] += jnp.sum(dy, axis=0, keepdims=True)
        dn2 = dy * gain2
        dh2 = r2 * (dn2 - row_mean(dn2) - n2 * row_mean(dn2 * n2))
        df = dh2.astype(HALF)
        df_ref[at, :] = df
        back = 0.0
        later = dot(df, wp_ref[spans[0], :], NT)
        for n, s in enumerate(spans):
            dg = later
            if n + 1 < len(spans):
                later = dot(df, wp_ref[spans[n + 1], :], NT)
            dz = (dg * d_s[:, s]).astype(HALF)
            dz_ref[at, s] = dz
            back = back + dot(dz, wh_ref[:, s], NT)
        dy1 = dh2 + back
        norm_ref[0:1, :] += jnp.sum(dy1 * n1, axis=0, keepdims=True)
        norm_ref[1:2, :] += jnp.sum(dy1, axis=0, keepdims=True)
        dn1 = dy1 * gain1
        dh1 = r1 * (dn1 - row_mean(dn1) - n1 * row_mean(dn1 * n1))
        dh1_ref[at, :] = dh1
        da = dh1.astype(HALF)
        da_ref[at, :] = da
        dctx = dot(da, wo_ref[...], NT).astype(HALF)
        for c in range(parts):
            do_ref[flip(me, c), at, :] = dctx[:, c * wide : (c + 1) * wide]
        for copy in rows_out(i, at) + rows_sent(i, at):
            copy.start()
        for stage in (1, 2):

            @pl.when(i == 2 * (stage - 1))
            def _():
                gather.step(stage)

        return 0

    lax.fori_loop(0, count, tile_step, 0)
    depth = width // parts
    cols = inner // parts
    low = depth // 2
    unit = width // LAYERS
    small = depth // SLICES

    def put(side, c, z, piece):
        to = flip(me, c)
        pa_ref[side, to, z, 0:low] = piece[:low]
        pb_ref[side, z, to] = piece[low:]

    layer = lax.rem(lax.div(rep, 2), LAYERS)
    norm_s[0] = norm_ref[...]
    sums = [wire.send(norm_s.at[0], norm_r.at[0, 0], *core)]

    def norm_layers():
        sums[0].wait_recv()
        norm_s[1] = norm_s[0] + norm_r[0, 0]
        norm_r[1, 0] = norm_s[1]
        return [wire.send(norm_s.at[1], norm_r.at[1, j], *p) for j, p in layers]

    def norm_group():
        for copy in sums:
            copy.wait_recv()
        total = functools.reduce(jnp.add, [norm_r[1, flip(layer, c)] for c in range(LAYERS)])
        for i, p in enumerate(far):
            norm_s[3 + i] = total
            copy = wire.send(norm_s.at[3 + i], norm_r.at[3 + i, 0], *p)
            copy.wait_recv()
            total = total + norm_r[3 + i, 0]
        norm_s[2] = total
        norm_r[2, 0] = total
        return [wire.send(norm_s.at[2], norm_r.at[2, r], *p) for r, p in near]

    df_t = df_ref[...].T
    for c in range(parts):
        grad = dot(df_t, g_ref[:, c * cols : (c + 1) * cols]).astype(HALF)
        for z in range(LAYERS):
            piece = grad[z * unit : (z + 1) * unit]
            if cols < width:
                piece = jnp.concatenate([piece[:depth], piece[depth:]], axis=1)
            put(1, c, z, piece)
        if c == parts // 2 - 1:
            sums = norm_layers()
    sums = norm_group()
    u_t = u_ref[...].T
    for z in range(LAYERS):
        grad = dot(u_t, dz_ref[:, z * width : (z + 1) * width]).astype(HALF)
        for c in range(parts):
            put(0, c, z, grad[c * depth : (c + 1) * depth])
    grad = dot(cat_ref[...].T, da_ref[...]).astype(HALF)
    for c in range(parts):
        for side in range(2):
            for z in range(LAYERS):
                at = c * depth + (side * LAYERS + z) * small
                pa_ref[side, flip(me, c), z, low : low + small] = grad[at : at + small]
    saves = [wire.keep(pa_ref, pa_hbm), wire.keep(pb_ref, pb_hbm)]

    def tile_end(i, _):
        at = tile_rows(i)
        for copy in rows_out(i, at):
            copy.wait()
        sent = rows_sent(i, at)
        for copy in sent:
            copy.wait()
        return 0

    lax.fori_loop(0, count, tile_end, 0)
    for copy in sums:
        copy.wait_recv()
    norm_out[...] = functools.reduce(jnp.add, [norm_r[2, flip(me, c)] for c in range(parts)])
    for copy in saves:
        copy.wait()
    gather.end()
    wire.finish()


def middle(parts, copies, heads, x, dy, ctx, wo, wh, wp, slices, vecs):
    rows, width = x.shape
    inner = wp.shape[0]
    tile = PAIR if rows % PAIR == 0 else BLOCK
    depth = width // parts
    wide = heads * HEAD
    tok = ((rows, width), HALF)
    full = ((rows, width), SINGLE)
    do = ((parts, rows, wide), HALF)
    pack = ((2, parts, LAYERS, depth // 2 + depth // SLICES, width), HALF)
    pack_b = ((2, LAYERS, parts, depth // 2, width), HALF)
    big = ((rows, inner), HALF)
    outs = [tok, full, do, pack, pack_b] + [((parts,) + w.shape, HALF) for w in slices]
    stages = copies.bit_length() + 1
    norm = (4, width)
    scratch = [(norm, SINGLE), ((stages,) + norm, SINGLE)]
    scratch += [((stages, max(parts, LAYERS)) + norm, SINGLE)]
    scratch += [tok, tok, (ctx.shape, HALF), ((width, width), HALF), ((width, inner), HALF)]
    scratch += [((inner, width), HALF), tok, full, do, pack, pack_b, tok, tok, tok, tok, big, big]
    scratch += [((tile, inner), SINGLE)]
    count = rows // tile
    return pl.pallas_call(
        functools.partial(middle_kernel, parts, copies, heads, tile),
        out_shape=[shape(*o) for o in outs] + [shape((4, width), SINGLE)],
        in_specs=[*anywhere(9), vmem(4)],
        out_specs=anywhere(len(outs)) + vmem(1),
        scratch_shapes=[pltpu.VMEM(*s) for s in scratch]
        + copies_of(12, 24 * parts)
        + [
            pltpu.SemaphoreType.DMA((2, count * parts)),
            pltpu.SemaphoreType.DMA((2 * count,)),
        ],
        compiler_params=params(1),
        name="middle",
    )(x, dy, ctx, wo, wh, wp, *slices, vecs)


class BackTile:
    def __init__(self, head, tree, trees, start, order_ref, ot_ref, lse_ref, do_ref, q_ref):
        here = slice(start, start + PAIR)
        self.head, self.tree, self.order_ref = head, tree, order_ref
        self.base = tree * TREE_BLOCKS
        self.first = self.base + start // BLOCK
        at = head * trees + tree
        do = jnp.concatenate([do_ref[order_ref[self.first + i]] for i in range(2)], axis=0)
        self.do = do[:, head * HEAD : (head + 1) * HEAD]
        self.delta = jnp.sum(
            self.do.astype(SINGLE).T * ot_ref[at, :, here], axis=0, keepdims=True
        )
        self.q = stack(q_ref, head, picks(order_ref, tree, start, PAIR), 0)
        self.lse = lse_ref[at, :, here]
        self.dq = 0.0

    def open(self, key, k_ref, v_ref):
        chosen = picks(self.order_ref, self.tree, key[0], key[1])
        s = dot(stack(k_ref, self.head, chosen, 0), self.q, NT)
        return self, key, chosen, s, dot(stack(v_ref, self.head, chosen, 0), self.do, NT)

    def close(self, key, chosen, s, dp, last, kt_ref, dq_s, dk_s, dv_s):
        off, size, kind = key
        out = slice(self.base + off // BLOCK, self.base + (off + size) // BLOCK)
        p = jnp.exp2(s * SCALE - self.lse)
        if kind:
            p = jnp.where(mask_of(kind), p, 0.0)
        ds = (p * (dp - self.delta)).astype(HALF)
        dv_s[out] += dot(p.astype(HALF), self.do).reshape(size // BLOCK, BLOCK, HEAD)
        dk_s[out] += dot(ds, self.q).reshape(size // BLOCK, BLOCK, HEAD)
        self.dq = self.dq + dot(stack(kt_ref, self.head, chosen, 1), ds)
        if last:
            dq_s[self.first : self.first + 2] = (self.dq * 0.125).T.reshape(2, BLOCK, HEAD)


def total_of(*refs):
    return functools.reduce(jnp.add, [r.astype(SINGLE) for r in refs])


def finish_kernel(
    parts,
    copies,
    heads,
    tile,
    order_ref,
    near_hbm,
    q_hbm,
    k_hbm,
    v_hbm,
    kt_hbm,
    ot_hbm,
    lse_hbm,
    do_hbm,
    dh1_hbm,
    wq_hbm,
    wk_hbm,
    wv_hbm,
    pa_hbm,
    pb_hbm,
    dx_hbm,
    qk_hbm,
    vv_hbm,
    wqk_hbm,
    wvv_hbm,
    fa_ref,
    fb_ref,
    dwf_ref,
    near_ref,
    q_ref,
    k_ref,
    v_ref,
    kt_ref,
    ot_ref,
    lse_ref,
    do_ref,
    dx_ref,
    wq_ref,
    dq_s,
    dk_s,
    dv_s,
    qk_ref,
    vv_ref,
    qk_in,
    vv_in,
    wqk_ref,
    wvv_ref,
    pa_ref,
    pac_ref,
    par_ref,
    pas_ref,
    paz_ref,
    pb_ref,
    pbc_ref,
    pbr_ref,
    pbs_ref,
    pbz_ref,
    far_ref,
    dws_ref,
    dwc_ref,
    dwz_ref,
    dwp_ref,
    local_sem,
    send_sem,
    recv_sem,
    row_sem,
):
    wire = Wire(local_sem, send_sem, recv_sem)
    me, rep, near, core, layers, far = places(parts, copies)
    blocks, _, width = near_ref.shape
    total = blocks * BLOCK
    rows = total // parts
    trees = total // TREE_TOK
    per = rows // BLOCK
    depth = width // parts
    side = lax.rem(rep, 2)
    layer = lax.rem(lax.div(rep, 2), LAYERS)
    other = 1 - side
    split = 2 * LAYERS // parts

    def load(source, target, head):
        return wire.keep(source.at[head], target[head])

    def load_tree(source, target, head):
        some = pl.ds(head * trees, trees)
        return wire.keep(source.at[some], target.at[some])

    def load_head(head):
        return [
            load(q_hbm, q_ref, head),
            load(k_hbm, k_ref, head),
            load(v_hbm, v_ref, head),
            load(kt_hbm, kt_ref, head),
            load_tree(ot_hbm, ot_ref, head),
            load_tree(lse_hbm, lse_ref, head),
        ]

    def arrived(copies_in):
        for copy in copies_in:
            copy.wait_recv()

    loads = [[wire.keep(do_hbm, do_ref)] + load_head(0)]
    greet([p for _, p in near] + [core] + [p for _, p in layers] + far)

    halves_out = [
        wire.send(pa_hbm.at[other], pac_ref, *core),
        wire.send(pb_hbm.at[other], pbc_ref, *core),
    ]
    halves_own = [wire.keep(pa_hbm.at[side], pa_ref), wire.keep(pb_hbm.at[side], pb_ref)]
    for h in range(1, heads):
        loads.append(load_head(h))
    near_load = wire.keep(near_hbm, near_ref)
    weight_load = [
        wire.keep(w, wq_ref.at[:, pl.ds(i * width, width)])
        for i, w in enumerate((wq_hbm, wk_hbm, wv_hbm))
    ]
    base_load = wire.keep(dh1_hbm, dx_ref)

    def beyond(value, slot):
        for i, p in enumerate(far):
            send, recv = far_ref.at[slot, i, 0], far_ref.at[slot, i, 1]
            n, m = value.shape
            send[0:n, 0:m] = value.astype(HALF)
            copy = wire.send(send, recv, *p)
            copy.wait_recv()
            value = value.astype(HALF).astype(SINGLE) + recv[0:n, 0:m].astype(SINGLE)
        return value.astype(HALF)

    low = pb_ref.shape[2]

    def pack_split():
        arrived(halves_out)
        for copy in halves_own:
            copy.wait()
        for r in range(parts):
            for z in range(LAYERS):
                pa_ref[r, z] = total_of(pa_ref[r, z], pac_ref[r, z]).astype(HALF)
        out_a = [wire.send(pa_ref.at[r], par_ref.at[r - 1], *p) for r, p in near]
        for z in range(LAYERS):
            for r in range(parts):
                pb_ref[z, r] = total_of(pb_ref[z, r], pbc_ref[z, r]).astype(HALF)
        out_b = [wire.send(pb_ref.at[flip(layer, j)], pbr_ref.at[j - 1], *p) for j, p in layers]
        return out_a, out_b

    def pack_a_scatter(waits):
        arrived(waits)
        for z in range(LAYERS):
            pas_ref[z] = total_of(
                pa_ref[0, z], *[par_ref[r, z] for r in range(parts - 1)]
            ).astype(HALF)
        return [wire.send(pas_ref.at[flip(layer, j)], paz_ref.at[j - 1], *p) for j, p in layers]

    def pack_a_spread(waits):
        arrived(waits)
        piece = total_of(pas_ref[layer], *[paz_ref[j] for j in range(LAYERS - 1)])
        fa_ref[side, layer] = beyond(piece, 0)
        here = fa_ref.at[side, layer]
        return [wire.send(here, here, *p) for _, p in layers]

    def pack_b_scatter(waits):
        arrived(waits)
        for r in range(parts):
            piece = total_of(pb_ref[layer, r], *[pbr_ref[j, r] for j in range(LAYERS - 1)])
            pbs_ref[r] = beyond(piece, 3 + r)
        return [wire.send(pbs_ref.at[r], pbz_ref.at[r - 1], *p) for r, p in near]

    def pack_b_spread(waits):
        arrived(waits)
        piece = total_of(pbs_ref[0], *[pbz_ref[r] for r in range(parts - 1)])
        fb_ref[side, layer] = piece.astype(HALF)
        here = fb_ref.at[side, layer]
        return [wire.send(here, here, *p) for _, p in layers]

    def pack_cores(waits):
        arrived(waits)
        return [
            wire.send(fa_ref.at[side], fa_ref.at[side], *core),
            wire.send(fb_ref.at[side], fb_ref.at[side], *core),
        ]

    def weights_cores(head):
        return [wire.send(dws_ref.at[head, other], dwc_ref.at[head], *core)]

    def weights_scatter(head, waits):
        arrived(waits)
        for z in range(LAYERS):
            dws_ref[head, side, z] = total_of(dws_ref[head, side, z], dwc_ref[head, z]).astype(HALF)
        return [
            wire.send(dws_ref.at[head, side, flip(layer, j)], dwz_ref.at[head, j - 1], *p)
            for j, p in layers
        ]

    to_row = layer if split == 2 else side * LAYERS + layer

    def weights_send(head, waits):
        arrived(waits)
        piece = total_of(
            dws_ref[head, side, layer], *[dwz_ref[head, j] for j in range(LAYERS - 1)]
        )
        dwp_ref[head] = beyond(piece, 1 + head)

        @pl.when(to_row == 0)
        def _():
            dwf_ref[head, side, layer] = dwp_ref[head]

        copy = pltpu.make_async_remote_copy(
            dwp_ref.at[head],
            dwf_ref.at[head, side, layer],
            row_sem.at[0, head],
            row_sem.at[1, head],
            device_id={"fsdp": flip_two(me, to_row, parts)},
            device_id_type=MESH,
        )

        @pl.when(to_row != 0)
        def _():
            copy.start()

        return copy

    def weights_spread(head, copy):
        @pl.when(to_row != 0)
        def _():
            copy.wait()

        here = dwf_ref.at[head, side, layer]
        return [wire.send(here, here, *p) for _, p in layers]

    def weights_last(head, waits):
        arrived(waits)
        return [wire.send(dwf_ref.at[head, side], dwf_ref.at[head, side], *core)]

    def unsort(head):
        for r in range(parts):

            def one(j, _):
                place = order_ref[blocks + r * per + j]
                both = jnp.concatenate([dq_s[place], dk_s[place] * 0.125], axis=1)
                qk_ref[head, r, block_at(j), :] = both.astype(HALF)
                lower = pl.ds(pl.multiple_of(j * (BLOCK // 2), BLOCK // 2), BLOCK // 2)
                vv_ref[head, r, lower, :] = fold(dv_s[place]).astype(HALF)
                return 0

            lax.fori_loop(0, per, one, 0)
        if head == heads - 1:
            kept.append(wire.keep(qk_ref.at[head, 0], qk_hbm.at[0]))
            kept.append(wire.keep(vv_ref.at[head, 0], vv_hbm.at[0]))
            return [wire.send(qk_ref.at[head, r], qk_hbm.at[r], *p) for r, p in near]
        qk_in[head, 0] = qk_ref[head, 0]
        vv_in[head, 0] = vv_ref[head, 0]
        return [wire.send(qk_ref.at[head, r], qk_in.at[head, r], *p) for r, p in near]

    def send_values(head):
        if head == heads - 1:
            return [wire.send(vv_ref.at[head, r], vv_hbm.at[r], *p) for r, p in near]
        return [wire.send(vv_ref.at[head, r], vv_in.at[head, r], *p) for r, p in near]

    def weight_grads(head):
        total_dw = 0.0
        for r in range(parts):
            grads = jnp.concatenate([qk_ref[head, r], unfold(vv_ref[head, r])], axis=1)
            total_dw = total_dw + dot(
                grads.T, near_ref[r * per : (r + 1) * per].reshape(rows, width)
            )
        dw = total_dw.astype(HALF)
        for c in range(parts):
            to = flip(me, c)
            piece = dw[:, c * depth : (c + 1) * depth]
            if split == 2:
                dws_ref[head, 0, to] = piece[: piece.shape[0] // 2]
                dws_ref[head, 1, to] = piece[piece.shape[0] // 2 :]
            else:
                dws_ref[head, lax.div(to, LAYERS), lax.rem(to, LAYERS)] = piece

    def turn_weights():
        for h in range(heads):
            for c in range(parts):
                at = (c * heads + h) * HEAD
                wqk_ref[h, :, c * 2 * HEAD : (c + 1) * 2 * HEAD] = jnp.concatenate(
                    [wq_ref[:, at : at + HEAD], wq_ref[:, width + at : width + at + HEAD]], axis=1
                )
                wvv_ref[h, :, c * HEAD : (c + 1) * HEAD] = wq_ref[
                    :, 2 * width + at : 2 * width + at + HEAD
                ]

    def input_grad(head):
        def pick(ref, c, at):
            return ref[head, flip(me, c), at, :]

        def step(i, _):
            at = pl.ds(pl.multiple_of(i * tile, tile), tile)
            lower = pl.ds(pl.multiple_of(i * (tile // 2), tile // 2), tile // 2)
            qk = jnp.concatenate([pick(qk_in, c, at) for c in range(parts)], axis=1)
            vv = jnp.concatenate([unfold(pick(vv_in, c, lower)) for c in range(parts)], axis=1)
            dx_ref[at, :] += dot(qk, wqk_ref[head], NT) + dot(vv, wvv_ref[head], NT)
            return 0

        lax.fori_loop(0, rows // tile, step, 0)

    kept = []
    sent, values, chains = [], [], {}
    for h in range(heads):
        for copy in loads[h]:
            copy.wait()
        dk_s[...] = jnp.zeros_like(dk_s)
        dv_s[...] = jnp.zeros_like(dv_s)
        held = None

        def close_held():
            tile, key, chosen, s, dp, last = held
            tile.close(key, chosen, s, dp, last, kt_ref, dq_s, dk_s, dv_s)

        for number, (begin, keys) in enumerate(tile_list()):
            for tree in range(trees):
                work = BackTile(h, tree, trees, begin, order_ref, ot_ref, lse_ref, do_ref, q_ref)
                for key in keys:
                    opened = work.open(key, k_ref, v_ref)
                    if held:
                        close_held()
                    held = (*opened, key is keys[-1])
            event = (h, number)
            if event == (0, 3):
                pack_a, pack_b = pack_split()
            elif event == (1, 1):
                chains[0] = weights_scatter(0, chains[0])
            elif event == (1, 4):
                pack_a = pack_a_scatter(pack_a)
            elif event == (1, 5):
                chains[0] = weights_send(0, chains[0])
            elif event == (1, 7):
                pack_b = pack_b_scatter(pack_b)
        close_held()
        sent.append(unsort(h))
        if h == 0:
            near_load.wait()
        if h < heads - 1:
            values.append(send_values(h))
            weight_grads(h)
            chains[h] = weights_cores(h)
    end_head = heads - 1
    if heads == 1:
        pack_a = pack_a_scatter(pack_a)
        pack_b = pack_b_scatter(pack_b)
    weight_grads(end_head)
    chains[end_head] = weights_cores(end_head)
    pack_a = pack_a_spread(pack_a)
    for copy in weight_load + [base_load]:
        copy.wait()
    turn_weights()
    kept.append(wire.keep(wqk_ref.at[end_head], wqk_hbm))
    kept.append(wire.keep(wvv_ref.at[end_head], wvv_hbm))
    chains[end_head] = weights_scatter(end_head, chains[end_head])
    if heads > 1:
        arrived(sent[0] + values[0])
        input_grad(0)
    kept.append(wire.keep(dx_ref, dx_hbm))
    chains[end_head] = weights_send(end_head, chains[end_head])
    values.append(send_values(end_head))
    pack_b = pack_b_spread(pack_b)
    if heads > 1:
        chains[0] = weights_spread(0, chains[0])
    last = pack_cores(pack_a + pack_b)
    chains[end_head] = weights_spread(end_head, chains[end_head])
    for h in range(heads):
        last += weights_last(h, chains[h])
    arrived(last + sent[end_head] + values[end_head])
    for copy in kept:
        copy.wait()
    wire.finish()


def finish(parts, copies, heads, order, saved, do, dh1, wq, wk, wv, pa, pb):
    near, q, k, v, kt, ot, lse = saved
    blocks, _, width = near.shape
    total = blocks * BLOCK
    rows = total // parts
    depth = width // parts
    tile = PAIR if rows % PAIR == 0 else BLOCK
    split = 2 * LAYERS // parts
    beyonds = max(copies // (2 * LAYERS), 2).bit_length() - 1
    flat = ((blocks, BLOCK, HEAD), SINGLE)
    qk = ((heads, parts, rows, 2 * HEAD), HALF)
    vv = ((heads, parts, rows // 2, 2 * HEAD), HALF)
    a, b = pa.shape[1:], pb.shape[1:]
    dws = (LAYERS, 3 * HEAD // split, depth)
    each = lambda r: [pltpu.VMEM(r.shape[1:], r.dtype)] * heads
    scratch = [(r.shape, r.dtype) for r in (ot, lse, do)]
    scratch += [((rows, width), SINGLE), ((width, 3 * width), HALF), flat, flat, flat]
    scratch += [qk, vv, qk, vv]
    scratch += [((heads, width, 2 * HEAD * parts), HALF), ((heads, width, HEAD * parts), HALF)]
    scratch += [(n, HALF) for n in (a, a, (parts - 1,) + a[1:], a[1:])]
    scratch += [((LAYERS - 1,) + a[2:], HALF)]
    scratch += [(n, HALF) for n in (b, b, (LAYERS - 1,) + b[1:], b[1:])]
    scratch += [((parts - 1,) + b[2:], HALF)]
    scratch += [((3 + parts, beyonds, 2, max(3 * HEAD, depth), width), HALF)]
    if copies == 2 * LAYERS:
        scratch[-1] = ((1, 1, 2, 16, width), HALF)
    scratch += [((heads, 2) + dws, HALF), ((heads,) + dws, HALF)]
    scratch += [((heads, LAYERS - 1) + dws[1:], HALF), ((heads,) + dws[1:], HALF)]
    outs = [((rows, width), SINGLE), (qk[0][1:], HALF), (vv[0][1:], HALF)]
    outs += [((width, 2 * HEAD * parts), HALF), ((width, HEAD * parts), HALF)]
    small = [((2, LAYERS) + a[2:], HALF), ((2, LAYERS) + b[2:], HALF), ((heads, 2) + dws, HALF)]
    return pl.pallas_call(
        functools.partial(finish_kernel, parts, copies, heads, tile),
        out_shape=[shape(*o) for o in outs + small],
        in_specs=[smem()] + anywhere(14),
        out_specs=anywhere(len(outs)) + vmem(len(small)),
        scratch_shapes=[pltpu.VMEM(near.shape, HALF)]
        + [each(r) for r in (q, k, v, kt)]
        + [pltpu.VMEM(*s) for s in scratch]
        + copies_of(16 + 6 * heads, 48 + 12 * parts)
        + [pltpu.SemaphoreType.DMA((2, heads))],
        compiler_params=params(2),
        name="finish",
    )(order, near, q, k, v, kt, ot, lse, do, dh1, wq, wk, wv, pa, pb)


def close_kernel(
    parts,
    heads,
    base_ref,
    qk_ref,
    vv_ref,
    out_in,
    wqk_ref,
    wvv_ref,
    fa_ref,
    fb_ref,
    dwf_ref,
    norm_in,
    out_ref,
    dx_ref,
    gq_ref,
    gk_ref,
    gv_ref,
    go_ref,
    gh_ref,
    gp_ref,
    *norm_refs,
):
    me = lax.axis_index("fsdp")
    width = base_ref.shape[1]
    depth = width // parts
    split = 2 * LAYERS // parts
    qk = jnp.concatenate([qk_ref[flip(me, c)] for c in range(parts)], axis=1)
    vv = jnp.concatenate([unfold(vv_ref[flip(me, c)]) for c in range(parts)], axis=1)
    dx_ref[...] = base_ref[...] + dot(qk, wqk_ref[...], NT) + dot(vv, wvv_ref[...], NT)
    out_ref[...] = out_in[...]

    step = pl.program_id(0)
    last = pl.num_programs(0) - 1
    low = fb_ref.shape[2]
    small = depth // SLICES
    cols = gp_ref.shape[0]
    unit = width // LAYERS

    def forward_grads(z):
        here = slice(z * width, (z + 1) * width)
        gh_ref[0:low, here] = fa_ref[0, z, 0:low].astype(SINGLE)
        gh_ref[low:depth, here] = fb_ref[0, z].astype(SINGLE)
        piece = jnp.concatenate([fa_ref[1, z, 0:low], fb_ref[1, z]], axis=0).astype(SINGLE)
        if cols < width:
            piece = jnp.concatenate([piece[:, :cols], piece[:, cols:]], axis=0)
        gp_ref[:, z * unit : (z + 1) * unit] = piece.T
        for i in range(2):
            at = (i * LAYERS + z) * small
            go_ref[at : at + small, :] = fa_ref[i, z, low : low + small].astype(SINGLE)

    def attention_grads():
        for i, ref in enumerate(norm_refs):
            ref[...] = norm_in[i : i + 1, :]
        for c in range(parts):
            for h in range(heads):
                r = flip(me, c)
                if split == 2:
                    piece = jnp.concatenate([dwf_ref[h, 0, r], dwf_ref[h, 1, r]], axis=0)
                else:
                    piece = dwf_ref[h, lax.div(r, LAYERS), lax.rem(r, LAYERS)]
                turned = piece.astype(SINGLE).T
                at = (c * heads + h) * HEAD
                for ref, k in ((gq_ref, 0), (gk_ref, 1), (gv_ref, 2)):
                    ref[:, at : at + HEAD] = turned[:, k * HEAD : (k + 1) * HEAD]

    for z in range(LAYERS):
        pl.when(step == jnp.minimum(z, last))(functools.partial(forward_grads, z))
    pl.when(step == last)(attention_grads)


def close(parts, heads, output, base, qk, vv, wqk, wvv, fa, fb, dwf, norms, inner):
    rows, width = base.shape
    tile = PAIR if rows % PAIR == 0 else BLOCK
    depth = width // parts
    row = pl.BlockSpec((tile, width), lambda i: (i, 0))
    once = lambda a: pl.BlockSpec(a, lambda i: (0,) * len(a), pipeline_mode=pl.Buffered(1))
    last = lambda a: pl.BlockSpec(a, lambda i: (0,) * len(a))
    grads = [(depth, width)] * 4 + [(depth, inner), (inner // parts, width)] + [(1, width)] * 4
    return pl.pallas_call(
        functools.partial(close_kernel, parts, heads),
        grid=(rows // tile,),
        in_specs=[
            row,
            pl.BlockSpec((parts, tile, 2 * HEAD), lambda i: (0, i, 0)),
            pl.BlockSpec((parts, tile // 2, 2 * HEAD), lambda i: (0, i, 0)),
            row,
        ]
        + [once(a.shape) for a in (wqk, wvv, fa, fb, dwf, norms)],
        out_specs=[row, row] + [last(g) for g in grads],
        out_shape=[shape((rows, width), HALF), shape((rows, width), SINGLE)]
        + [shape(g, SINGLE) for g in grads],
        compiler_params=pltpu.CompilerParams(vmem_limit_bytes=VMEM_LIMIT),
        name="close",
    )(base, qk, vv, output, wqk, wvv, fa, fb, dwf, norms)


def shards(
    parts,
    copies,
    inputs,
    cotangent,
    segments,
    trees,
    parents,
    w_query,
    w_key,
    w_value,
    w_out,
    w_hidden,
    w_proj,
    norm1_gain,
    norm1_bias,
    norm2_gain,
    norm2_bias,
):
    x = inputs[0]
    rows, width = x.shape
    inner = w_hidden.shape[1]
    heads = HEADS // parts
    wide = heads * HEAD
    depth = width // parts
    me = lax.axis_index("fsdp")
    order = block_order(segments[0], trees[0], parents[0], rows, me)
    by = [w_query, w_key, w_value]
    if wide % BLOCK:
        by = jnp.concatenate([w.reshape(depth, parts, wide) for w in by], axis=2)
        by = [by.transpose(1, 0, 2)]
    cut = lambda w: w.reshape(SLICES, w.shape[0] // SLICES, w.shape[1])
    whole = lambda w: w.reshape(-1, w.shape[-1])
    slices = [cut(w) for w in (w_out, w_hidden, w_proj)]
    near, q, k, v, kt, ot, lse, ctx, *gathered = start(parts, copies, heads, order, x, by, slices)
    vecs = [n.reshape(1, width) for n in (norm1_gain, norm1_bias, norm2_gain, norm2_bias)]
    output, dh1, do, pa, pb, wq, wk, wv, norms = middle(
        parts,
        copies,
        heads,
        x,
        cotangent[0],
        ctx,
        *[whole(w) for w in gathered],
        [cut(w) for w in (w_query, w_key, w_value)],
        vecs,
    )
    saved = (near, q, k, v, kt, ot, lse)
    do = do.reshape(-1, BLOCK, wide)
    weights = [whole(w) for w in (wq, wk, wv)]
    left = finish(parts, copies, heads, order, saved, do, dh1, *weights, pa, pb)
    output, input_grad, *grads = close(parts, heads, output, *left, norms, inner)
    return (output[None], input_grad[None], *grads[:6], *[n.reshape(width) for n in grads[6:]])


def solution(mesh):
    token = P("rep", "fsdp", None)
    weight = P("fsdp", None)
    placed = (token, token, P("rep", None), P("rep", None), P("rep", None, None))
    return jax.shard_map(
        functools.partial(shards, mesh.shape["fsdp"], mesh.shape["rep"]),
        mesh=mesh,
        in_specs=placed + (weight,) * 6 + (P(),) * 4,
        out_specs=(token, token) + (weight,) * 6 + (P(),) * 4,
        check_vma=False,
    )
```

```python
import functools

import jax
import jax.numpy as jnp
from jax import lax
from jax.experimental import pallas as pl
from jax.experimental.pallas import tpu as pltpu
from jax.sharding import PartitionSpec as P

HEADS = 8
HEAD = 64
BLOCK = 128
PAIR = 2 * BLOCK
TRUNK = 8
BRANCHES = 4
LEAVES = 8
TREE_BLOCKS = TRUNK + BRANCHES + LEAVES
TREE_TOK = TREE_BLOCKS * BLOCK
SINGLE = jnp.float32
HALF = jnp.bfloat16
NN = (((1,), (0,)), ((), ()))
NT = (((1,), (1,)), ((), ()))
LOG2E = 1.4426950408889634
SCALE = 0.125 * LOG2E
VMEM_LIMIT = 58 << 20
MESH = pl.DeviceIdType.MESH
SLICES = 8
LAYERS = 4


def dot(left, right, dims=NN):
    return lax.dot_general(left, right, dims, preferred_element_type=SINGLE)


def row_mean(values):
    return jnp.mean(values, axis=-1, keepdims=True)


def block_order(segments, trees, parents, rows, me):
    seg = segments.reshape(-1, BLOCK)[:, 0]
    tree = trees.reshape(-1, BLOCK)[:, 0]
    count = seg.shape[0]
    table = parents.reshape(-1)
    slot = tree * parents.shape[1] + seg
    parent = jnp.sum(
        jnp.where(slot[:, None] == jnp.arange(table.shape[0])[None, :], table[None, :], 0), axis=1
    )
    place = jnp.arange(count, dtype=jnp.int32)
    kind = jnp.where(seg == 0, 0, jnp.where(seg <= BRANCHES, seg, 16 * parent + seg))
    key = (tree * 256 + kind) * 64 + place
    rank = jnp.sum((key[None, :] < key[:, None]).astype(jnp.int32), axis=1)
    per = rows // BLOCK
    near = ((place // per) ^ me) * per + place % per
    order = jnp.sum(jnp.where(rank[None, :] == place[:, None], near[None, :], 0), axis=1)
    back = jnp.sum(jnp.where(near[None, :] == place[:, None], rank[None, :], 0), axis=1)
    return jnp.concatenate([order, back]).astype(jnp.int32)


def tile_list():
    out = []
    trunk = TRUNK * BLOCK
    for start in range(0, trunk, PAIR):
        keys = [(0, start, None)] if start else []
        out.append((start, keys + [(start, PAIR, "causal")]))
    for pair in range(BRANCHES // 2):
        start = trunk + pair * PAIR
        out.append((start, [(0, trunk, None), (start, PAIR, "own")]))
    for branch in range(BRANCHES):
        start = trunk + BRANCHES * BLOCK + branch * PAIR
        out.append(
            (
                start,
                [(0, trunk, None), (trunk + branch * BLOCK, BLOCK, None), (start, PAIR, "own")],
            )
        )
    return out


def mask_of(kind):
    key = lax.broadcasted_iota(jnp.int32, (PAIR, PAIR), 0)
    query = lax.broadcasted_iota(jnp.int32, (PAIR, PAIR), 1)
    mask = key <= query
    if kind == "own":
        mask = mask & ((key >= BLOCK) == (query >= BLOCK))
    return mask


def flip(value, bits):
    bit = 1
    while bit <= bits:
        if bits & bit:
            value = value + bit - 2 * bit * lax.rem(lax.div(value, bit), 2)
        bit *= 2
    return value


def flip_two(one, two, size):
    out = 0
    bit = 1
    while bit < size:
        out = out + bit * lax.rem(lax.rem(lax.div(one, bit), 2) + lax.rem(lax.div(two, bit), 2), 2)
        bit *= 2
    return out


class Wire:
    def __init__(self, local_sem, send_sem, recv_sem):
        self.local_sem, self.send_sem, self.recv_sem = local_sem, send_sem, recv_sem
        self.locals = self.remotes = 0
        self.open = []

    def keep(self, source, target):
        copy = pltpu.make_async_copy(source, target, self.local_sem.at[self.locals])
        self.locals += 1
        copy.start()
        return copy

    def plan(self, source, target, axis, peer):
        copy = pltpu.make_async_remote_copy(
            source,
            target,
            self.send_sem.at[self.remotes],
            self.recv_sem.at[self.remotes],
            device_id={axis: peer},
            device_id_type=MESH,
        )
        self.remotes += 1
        self.open.append(copy)
        return copy

    def send(self, *route):
        copy = self.plan(*route)
        copy.start()
        return copy

    def finish(self):
        for copy in self.open:
            copy.wait_send()


def greet(peers):
    barrier = pltpu.get_barrier_semaphore()
    for axis, peer in peers:
        pl.semaphore_signal(barrier, inc=1, device_id={axis: peer}, device_id_type=MESH)
    pl.semaphore_wait(barrier, len(peers))


def places(parts, copies):
    me = lax.axis_index("fsdp")
    rep = lax.axis_index("rep")
    near = [(r, ("fsdp", flip(me, r))) for r in range(1, parts)]
    core = ("rep", flip(rep, 1))
    layers = [(j, ("rep", flip(rep, 2 * j))) for j in range(1, LAYERS)]
    far = []
    bit = 2 * LAYERS
    while bit < copies:
        far.append(("rep", flip(rep, bit)))
        bit *= 2
    return me, rep, near, core, layers, far


class Gather:
    def __init__(self, wire, spots, shards_in, full):
        self.wire, self.spots, self.shards_in, self.full = wire, spots, shards_in, full
        me, rep, near, core, layers, far = spots
        self.side = lax.rem(rep, 2)
        mine = self.side * LAYERS + lax.rem(lax.div(rep, 2), LAYERS)
        half = pl.ds(self.side * LAYERS, LAYERS)
        others = [flip(me, r) for r, _ in near]
        pairs = list(zip(shards_in, full))
        self.own = []
        self.stages = [
            [wire.plan(a.at[mine], b.at[me, mine], *p) for _, p in near for a, b in pairs],
            [
                wire.plan(b.at[c, mine], b.at[c, mine], *p)
                for _, p in layers
                for c in others
                for b in full
            ],
            [wire.plan(b.at[c, half], b.at[c, half], *core) for c in others for b in full],
        ]

    def start(self):
        for copy in self.stages[0]:
            copy.start()
        me = self.spots[0]
        self.own = [self.wire.keep(a, b.at[me]) for a, b in zip(self.shards_in, self.full)]

    def step(self, i):
        for copy in self.stages[i - 1]:
            copy.wait_recv()
        for copy in self.stages[i]:
            copy.start()

    def end(self):
        for copy in self.stages[2]:
            copy.wait_recv()
        for copy in self.own:
            copy.wait()


def picks(order_ref, tree, start, size):
    first = tree * TREE_BLOCKS + start // BLOCK
    return [order_ref[first + i] for i in range(size // BLOCK)]


def stack(ref, head, chosen, axis):
    blocks = [ref[head][i] for i in chosen]
    return jnp.concatenate(blocks, axis=axis) if len(blocks) > 1 else blocks[0]


def attend_head(head, trees, order_ref, q_ref, k_ref, vt_ref, ot_ref, lse_ref, flat_ref):
    def scores_of(tree, start, keys):
        q = stack(q_ref, head, picks(order_ref, tree, start, PAIR), 0)
        scores = []
        for off, size, kind in keys:
            s = dot(stack(k_ref, head, picks(order_ref, tree, off, size), 0), q, NT)
            if kind:
                s = jnp.where(mask_of(kind), s, -1e30)
            scores.append(s)
        return scores

    def finish_tile(tree, start, keys, scores):
        here = slice(start, start + PAIR)
        at = head * trees + tree
        top = functools.reduce(jnp.maximum, [jnp.max(s, axis=0, keepdims=True) for s in scores])
        top = top * SCALE
        mass = 0.0
        acc = 0.0
        for (off, size, _), s in zip(keys, scores):
            e = jnp.exp2(s * SCALE - top)
            mass = mass + jnp.sum(e, axis=0, keepdims=True)
            vt = stack(vt_ref, head, picks(order_ref, tree, off, size), 1)
            acc = acc + dot(vt, e.astype(HALF))
        out = acc * (1.0 / mass)
        lse_ref[at, :, here] = top + jnp.log2(mass)
        ot_ref[at, :, here] = out
        place = tree * TREE_BLOCKS + start // BLOCK
        flat_ref[place : place + 2] = out.T.astype(HALF).reshape(2, BLOCK, HEAD)

    held = []
    for start, keys in tile_list():
        for tree in range(trees):
            held.append((tree, start, keys, scores_of(tree, start, keys)))
            if len(held) > 2:
                finish_tile(*held.pop(0))
    for tile in held:
        finish_tile(*tile)


def fold(block):
    return jnp.concatenate([block[: BLOCK // 2], block[BLOCK // 2 :]], axis=1)


def unfold(packed):
    parts = []
    for i in range(packed.shape[0] // (BLOCK // 2)):
        piece = packed[i * (BLOCK // 2) : (i + 1) * (BLOCK // 2)]
        parts += [piece[:, :HEAD], piece[:, HEAD:]]
    return jnp.concatenate(parts, axis=0)


def block_at(index):
    return pl.ds(pl.multiple_of(index * BLOCK, BLOCK), BLOCK)


def start_kernel(
    parts,
    copies,
    heads,
    order_ref,
    x_hbm,
    by_hbm,
    so_hbm,
    sh_hbm,
    sp_hbm,
    near_hbm,
    q_hbm,
    k_hbm,
    v_hbm,
    kt_hbm,
    ot_hbm,
    lse_hbm,
    ctx_hbm,
    wo_hbm,
    wh_hbm,
    wp_hbm,
    near_ref,
    own_ref,
    q_ref,
    k_ref,
    v_ref,
    kt_ref,
    vt_ref,
    ot_ref,
    lse_ref,
    flat_ref,
    ctx_ref,
    local_sem,
    send_sem,
    recv_sem,
):
    wire = Wire(local_sem, send_sem, recv_sem)
    spots = places(parts, copies)
    me, rep, near, core, layers, far = spots
    per = x_hbm.shape[0]
    blocks = parts * per
    trees = blocks // TREE_BLOCKS
    wide = heads * HEAD
    greet([p for _, p in near] + [core] + [p for _, p in layers])

    def own_piece(device):
        if len(by_hbm) == 1:
            return [(by_hbm[0].at[device], own_ref.at[me])]
        at = pl.ds(pl.multiple_of(device * wide, wide), wide)
        return [
            (w.at[:, at], own_ref.at[me, :, pl.ds(i * wide, wide)]) for i, w in enumerate(by_hbm)
        ]

    kept = [wire.keep(*pair) for pair in own_piece(me)]
    kept.append(wire.keep(x_hbm, near_ref.at[pl.ds(0, per)]))
    own_copies = [wire.send(*pair, *p) for _, p in near for pair in own_piece(p[1])]
    gather = Gather(wire, spots, (so_hbm, sh_hbm, sp_hbm), (wo_hbm, wh_hbm, wp_hbm))
    gather.start()

    def project(first, count):
        weight = own_ref[...].reshape(parts * own_ref.shape[1], 3 * wide)
        x = near_ref[first : first + count].reshape(count * BLOCK, near_ref.shape[2])
        out = dot(x, weight).astype(HALF)
        for i in range(count):
            block = out[i * BLOCK : (i + 1) * BLOCK]
            kt = block[:, wide : 2 * wide].T
            vt = block[:, 2 * wide :].T
            for h in range(heads):
                cols = slice(h * HEAD, (h + 1) * HEAD)
                q_ref[h, first + i] = block[:, cols]
                k_ref[h, first + i] = block[:, wide:][:, cols]
                v_ref[h, first + i] = block[:, 2 * wide :][:, cols]
                kt_ref[h, first + i] = kt[cols]
                vt_ref[h, first + i] = vt[cols]

    def wait_all(copies_in):
        for copy in copies_in:
            copy.wait_recv()

    if parts == 4:
        cuts = [i * per // 4 for i in range(5)]

        def part(chunk, i):
            return pl.ds(chunk * per + cuts[i], cuts[i + 1] - cuts[i])

        (_, px), (_, py), _ = near
        one, two = {}, {}
        for a, b in zip((0, 1, 2, 3), (2, 3, 0, 1)):
            one[a] = wire.send(x_hbm.at[part(0, a)], near_ref.at[part(1, a)], *px)
            two[b] = wire.send(x_hbm.at[part(0, b)], near_ref.at[part(2, b)], *py)
        three = {}
        for a, b in ((0, 2), (1, 3)):
            one[a].wait_recv()
            three[a] = wire.send(near_ref.at[part(1, a)], near_ref.at[part(3, a)], *py)
            two[b].wait_recv()
            three[b] = wire.send(near_ref.at[part(2, b)], near_ref.at[part(3, b)], *px)
            if a == 0:
                gather.step(1)
                for copy in kept:
                    copy.wait()
                wait_all(own_copies)
                project(0, per)
        wait_all([one[2], one[3]])
        project(per, per)
        wait_all([two[0], two[1]])
        project(2 * per, per)
        wait_all([three[0], three[2]])
        project(3 * per, cuts[1])
        project(3 * per + cuts[2], cuts[3] - cuts[2])
        wait_all([three[1], three[3]])
        project(3 * per + cuts[1], cuts[2] - cuts[1])
        project(3 * per + cuts[3], cuts[4] - cuts[3])
    else:
        waits = [wire.send(x_hbm, near_ref.at[pl.ds(r * per, per)], *p) for r, p in near]
        gather.step(1)
        for copy in kept:
            copy.wait()
        wait_all(own_copies + waits)
        for r in range(parts):
            project(r * per, per)
    saves = [wire.keep(near_ref, near_hbm)]
    saves += [
        wire.keep(a, b)
        for a, b in ((q_ref, q_hbm), (k_ref, k_hbm), (v_ref, v_hbm), (kt_ref, kt_hbm))
    ]
    context = []
    for h in range(heads):
        if h == heads - 1:
            gather.step(2)
        views = [[ref.at[i] for i in range(heads)] for ref in (q_ref, k_ref, vt_ref)]
        attend_head(h, trees, order_ref, *views, ot_ref, lse_ref, flat_ref)
        for r in range(parts):

            def unsort(j, _):
                block = flat_ref[order_ref[blocks + r * per + j]]
                at = pl.ds(pl.multiple_of(j * (BLOCK // 2), BLOCK // 2), BLOCK // 2)
                ctx_ref[h, r, at, :] = fold(block)
                return 0

            lax.fori_loop(0, per, unsort, 0)
            if r:
                context.append(wire.send(ctx_ref.at[h, r], ctx_hbm.at[h, r], *near[r - 1][1]))
            else:
                saves.append(wire.keep(ctx_ref.at[h, 0], ctx_hbm.at[h, 0]))
        some = pl.ds(h * trees, trees)
        saves.append(wire.keep(ot_ref.at[some], ot_hbm.at[some]))
        saves.append(wire.keep(lse_ref.at[some], lse_hbm.at[some]))
    wait_all(context)
    gather.end()
    for copy in saves:
        copy.wait()
    wire.finish()


def anywhere(count):
    return [pl.BlockSpec(memory_space=pl.ANY)] * count


def vmem(count):
    return [pl.BlockSpec(memory_space=pltpu.VMEM)] * count


def smem():
    return pl.BlockSpec(memory_space=pltpu.SMEM)


def shape(dims, dtype):
    return jax.ShapeDtypeStruct(dims, dtype)


def copies_of(count_local, count_remote):
    return [
        pltpu.SemaphoreType.DMA((count_local,)),
        pltpu.SemaphoreType.DMA((count_remote,)),
        pltpu.SemaphoreType.DMA((count_remote,)),
    ]


def params(number):
    return pltpu.CompilerParams(
        vmem_limit_bytes=VMEM_LIMIT, collective_id=number, has_side_effects=True
    )


def start(parts, copies, heads, order, x, by, slices):
    rows, width = x.shape
    total = parts * rows
    trees = total // TREE_TOK
    n = trees * heads
    tok = ((heads, total // BLOCK, BLOCK, HEAD), HALF)
    turned = ((heads, total // BLOCK, HEAD, BLOCK), HALF)
    near = ((total // BLOCK, BLOCK, width), HALF)
    ot = ((n, HEAD, TREE_TOK), SINGLE)
    lse = ((n, 1, TREE_TOK), SINGLE)
    ctx = ((heads, parts, rows // 2, 2 * HEAD), HALF)
    outs = [near, tok, tok, tok, turned, ot, lse, ctx]
    outs += [((parts,) + w.shape, HALF) for w in slices]
    scratch = [near, ((parts, width // parts, 3 * heads * HEAD), HALF), tok, tok, tok, turned, turned, ot, lse]
    scratch += [((total // BLOCK, BLOCK, HEAD), HALF), ctx]
    return pl.pallas_call(
        functools.partial(start_kernel, parts, copies, heads),
        out_shape=[shape(*o) for o in outs],
        in_specs=[smem(), *anywhere(1), anywhere(len(by)), *anywhere(3)],
        out_specs=anywhere(len(outs)),
        scratch_shapes=[pltpu.VMEM(*s) for s in scratch]
        + copies_of(12 + 3 * heads, 32 + (parts - 1) * 24),
        compiler_params=params(0),
        name="start",
    )(order, x.reshape(rows // BLOCK, BLOCK, width), by, *slices)


def middle_kernel(
    parts,
    copies,
    heads,
    tile,
    x_hbm,
    dy_hbm,
    ctx_hbm,
    wo_hbm,
    wh_hbm,
    wp_hbm,
    sq_hbm,
    sk_hbm,
    sv_hbm,
    vec_refs,
    out_hbm,
    dh1_hbm,
    do_hbm,
    pa_hbm,
    pb_hbm,
    wq_hbm,
    wk_hbm,
    wv_hbm,
    norm_out,
    norm_ref,
    norm_s,
    norm_r,
    x_ref,
    dy_ref,
    ctx_ref,
    wo_ref,
    wh_ref,
    wp_ref,
    out_ref,
    dh1_ref,
    do_ref,
    pa_ref,
    pb_ref,
    cat_ref,
    u_ref,
    df_ref,
    da_ref,
    g_ref,
    dz_ref,
    d_s,
    local_sem,
    send_sem,
    recv_sem,
    tile_sem,
    out_sem,
):
    wire = Wire(local_sem, send_sem, recv_sem)
    spots = places(parts, copies)
    me, rep, near, core, layers, far = spots
    rows, width = x_ref.shape
    inner = wh_ref.shape[1]
    wide = heads * HEAD
    chunk = 512
    count = rows // tile
    loads = [
        wire.keep(ctx_hbm, ctx_ref),
        wire.keep(wo_hbm, wo_ref),
        wire.keep(x_hbm, x_ref),
        wire.keep(wh_hbm, wh_ref),
        wire.keep(wp_hbm, wp_ref),
        wire.keep(dy_hbm, dy_ref),
    ]
    greet([p for _, p in near] + [core] + [p for _, p in layers] + far)
    gather = Gather(wire, spots, (sq_hbm, sk_hbm, sv_hbm), (wq_hbm, wk_hbm, wv_hbm))
    gather.start()
    gain1, bias1, gain2, bias2 = [ref[...] for ref in vec_refs]
    norm_ref[...] = jnp.zeros_like(norm_ref)
    for copy in loads:
        copy.wait()

    def rows_out(i, at):
        return [
            pltpu.make_async_copy(out_ref.at[at], out_hbm.at[at], out_sem.at[2 * i]),
            pltpu.make_async_copy(dh1_ref.at[at], dh1_hbm.at[at], out_sem.at[2 * i + 1]),
        ]

    def rows_sent(i, at):
        return [
            pltpu.make_async_remote_copy(
                do_ref.at[r, at],
                do_hbm.at[r, at],
                tile_sem.at[0, i * parts + r],
                tile_sem.at[1, i * parts + r],
                device_id={p[0]: p[1]},
                device_id_type=MESH,
            )
            for r, p in near
        ] + [
            pltpu.make_async_copy(do_ref.at[0, at], do_hbm.at[0, at], tile_sem.at[0, i * parts])
        ]

    def tile_rows(i):
        return pl.ds(pl.multiple_of(i * tile, tile), tile)

    def tile_step(i, _):
        at = tile_rows(i)
        packed = pl.ds(pl.multiple_of(i * (tile // 2), tile // 2), tile // 2)
        ctx = jnp.concatenate(
            [
                unfold(ctx_ref[h, flip(me, c), packed, :])
                for c in range(parts)
                for h in range(heads)
            ],
            axis=-1,
        )
        cat_ref[at, :] = ctx
        h1 = x_ref[at, :].astype(SINGLE) + dot(ctx, wo_ref[...])
        c1 = h1 - row_mean(h1)
        r1 = lax.rsqrt(row_mean(c1 * c1) + 1e-5)
        n1 = c1 * r1
        y1 = n1 * gain1 + bias1
        u = y1.astype(HALF)
        u_ref[at, :] = u
        branch = 0.0
        spans = [slice(j, j + chunk) for j in range(0, inner, chunk)]
        later = dot(u, wh_ref[:, spans[0]])
        for n, s in enumerate(spans):
            z = later
            if n + 1 < len(spans):
                later = dot(u, wh_ref[:, spans[n + 1]])
            cdf = 0.5 * (1.0 + lax.erf(z * 0.7071067811865476))
            pdf = jnp.exp2(z * z * (-0.5 * LOG2E)) * 0.3989422804014327
            g = (z * cdf).astype(HALF)
            g_ref[at, s] = g
            d_s[:, s] = cdf + z * pdf
            branch = branch + dot(g, wp_ref[s, :])
        h2 = y1 + branch
        c2 = h2 - row_mean(h2)
        r2 = lax.rsqrt(row_mean(c2 * c2) + 1e-5)
        n2 = c2 * r2
        out_ref[at, :] = (n2 * gain2 + bias2).astype(HALF)
        dy = dy_ref[at, :].astype(SINGLE)
        norm_ref[2:3, :] += jnp.sum(dy * n2, axis=0, keepdims=True)
        norm_ref[3:4, :] += jnp.sum(dy, axis=0, keepdims=True)
        dn2 = dy * gain2
        dh2 = r2 * (dn2 - row_mean(dn2) - n2 * row_mean(dn2 * n2))
        df = dh2.astype(HALF)
        df_ref[at, :] = df
        back = 0.0
        later = dot(df, wp_ref[spans[0], :], NT)
        for n, s in enumerate(spans):
            dg = later
            if n + 1 < len(spans):
                later = dot(df, wp_ref[spans[n + 1], :], NT)
            dz = (dg * d_s[:, s]).astype(HALF)
            dz_ref[at, s] = dz
            back = back + dot(dz, wh_ref[:, s], NT)
        dy1 = dh2 + back
        norm_ref[0:1, :] += jnp.sum(dy1 * n1, axis=0, keepdims=True)
        norm_ref[1:2, :] += jnp.sum(dy1, axis=0, keepdims=True)
        dn1 = dy1 * gain1
        dh1 = r1 * (dn1 - row_mean(dn1) - n1 * row_mean(dn1 * n1))
        dh1_ref[at, :] = dh1
        da = dh1.astype(HALF)
        da_ref[at, :] = da
        dctx = dot(da, wo_ref[...], NT).astype(HALF)
        for c in range(parts):
            do_ref[flip(me, c), at, :] = dctx[:, c * wide : (c + 1) * wide]
        for copy in rows_out(i, at) + rows_sent(i, at):
            copy.start()
        for stage in (1, 2):

            @pl.when(i == 1 + (count - 2) * (stage - 1))
            def _():
                gather.step(stage)

        return 0

    lax.fori_loop(0, count, tile_step, 0)
    depth = width // parts
    cols = inner // parts
    low = depth // 2
    unit = width // LAYERS
    small = depth // SLICES

    def put(side, c, z, piece):
        to = flip(me, c)
        pa_ref[side, to, z, 0:low] = piece[:low]
        pb_ref[side, z, to] = piece[low:]

    layer = lax.rem(lax.div(rep, 2), LAYERS)
    norm_s[0] = norm_ref[...]
    norm_r[0, 0] = norm_ref[...]
    sums = [wire.send(norm_s.at[0], norm_r.at[0, j], *p) for j, p in layers]

    def norm_cores():
        for copy in sums:
            copy.wait_recv()
        total = functools.reduce(jnp.add, [norm_r[0, flip(layer, c)] for c in range(LAYERS)])
        for i, p in enumerate(far):
            norm_s[3 + i] = total
            copy = wire.send(norm_s.at[3 + i], norm_r.at[3 + i, 0], *p)
            copy.wait_recv()
            total = total + norm_r[3 + i, 0]
        norm_s[1] = total
        return [wire.send(norm_s.at[1], norm_r.at[1, 0], *core)]

    def norm_group():
        sums[0].wait_recv()
        norm_s[2] = norm_s[1] + norm_r[1, 0]
        norm_r[2, 0] = norm_s[2]
        return [wire.send(norm_s.at[2], norm_r.at[2, r], *p) for r, p in near]

    df_t = df_ref[...].T
    for c in range(parts):
        grad = dot(df_t, g_ref[:, c * cols : (c + 1) * cols]).astype(HALF)
        for z in range(LAYERS):
            piece = grad[z * unit : (z + 1) * unit]
            if cols < width:
                piece = jnp.concatenate([piece[:depth], piece[depth:]], axis=1)
            put(1, c, z, piece)
    sums = norm_cores()
    saves = [wire.keep(pb_ref.at[1], pb_hbm.at[1])]
    u_t = u_ref[...].T
    for z in range(LAYERS):
        grad = dot(u_t, dz_ref[:, z * width : (z + 1) * width]).astype(HALF)
        for c in range(parts):
            put(0, c, z, grad[c * depth : (c + 1) * depth])
    sums = norm_group()
    saves.append(wire.keep(pb_ref.at[0], pb_hbm.at[0]))
    grad = dot(cat_ref[...].T, da_ref[...]).astype(HALF)
    for c in range(parts):
        for side in range(2):
            for z in range(LAYERS):
                at = c * depth + (side * LAYERS + z) * small
                pa_ref[side, flip(me, c), z, low : low + small] = grad[at : at + small]
    saves.append(wire.keep(pa_ref, pa_hbm))

    def tile_end(i, _):
        at = tile_rows(i)
        for copy in rows_out(i, at):
            copy.wait()
        sent = rows_sent(i, at)
        for copy in sent:
            copy.wait()
        return 0

    lax.fori_loop(0, count, tile_end, 0)
    for copy in sums:
        copy.wait_recv()
    norm_out[...] = functools.reduce(jnp.add, [norm_r[2, flip(me, c)] for c in range(parts)])
    for copy in saves:
        copy.wait()
    gather.end()
    wire.finish()


def middle(parts, copies, heads, x, dy, ctx, wo, wh, wp, slices, vecs):
    rows, width = x.shape
    inner = wp.shape[0]
    tile = PAIR if rows % PAIR == 0 else BLOCK
    depth = width // parts
    wide = heads * HEAD
    tok = ((rows, width), HALF)
    full = ((rows, width), SINGLE)
    do = ((parts, rows, wide), HALF)
    pack = ((2, parts, LAYERS, depth // 2 + depth // SLICES, width), HALF)
    pack_b = ((2, LAYERS, parts, depth // 2, width), HALF)
    big = ((rows, inner), HALF)
    outs = [tok, full, do, pack, pack_b] + [((parts,) + w.shape, HALF) for w in slices]
    stages = copies.bit_length() + 1
    norm = (4, width)
    scratch = [(norm, SINGLE), ((stages,) + norm, SINGLE)]
    scratch += [((stages, max(parts, LAYERS)) + norm, SINGLE)]
    scratch += [tok, tok, (ctx.shape, HALF), ((width, width), HALF), ((width, inner), HALF)]
    scratch += [((inner, width), HALF), tok, full, do, pack, pack_b, tok, tok, tok, tok, big, big]
    scratch += [((tile, inner), SINGLE)]
    count = rows // tile
    return pl.pallas_call(
        functools.partial(middle_kernel, parts, copies, heads, tile),
        out_shape=[shape(*o) for o in outs] + [shape((4, width), SINGLE)],
        in_specs=[*anywhere(9), vmem(4)],
        out_specs=anywhere(len(outs)) + vmem(1),
        scratch_shapes=[pltpu.VMEM(*s) for s in scratch]
        + copies_of(12, 24 * parts)
        + [
            pltpu.SemaphoreType.DMA((2, count * parts)),
            pltpu.SemaphoreType.DMA((2 * count,)),
        ],
        compiler_params=params(1),
        name="middle",
    )(x, dy, ctx, wo, wh, wp, *slices, vecs)


class BackTile:
    def __init__(self, head, tree, trees, start, order_ref, ot_ref, lse_ref, do_ref, q_ref):
        here = slice(start, start + PAIR)
        self.head, self.tree, self.order_ref = head, tree, order_ref
        self.base = tree * TREE_BLOCKS
        self.first = self.base + start // BLOCK
        at = head * trees + tree
        do = jnp.concatenate([do_ref[order_ref[self.first + i]] for i in range(2)], axis=0)
        self.do = do[:, head * HEAD : (head + 1) * HEAD]
        self.delta = jnp.sum(
            self.do.astype(SINGLE).T * ot_ref[at, :, here], axis=0, keepdims=True
        )
        self.q = stack(q_ref, head, picks(order_ref, tree, start, PAIR), 0)
        self.lse = lse_ref[at, :, here]
        self.dq = 0.0

    def open(self, key, k_ref, v_ref):
        chosen = picks(self.order_ref, self.tree, key[0], key[1])
        s = dot(stack(k_ref, self.head, chosen, 0), self.q, NT)
        return self, key, chosen, s, dot(stack(v_ref, self.head, chosen, 0), self.do, NT)

    def close(self, key, chosen, s, dp, last, kt_ref, dq_s, dk_s, dv_s):
        off, size, kind = key
        out = slice(self.base + off // BLOCK, self.base + (off + size) // BLOCK)
        p = jnp.exp2(s * SCALE - self.lse)
        if kind:
            p = jnp.where(mask_of(kind), p, 0.0)
        ds = (p * (dp - self.delta)).astype(HALF)
        dv_s[out] += dot(p.astype(HALF), self.do).reshape(size // BLOCK, BLOCK, HEAD)
        dk_s[out] += dot(ds, self.q).reshape(size // BLOCK, BLOCK, HEAD)
        self.dq = self.dq + dot(stack(kt_ref, self.head, chosen, 1), ds)
        if last:
            dq_s[self.first : self.first + 2] = (self.dq * 0.125).T.reshape(2, BLOCK, HEAD)


def total_of(*refs):
    return functools.reduce(jnp.add, [r.astype(SINGLE) for r in refs])


def finish_kernel(
    parts,
    copies,
    heads,
    tile,
    order_ref,
    near_hbm,
    q_hbm,
    k_hbm,
    v_hbm,
    kt_hbm,
    ot_hbm,
    lse_hbm,
    do_hbm,
    dh1_hbm,
    wq_hbm,
    wk_hbm,
    wv_hbm,
    pa_hbm,
    pb_hbm,
    dx_hbm,
    qk_hbm,
    vv_hbm,
    wqk_hbm,
    wvv_hbm,
    fa_ref,
    fb_ref,
    dwf_ref,
    near_ref,
    q_ref,
    k_ref,
    v_ref,
    kt_ref,
    ot_ref,
    lse_ref,
    do_ref,
    dx_ref,
    wq_ref,
    dq_s,
    dk_s,
    dv_s,
    qk_ref,
    vv_ref,
    qk_in,
    vv_in,
    wqk_ref,
    wvv_ref,
    pa_ref,
    pac_ref,
    par_ref,
    pas_ref,
    paz_ref,
    pb_ref,
    pbc_ref,
    pbr_ref,
    pbs_ref,
    pbz_ref,
    far_ref,
    dws_ref,
    dwc_ref,
    dwz_ref,
    dwp_ref,
    local_sem,
    send_sem,
    recv_sem,
    row_sem,
):
    wire = Wire(local_sem, send_sem, recv_sem)
    me, rep, near, core, layers, far = places(parts, copies)
    blocks, _, width = near_ref.shape
    total = blocks * BLOCK
    rows = total // parts
    trees = total // TREE_TOK
    per = rows // BLOCK
    depth = width // parts
    side = lax.rem(rep, 2)
    layer = lax.rem(lax.div(rep, 2), LAYERS)
    other = 1 - side
    split = 2 * LAYERS // parts

    def load(source, target, head):
        return wire.keep(source.at[head], target[head])

    def load_tree(source, target, head):
        some = pl.ds(head * trees, trees)
        return wire.keep(source.at[some], target.at[some])

    def load_head(head):
        return [
            load(q_hbm, q_ref, head),
            load(k_hbm, k_ref, head),
            load(v_hbm, v_ref, head),
            load(kt_hbm, kt_ref, head),
            load_tree(ot_hbm, ot_ref, head),
            load_tree(lse_hbm, lse_ref, head),
        ]

    def arrived(copies_in):
        for copy in copies_in:
            copy.wait_recv()

    loads = [[wire.keep(do_hbm, do_ref)] + load_head(0)]
    greet([p for _, p in near] + [core] + [p for _, p in layers] + far)

    halves_out = [
        wire.send(pa_hbm.at[other], pac_ref, *core),
        wire.send(pb_hbm.at[other], pbc_ref, *core),
    ]
    halves_own = [wire.keep(pa_hbm.at[side], pa_ref), wire.keep(pb_hbm.at[side], pb_ref)]
    for h in range(1, heads):
        loads.append(load_head(h))
    near_load = wire.keep(near_hbm, near_ref)
    weight_load = [
        wire.keep(w, wq_ref.at[:, pl.ds(i * width, width)])
        for i, w in enumerate((wq_hbm, wk_hbm, wv_hbm))
    ]
    base_load = wire.keep(dh1_hbm, dx_ref)

    def beyond(value, slot):
        for i, p in enumerate(far):
            send, recv = far_ref.at[slot, i, 0], far_ref.at[slot, i, 1]
            n, m = value.shape
            send[0:n, 0:m] = value.astype(HALF)
            copy = wire.send(send, recv, *p)
            copy.wait_recv()
            value = value.astype(HALF).astype(SINGLE) + recv[0:n, 0:m].astype(SINGLE)
        return value.astype(HALF)

    low = pb_ref.shape[2]

    def pack_split():
        arrived(halves_out)
        for copy in halves_own:
            copy.wait()
        for r in range(parts):
            for z in range(LAYERS):
                pa_ref[r, z] = total_of(pa_ref[r, z], pac_ref[r, z]).astype(HALF)
        out_a = [wire.send(pa_ref.at[r], par_ref.at[r - 1], *p) for r, p in near]
        for z in range(LAYERS):
            for r in range(parts):
                pb_ref[z, r] = total_of(pb_ref[z, r], pbc_ref[z, r]).astype(HALF)
        out_b = [wire.send(pb_ref.at[flip(layer, j)], pbr_ref.at[j - 1], *p) for j, p in layers]
        return out_a, out_b

    def pack_a_scatter(waits):
        arrived(waits)
        for z in range(LAYERS):
            pas_ref[z] = total_of(
                pa_ref[0, z], *[par_ref[r, z] for r in range(parts - 1)]
            ).astype(HALF)
        return [wire.send(pas_ref.at[flip(layer, j)], paz_ref.at[j - 1], *p) for j, p in layers]

    def pack_a_spread(waits):
        arrived(waits)
        piece = total_of(pas_ref[layer], *[paz_ref[j] for j in range(LAYERS - 1)])
        fa_ref[side, layer] = beyond(piece, 0)
        here = fa_ref.at[side, layer]
        return [wire.send(here, here, *p) for _, p in layers]

    def pack_b_scatter(waits):
        arrived(waits)
        for r in range(parts):
            piece = total_of(pb_ref[layer, r], *[pbr_ref[j, r] for j in range(LAYERS - 1)])
            pbs_ref[r] = beyond(piece, 3 + r)
        return [wire.send(pbs_ref.at[r], pbz_ref.at[r - 1], *p) for r, p in near]

    def pack_b_spread(waits):
        arrived(waits)
        piece = total_of(pbs_ref[0], *[pbz_ref[r] for r in range(parts - 1)])
        fb_ref[side, layer] = piece.astype(HALF)
        here = fb_ref.at[side, layer]
        return [wire.send(here, here, *p) for _, p in layers]

    def pack_cores(waits):
        arrived(waits)
        return [
            wire.send(fa_ref.at[side], fa_ref.at[side], *core),
            wire.send(fb_ref.at[side], fb_ref.at[side], *core),
        ]

    def weights_cores(head):
        return [wire.send(dws_ref.at[head, other], dwc_ref.at[head], *core)]

    def weights_scatter(head, waits):
        arrived(waits)
        for z in range(LAYERS):
            dws_ref[head, side, z] = total_of(dws_ref[head, side, z], dwc_ref[head, z]).astype(HALF)
        return [
            wire.send(dws_ref.at[head, side, flip(layer, j)], dwz_ref.at[head, j - 1], *p)
            for j, p in layers
        ]

    to_row = layer if split == 2 else side * LAYERS + layer

    def weights_send(head, waits):
        arrived(waits)
        piece = total_of(
            dws_ref[head, side, layer], *[dwz_ref[head, j] for j in range(LAYERS - 1)]
        )
        dwp_ref[head] = beyond(piece, 1 + head)

        @pl.when(to_row == 0)
        def _():
            dwf_ref[head, side, layer] = dwp_ref[head]

        copy = pltpu.make_async_remote_copy(
            dwp_ref.at[head],
            dwf_ref.at[head, side, layer],
            row_sem.at[0, head],
            row_sem.at[1, head],
            device_id={"fsdp": flip_two(me, to_row, parts)},
            device_id_type=MESH,
        )

        @pl.when(to_row != 0)
        def _():
            copy.start()

        return copy

    def weights_spread(head, copy):
        @pl.when(to_row != 0)
        def _():
            copy.wait()

        here = dwf_ref.at[head, side, layer]
        return [wire.send(here, here, *p) for _, p in layers]

    def weights_last(head, waits):
        arrived(waits)
        return [wire.send(dwf_ref.at[head, side], dwf_ref.at[head, side], *core)]

    def unsort(head):
        for r in range(parts):

            def one(j, _):
                place = order_ref[blocks + r * per + j]
                both = jnp.concatenate([dq_s[place], dk_s[place] * 0.125], axis=1)
                qk_ref[head, r, block_at(j), :] = both.astype(HALF)
                lower = pl.ds(pl.multiple_of(j * (BLOCK // 2), BLOCK // 2), BLOCK // 2)
                vv_ref[head, r, lower, :] = fold(dv_s[place]).astype(HALF)
                return 0

            lax.fori_loop(0, per, one, 0)
        if head == heads - 1:
            kept.append(wire.keep(qk_ref.at[head, 0], qk_hbm.at[0]))
            kept.append(wire.keep(vv_ref.at[head, 0], vv_hbm.at[0]))
            return [wire.send(qk_ref.at[head, r], qk_hbm.at[r], *p) for r, p in near]
        qk_in[head, 0] = qk_ref[head, 0]
        vv_in[head, 0] = vv_ref[head, 0]
        return [wire.send(qk_ref.at[head, r], qk_in.at[head, r], *p) for r, p in near]

    def send_values(head):
        if head == heads - 1:
            return [wire.send(vv_ref.at[head, r], vv_hbm.at[r], *p) for r, p in near]
        return [wire.send(vv_ref.at[head, r], vv_in.at[head, r], *p) for r, p in near]

    def weight_grads(head):
        total_dw = 0.0
        for r in range(parts):
            grads = jnp.concatenate([qk_ref[head, r], unfold(vv_ref[head, r])], axis=1)
            total_dw = total_dw + dot(
                grads.T, near_ref[r * per : (r + 1) * per].reshape(rows, width)
            )
        dw = total_dw.astype(HALF)
        for c in range(parts):
            to = flip(me, c)
            piece = dw[:, c * depth : (c + 1) * depth]
            if split == 2:
                dws_ref[head, 0, to] = piece[: piece.shape[0] // 2]
                dws_ref[head, 1, to] = piece[piece.shape[0] // 2 :]
            else:
                dws_ref[head, lax.div(to, LAYERS), lax.rem(to, LAYERS)] = piece

    def turn_weights():
        for h in range(heads):
            for c in range(parts):
                at = (c * heads + h) * HEAD
                wqk_ref[h, :, c * 2 * HEAD : (c + 1) * 2 * HEAD] = jnp.concatenate(
                    [wq_ref[:, at : at + HEAD], wq_ref[:, width + at : width + at + HEAD]], axis=1
                )
                wvv_ref[h, :, c * HEAD : (c + 1) * HEAD] = wq_ref[
                    :, 2 * width + at : 2 * width + at + HEAD
                ]

    def input_grad(head):
        def pick(ref, c, at):
            return ref[head, flip(me, c), at, :]

        def step(i, _):
            at = pl.ds(pl.multiple_of(i * tile, tile), tile)
            lower = pl.ds(pl.multiple_of(i * (tile // 2), tile // 2), tile // 2)
            qk = jnp.concatenate([pick(qk_in, c, at) for c in range(parts)], axis=1)
            vv = jnp.concatenate([unfold(pick(vv_in, c, lower)) for c in range(parts)], axis=1)
            dx_ref[at, :] += dot(qk, wqk_ref[head], NT) + dot(vv, wvv_ref[head], NT)
            return 0

        lax.fori_loop(0, rows // tile, step, 0)

    kept = []
    sent, values, chains = [], [], {}
    for h in range(heads):
        for copy in loads[h]:
            copy.wait()
        dk_s[...] = jnp.zeros_like(dk_s)
        dv_s[...] = jnp.zeros_like(dv_s)
        held = None

        def close_held():
            tile, key, chosen, s, dp, last = held
            tile.close(key, chosen, s, dp, last, kt_ref, dq_s, dk_s, dv_s)

        for number, (begin, keys) in enumerate(tile_list()):
            for tree in range(trees):
                work = BackTile(h, tree, trees, begin, order_ref, ot_ref, lse_ref, do_ref, q_ref)
                for key in keys:
                    opened = work.open(key, k_ref, v_ref)
                    if held:
                        close_held()
                    held = (*opened, key is keys[-1])
            event = (h, number)
            if event == (0, 3):
                pack_a, pack_b = pack_split()
            elif event == (1, 1):
                chains[0] = weights_scatter(0, chains[0])
            elif event == (1, 4):
                pack_a = pack_a_scatter(pack_a)
            elif event == (1, 5):
                chains[0] = weights_send(0, chains[0])
            elif event == (1, 7):
                pack_b = pack_b_scatter(pack_b)
        close_held()
        sent.append(unsort(h))
        if h == 0:
            near_load.wait()
        if h < heads - 1:
            values.append(send_values(h))
            weight_grads(h)
            chains[h] = weights_cores(h)
    end_head = heads - 1
    if heads == 1:
        pack_a = pack_a_scatter(pack_a)
        pack_b = pack_b_scatter(pack_b)
    weight_grads(end_head)
    chains[end_head] = weights_cores(end_head)
    pack_a = pack_a_spread(pack_a)
    for copy in weight_load + [base_load]:
        copy.wait()
    turn_weights()
    kept.append(wire.keep(wqk_ref.at[end_head], wqk_hbm))
    kept.append(wire.keep(wvv_ref.at[end_head], wvv_hbm))
    chains[end_head] = weights_scatter(end_head, chains[end_head])
    if heads > 1:
        arrived(sent[0] + values[0])
        input_grad(0)
    kept.append(wire.keep(dx_ref, dx_hbm))
    chains[end_head] = weights_send(end_head, chains[end_head])
    values.append(send_values(end_head))
    pack_b = pack_b_spread(pack_b)
    if heads > 1:
        chains[0] = weights_spread(0, chains[0])
    last = pack_cores(pack_a + pack_b)
    chains[end_head] = weights_spread(end_head, chains[end_head])
    for h in range(heads):
        last += weights_last(h, chains[h])
    arrived(last + sent[end_head] + values[end_head])
    for copy in kept:
        copy.wait()
    wire.finish()


def finish(parts, copies, heads, order, saved, do, dh1, wq, wk, wv, pa, pb):
    near, q, k, v, kt, ot, lse = saved
    blocks, _, width = near.shape
    total = blocks * BLOCK
    rows = total // parts
    depth = width // parts
    tile = PAIR if rows % PAIR == 0 else BLOCK
    split = 2 * LAYERS // parts
    beyonds = max(copies // (2 * LAYERS), 2).bit_length() - 1
    flat = ((blocks, BLOCK, HEAD), SINGLE)
    qk = ((heads, parts, rows, 2 * HEAD), HALF)
    vv = ((heads, parts, rows // 2, 2 * HEAD), HALF)
    a, b = pa.shape[1:], pb.shape[1:]
    dws = (LAYERS, 3 * HEAD // split, depth)
    each = lambda r: [pltpu.VMEM(r.shape[1:], r.dtype)] * heads
    scratch = [(r.shape, r.dtype) for r in (ot, lse, do)]
    scratch += [((rows, width), SINGLE), ((width, 3 * width), HALF), flat, flat, flat]
    scratch += [qk, vv, qk, vv]
    scratch += [((heads, width, 2 * HEAD * parts), HALF), ((heads, width, HEAD * parts), HALF)]
    scratch += [(n, HALF) for n in (a, a, (parts - 1,) + a[1:], a[1:])]
    scratch += [((LAYERS - 1,) + a[2:], HALF)]
    scratch += [(n, HALF) for n in (b, b, (LAYERS - 1,) + b[1:], b[1:])]
    scratch += [((parts - 1,) + b[2:], HALF)]
    scratch += [((3 + parts, beyonds, 2, max(3 * HEAD, depth), width), HALF)]
    if copies == 2 * LAYERS:
        scratch[-1] = ((1, 1, 2, 16, width), HALF)
    scratch += [((heads, 2) + dws, HALF), ((heads,) + dws, HALF)]
    scratch += [((heads, LAYERS - 1) + dws[1:], HALF), ((heads,) + dws[1:], HALF)]
    outs = [((rows, width), SINGLE), (qk[0][1:], HALF), (vv[0][1:], HALF)]
    outs += [((width, 2 * HEAD * parts), HALF), ((width, HEAD * parts), HALF)]
    small = [((2, LAYERS) + a[2:], HALF), ((2, LAYERS) + b[2:], HALF), ((heads, 2) + dws, HALF)]
    return pl.pallas_call(
        functools.partial(finish_kernel, parts, copies, heads, tile),
        out_shape=[shape(*o) for o in outs + small],
        in_specs=[smem()] + anywhere(14),
        out_specs=anywhere(len(outs)) + vmem(len(small)),
        scratch_shapes=[pltpu.VMEM(near.shape, HALF)]
        + [each(r) for r in (q, k, v, kt)]
        + [pltpu.VMEM(*s) for s in scratch]
        + copies_of(16 + 6 * heads, 48 + 12 * parts)
        + [pltpu.SemaphoreType.DMA((2, heads))],
        compiler_params=params(2),
        name="finish",
    )(order, near, q, k, v, kt, ot, lse, do, dh1, wq, wk, wv, pa, pb)


def close_kernel(
    parts,
    heads,
    base_ref,
    qk_ref,
    vv_ref,
    out_in,
    wqk_ref,
    wvv_ref,
    fa_ref,
    fb_ref,
    dwf_ref,
    norm_in,
    out_ref,
    dx_ref,
    gq_ref,
    gk_ref,
    gv_ref,
    go_ref,
    gh_ref,
    gp_ref,
    *norm_refs,
):
    me = lax.axis_index("fsdp")
    width = base_ref.shape[1]
    depth = width // parts
    split = 2 * LAYERS // parts
    qk = jnp.concatenate([qk_ref[flip(me, c)] for c in range(parts)], axis=1)
    vv = jnp.concatenate([unfold(vv_ref[flip(me, c)]) for c in range(parts)], axis=1)
    dx_ref[...] = base_ref[...] + dot(qk, wqk_ref[...], NT) + dot(vv, wvv_ref[...], NT)
    out_ref[...] = out_in[...]

    step = pl.program_id(0)
    last = pl.num_programs(0) - 1
    low = fb_ref.shape[2]
    small = depth // SLICES
    cols = gp_ref.shape[0]
    unit = width // LAYERS

    def forward_grads(z):
        here = slice(z * width, (z + 1) * width)
        gh_ref[0:low, here] = fa_ref[0, z, 0:low].astype(SINGLE)
        gh_ref[low:depth, here] = fb_ref[0, z].astype(SINGLE)
        piece = jnp.concatenate([fa_ref[1, z, 0:low], fb_ref[1, z]], axis=0).astype(SINGLE)
        if cols < width:
            piece = jnp.concatenate([piece[:, :cols], piece[:, cols:]], axis=0)
        gp_ref[:, z * unit : (z + 1) * unit] = piece.T
        for i in range(2):
            at = (i * LAYERS + z) * small
            go_ref[at : at + small, :] = fa_ref[i, z, low : low + small].astype(SINGLE)

    def attention_grads():
        for i, ref in enumerate(norm_refs):
            ref[...] = norm_in[i : i + 1, :]
        for c in range(parts):
            for h in range(heads):
                r = flip(me, c)
                if split == 2:
                    piece = jnp.concatenate([dwf_ref[h, 0, r], dwf_ref[h, 1, r]], axis=0)
                else:
                    piece = dwf_ref[h, lax.div(r, LAYERS), lax.rem(r, LAYERS)]
                turned = piece.astype(SINGLE).T
                at = (c * heads + h) * HEAD
                for ref, k in ((gq_ref, 0), (gk_ref, 1), (gv_ref, 2)):
                    ref[:, at : at + HEAD] = turned[:, k * HEAD : (k + 1) * HEAD]

    for z in range(LAYERS):
        pl.when(step == jnp.minimum(z, last))(functools.partial(forward_grads, z))
    pl.when(step == last)(attention_grads)


def close(parts, heads, output, base, qk, vv, wqk, wvv, fa, fb, dwf, norms, inner):
    rows, width = base.shape
    tile = PAIR if rows % PAIR == 0 else BLOCK
    depth = width // parts
    row = pl.BlockSpec((tile, width), lambda i: (i, 0))
    once = lambda a: pl.BlockSpec(a, lambda i: (0,) * len(a), pipeline_mode=pl.Buffered(1))
    last = lambda a: pl.BlockSpec(a, lambda i: (0,) * len(a))
    grads = [(depth, width)] * 4 + [(depth, inner), (inner // parts, width)] + [(1, width)] * 4
    return pl.pallas_call(
        functools.partial(close_kernel, parts, heads),
        grid=(rows // tile,),
        in_specs=[
            row,
            pl.BlockSpec((parts, tile, 2 * HEAD), lambda i: (0, i, 0)),
            pl.BlockSpec((parts, tile // 2, 2 * HEAD), lambda i: (0, i, 0)),
            row,
        ]
        + [once(a.shape) for a in (wqk, wvv, fa, fb, dwf, norms)],
        out_specs=[row, row] + [last(g) for g in grads],
        out_shape=[shape((rows, width), HALF), shape((rows, width), SINGLE)]
        + [shape(g, SINGLE) for g in grads],
        compiler_params=pltpu.CompilerParams(vmem_limit_bytes=VMEM_LIMIT),
        name="close",
    )(base, qk, vv, output, wqk, wvv, fa, fb, dwf, norms)


def shards(
    parts,
    copies,
    inputs,
    cotangent,
    segments,
    trees,
    parents,
    w_query,
    w_key,
    w_value,
    w_out,
    w_hidden,
    w_proj,
    norm1_gain,
    norm1_bias,
    norm2_gain,
    norm2_bias,
):
    x = inputs[0]
    rows, width = x.shape
    inner = w_hidden.shape[1]
    heads = HEADS // parts
    wide = heads * HEAD
    depth = width // parts
    me = lax.axis_index("fsdp")
    order = block_order(segments[0], trees[0], parents[0], rows, me)
    by = [w_query, w_key, w_value]
    if wide % BLOCK:
        by = jnp.concatenate([w.reshape(depth, parts, wide) for w in by], axis=2)
        by = [by.transpose(1, 0, 2)]
    cut = lambda w: w.reshape(SLICES, w.shape[0] // SLICES, w.shape[1])
    whole = lambda w: w.reshape(-1, w.shape[-1])
    slices = [cut(w) for w in (w_out, w_hidden, w_proj)]
    near, q, k, v, kt, ot, lse, ctx, *gathered = start(parts, copies, heads, order, x, by, slices)
    vecs = [n.reshape(1, width) for n in (norm1_gain, norm1_bias, norm2_gain, norm2_bias)]
    output, dh1, do, pa, pb, wq, wk, wv, norms = middle(
        parts,
        copies,
        heads,
        x,
        cotangent[0],
        ctx,
        *[whole(w) for w in gathered],
        [cut(w) for w in (w_query, w_key, w_value)],
        vecs,
    )
    saved = (near, q, k, v, kt, ot, lse)
    do = do.reshape(-1, BLOCK, wide)
    weights = [whole(w) for w in (wq, wk, wv)]
    left = finish(parts, copies, heads, order, saved, do, dh1, *weights, pa, pb)
    output, input_grad, *grads = close(parts, heads, output, *left, norms, inner)
    return (output[None], input_grad[None], *grads[:6], *[n.reshape(width) for n in grads[6:]])


def solution(mesh):
    token = P("rep", "fsdp", None)
    weight = P("fsdp", None)
    placed = (token, token, P("rep", None), P("rep", None), P("rep", None, None))
    return jax.shard_map(
        functools.partial(shards, mesh.shape["fsdp"], mesh.shape["rep"]),
        mesh=mesh,
        in_specs=placed + (weight,) * 6 + (P(),) * 4,
        out_specs=(token, token) + (weight,) * 6 + (P(),) * 4,
        check_vma=False,
    )
```

```python
import functools

import jax
import jax.numpy as jnp
from jax import lax
from jax.experimental import pallas as pl
from jax.experimental.pallas import tpu as pltpu
from jax.sharding import PartitionSpec as P

HEADS = 8
HEAD = 64
BLOCK = 128
PAIR = 2 * BLOCK
TRUNK = 8
BRANCHES = 4
LEAVES = 8
TREE_BLOCKS = TRUNK + BRANCHES + LEAVES
TREE_TOK = TREE_BLOCKS * BLOCK
SINGLE = jnp.float32
HALF = jnp.bfloat16
NN = (((1,), (0,)), ((), ()))
NT = (((1,), (1,)), ((), ()))
LOG2E = 1.4426950408889634
SCALE = 0.125 * LOG2E
VMEM_LIMIT = 58 << 20
MESH = pl.DeviceIdType.MESH
SLICES = 8
LAYERS = 4


def dot(left, right, dims=NN):
    return lax.dot_general(left, right, dims, preferred_element_type=SINGLE)


def row_mean(values):
    return jnp.mean(values, axis=-1, keepdims=True)


def block_order(segments, trees, parents, rows, me):
    seg = segments.reshape(-1, BLOCK)[:, 0]
    tree = trees.reshape(-1, BLOCK)[:, 0]
    count = seg.shape[0]
    table = parents.reshape(-1)
    slot = tree * parents.shape[1] + seg
    parent = jnp.sum(
        jnp.where(slot[:, None] == jnp.arange(table.shape[0])[None, :], table[None, :], 0), axis=1
    )
    place = jnp.arange(count, dtype=jnp.int32)
    kind = jnp.where(seg == 0, 0, jnp.where(seg <= BRANCHES, seg, 16 * parent + seg))
    key = (tree * 256 + kind) * 64 + place
    rank = jnp.sum((key[None, :] < key[:, None]).astype(jnp.int32), axis=1)
    per = rows // BLOCK
    near = ((place // per) ^ me) * per + place % per
    order = jnp.sum(jnp.where(rank[None, :] == place[:, None], near[None, :], 0), axis=1)
    back = jnp.sum(jnp.where(near[None, :] == place[:, None], rank[None, :], 0), axis=1)
    return jnp.concatenate([order, back]).astype(jnp.int32)


def tile_list():
    out = []
    trunk = TRUNK * BLOCK
    for start in range(0, trunk, PAIR):
        keys = [(0, start, None)] if start else []
        out.append((start, keys + [(start, PAIR, "causal")]))
    for pair in range(BRANCHES // 2):
        start = trunk + pair * PAIR
        out.append((start, [(0, trunk, None), (start, PAIR, "own")]))
    for branch in range(BRANCHES):
        start = trunk + BRANCHES * BLOCK + branch * PAIR
        out.append(
            (
                start,
                [(0, trunk, None), (trunk + branch * BLOCK, BLOCK, None), (start, PAIR, "own")],
            )
        )
    return out


def mask_of(kind):
    key = lax.broadcasted_iota(jnp.int32, (PAIR, PAIR), 0)
    query = lax.broadcasted_iota(jnp.int32, (PAIR, PAIR), 1)
    mask = key <= query
    if kind == "own":
        mask = mask & ((key >= BLOCK) == (query >= BLOCK))
    return mask


def flip(value, bits):
    bit = 1
    while bit <= bits:
        if bits & bit:
            value = value + bit - 2 * bit * lax.rem(lax.div(value, bit), 2)
        bit *= 2
    return value


def flip_two(one, two, size):
    out = 0
    bit = 1
    while bit < size:
        out = out + bit * lax.rem(lax.rem(lax.div(one, bit), 2) + lax.rem(lax.div(two, bit), 2), 2)
        bit *= 2
    return out


class Wire:
    def __init__(self, local_sem, send_sem, recv_sem):
        self.local_sem, self.send_sem, self.recv_sem = local_sem, send_sem, recv_sem
        self.locals = self.remotes = 0
        self.open = []

    def keep(self, source, target):
        copy = pltpu.make_async_copy(source, target, self.local_sem.at[self.locals])
        self.locals += 1
        copy.start()
        return copy

    def plan(self, source, target, axis, peer):
        copy = pltpu.make_async_remote_copy(
            source,
            target,
            self.send_sem.at[self.remotes],
            self.recv_sem.at[self.remotes],
            device_id={axis: peer},
            device_id_type=MESH,
        )
        self.remotes += 1
        self.open.append(copy)
        return copy

    def send(self, *route):
        copy = self.plan(*route)
        copy.start()
        return copy

    def finish(self):
        for copy in self.open:
            copy.wait_send()


def greet(peers):
    barrier = pltpu.get_barrier_semaphore()
    for axis, peer in peers:
        pl.semaphore_signal(barrier, inc=1, device_id={axis: peer}, device_id_type=MESH)
    pl.semaphore_wait(barrier, len(peers))


def places(parts, copies):
    me = lax.axis_index("fsdp")
    rep = lax.axis_index("rep")
    near = [(r, ("fsdp", flip(me, r))) for r in range(1, parts)]
    core = ("rep", flip(rep, 1))
    layers = [(j, ("rep", flip(rep, 2 * j))) for j in range(1, LAYERS)]
    far = []
    bit = 2 * LAYERS
    while bit < copies:
        far.append(("rep", flip(rep, bit)))
        bit *= 2
    return me, rep, near, core, layers, far


class Gather:
    def __init__(self, wire, spots, shards_in, full):
        self.wire, self.spots, self.shards_in, self.full = wire, spots, shards_in, full
        me, rep, near, core, layers, far = spots
        self.side = lax.rem(rep, 2)
        mine = self.side * LAYERS + lax.rem(lax.div(rep, 2), LAYERS)
        half = pl.ds(self.side * LAYERS, LAYERS)
        others = [flip(me, r) for r, _ in near]
        pairs = list(zip(shards_in, full))
        self.own = []
        self.stages = [
            [wire.plan(a.at[mine], b.at[me, mine], *p) for _, p in near for a, b in pairs],
            [
                wire.plan(b.at[c, mine], b.at[c, mine], *p)
                for _, p in layers
                for c in others
                for b in full
            ],
            [wire.plan(b.at[c, half], b.at[c, half], *core) for c in others for b in full],
        ]

    def start(self):
        for copy in self.stages[0]:
            copy.start()
        me = self.spots[0]
        self.own = [self.wire.keep(a, b.at[me]) for a, b in zip(self.shards_in, self.full)]

    def step(self, i):
        for copy in self.stages[i - 1]:
            copy.wait_recv()
        for copy in self.stages[i]:
            copy.start()

    def end(self):
        for copy in self.stages[2]:
            copy.wait_recv()
        for copy in self.own:
            copy.wait()


def picks(order_ref, tree, start, size):
    first = tree * TREE_BLOCKS + start // BLOCK
    return [order_ref[first + i] for i in range(size // BLOCK)]


def stack(ref, head, chosen, axis):
    blocks = [ref[head][i] for i in chosen]
    return jnp.concatenate(blocks, axis=axis) if len(blocks) > 1 else blocks[0]


def attend_head(head, trees, order_ref, q_ref, k_ref, vt_ref, ot_ref, lse_ref, flat_ref):
    def scores_of(tree, start, keys):
        q = stack(q_ref, head, picks(order_ref, tree, start, PAIR), 0)
        scores = []
        for off, size, kind in keys:
            s = dot(stack(k_ref, head, picks(order_ref, tree, off, size), 0), q, NT)
            if kind:
                s = jnp.where(mask_of(kind), s, -1e30)
            scores.append(s)
        return scores

    def finish_tile(tree, start, keys, scores):
        here = slice(start, start + PAIR)
        at = head * trees + tree
        top = functools.reduce(jnp.maximum, [jnp.max(s, axis=0, keepdims=True) for s in scores])
        top = top * SCALE
        mass = 0.0
        acc = 0.0
        for (off, size, _), s in zip(keys, scores):
            e = jnp.exp2(s * SCALE - top)
            mass = mass + jnp.sum(e, axis=0, keepdims=True)
            vt = stack(vt_ref, head, picks(order_ref, tree, off, size), 1)
            acc = acc + dot(vt, e.astype(HALF))
        out = acc * (1.0 / mass)
        lse_ref[at, :, here] = top + jnp.log2(mass)
        ot_ref[at, :, here] = out
        place = tree * TREE_BLOCKS + start // BLOCK
        flat_ref[place : place + 2] = out.T.astype(HALF).reshape(2, BLOCK, HEAD)

    held = []
    for start, keys in tile_list():
        for tree in range(trees):
            held.append((tree, start, keys, scores_of(tree, start, keys)))
            if len(held) > 2:
                finish_tile(*held.pop(0))
    for tile in held:
        finish_tile(*tile)


def fold(block):
    return jnp.concatenate([block[: BLOCK // 2], block[BLOCK // 2 :]], axis=1)


def unfold(packed):
    parts = []
    for i in range(packed.shape[0] // (BLOCK // 2)):
        piece = packed[i * (BLOCK // 2) : (i + 1) * (BLOCK // 2)]
        parts += [piece[:, :HEAD], piece[:, HEAD:]]
    return jnp.concatenate(parts, axis=0)


def block_at(index):
    return pl.ds(pl.multiple_of(index * BLOCK, BLOCK), BLOCK)


def start_kernel(
    parts,
    copies,
    heads,
    order_ref,
    x_hbm,
    by_hbm,
    so_hbm,
    sh_hbm,
    sp_hbm,
    near_hbm,
    q_hbm,
    k_hbm,
    v_hbm,
    kt_hbm,
    ot_hbm,
    lse_hbm,
    ctx_hbm,
    wo_hbm,
    wh_hbm,
    wp_hbm,
    near_ref,
    own_ref,
    q_ref,
    k_ref,
    v_ref,
    kt_ref,
    vt_ref,
    ot_ref,
    lse_ref,
    flat_ref,
    ctx_ref,
    local_sem,
    send_sem,
    recv_sem,
):
    wire = Wire(local_sem, send_sem, recv_sem)
    spots = places(parts, copies)
    me, rep, near, core, layers, far = spots
    per = x_hbm.shape[0]
    blocks = parts * per
    trees = blocks // TREE_BLOCKS
    wide = heads * HEAD
    greet([p for _, p in near] + [core] + [p for _, p in layers])

    def own_piece(device):
        if len(by_hbm) == 1:
            return [(by_hbm[0].at[device], own_ref.at[me])]
        at = pl.ds(pl.multiple_of(device * wide, wide), wide)
        return [
            (w.at[:, at], own_ref.at[me, :, pl.ds(i * wide, wide)]) for i, w in enumerate(by_hbm)
        ]

    kept = [wire.keep(*pair) for pair in own_piece(me)]
    kept.append(wire.keep(x_hbm, near_ref.at[pl.ds(0, per)]))
    own_copies = [wire.send(*pair, *p) for _, p in near for pair in own_piece(p[1])]
    gather = Gather(wire, spots, (so_hbm, sh_hbm, sp_hbm), (wo_hbm, wh_hbm, wp_hbm))
    gather.start()

    def project(first, count):
        weight = own_ref[...].reshape(parts * own_ref.shape[1], 3 * wide)
        x = near_ref[first : first + count].reshape(count * BLOCK, near_ref.shape[2])
        out = dot(x, weight).astype(HALF)
        for i in range(count):
            block = out[i * BLOCK : (i + 1) * BLOCK]
            kt = block[:, wide : 2 * wide].T
            vt = block[:, 2 * wide :].T
            for h in range(heads):
                cols = slice(h * HEAD, (h + 1) * HEAD)
                q_ref[h, first + i] = block[:, cols]
                k_ref[h, first + i] = block[:, wide:][:, cols]
                v_ref[h, first + i] = block[:, 2 * wide :][:, cols]
                kt_ref[h, first + i] = kt[cols]
                vt_ref[h, first + i] = vt[cols]

    def wait_all(copies_in):
        for copy in copies_in:
            copy.wait_recv()

    if parts == 4:
        cuts = [i * per // 4 for i in range(5)]

        def part(chunk, i):
            return pl.ds(chunk * per + cuts[i], cuts[i + 1] - cuts[i])

        (_, px), (_, py), _ = near
        one, two = {}, {}
        for a, b in zip((0, 1, 2, 3), (2, 3, 0, 1)):
            one[a] = wire.send(x_hbm.at[part(0, a)], near_ref.at[part(1, a)], *px)
            two[b] = wire.send(x_hbm.at[part(0, b)], near_ref.at[part(2, b)], *py)
        three = {}
        for a, b in ((0, 2), (1, 3)):
            one[a].wait_recv()
            three[a] = wire.send(near_ref.at[part(1, a)], near_ref.at[part(3, a)], *py)
            two[b].wait_recv()
            three[b] = wire.send(near_ref.at[part(2, b)], near_ref.at[part(3, b)], *px)
            if a == 0:
                gather.step(1)
                for copy in kept:
                    copy.wait()
                wait_all(own_copies)
                project(0, per)
        wait_all([one[2], one[3]])
        project(per, per)
        wait_all([two[0], two[1]])
        project(2 * per, per)
        wait_all([three[0], three[2]])
        project(3 * per, cuts[1])
        project(3 * per + cuts[2], cuts[3] - cuts[2])
        wait_all([three[1], three[3]])
        project(3 * per + cuts[1], cuts[2] - cuts[1])
        project(3 * per + cuts[3], cuts[4] - cuts[3])
    else:
        waits = [wire.send(x_hbm, near_ref.at[pl.ds(r * per, per)], *p) for r, p in near]
        gather.step(1)
        for copy in kept:
            copy.wait()
        wait_all(own_copies + waits)
        for r in range(parts):
            project(r * per, per)
    saves = [wire.keep(near_ref, near_hbm)]
    saves += [
        wire.keep(a, b)
        for a, b in ((q_ref, q_hbm), (k_ref, k_hbm), (v_ref, v_hbm), (kt_ref, kt_hbm))
    ]
    context = []
    for h in range(heads):
        if h == heads - 1:
            gather.step(2)
        views = [[ref.at[i] for i in range(heads)] for ref in (q_ref, k_ref, vt_ref)]
        attend_head(h, trees, order_ref, *views, ot_ref, lse_ref, flat_ref)
        for r in [*range(1, parts), 0]:

            def unsort(j, _):
                block = flat_ref[order_ref[blocks + r * per + j]]
                at = pl.ds(pl.multiple_of(j * (BLOCK // 2), BLOCK // 2), BLOCK // 2)
                ctx_ref[h, r, at, :] = fold(block)
                return 0

            lax.fori_loop(0, per, unsort, 0)
            if r:
                context.append(wire.send(ctx_ref.at[h, r], ctx_hbm.at[h, r], *near[r - 1][1]))
            else:
                saves.append(wire.keep(ctx_ref.at[h, 0], ctx_hbm.at[h, 0]))
        some = pl.ds(h * trees, trees)
        saves.append(wire.keep(ot_ref.at[some], ot_hbm.at[some]))
        saves.append(wire.keep(lse_ref.at[some], lse_hbm.at[some]))
    wait_all(context)
    gather.end()
    for copy in saves:
        copy.wait()
    wire.finish()


def anywhere(count):
    return [pl.BlockSpec(memory_space=pl.ANY)] * count


def vmem(count):
    return [pl.BlockSpec(memory_space=pltpu.VMEM)] * count


def smem():
    return pl.BlockSpec(memory_space=pltpu.SMEM)


def shape(dims, dtype):
    return jax.ShapeDtypeStruct(dims, dtype)


def copies_of(count_local, count_remote):
    return [
        pltpu.SemaphoreType.DMA((count_local,)),
        pltpu.SemaphoreType.DMA((count_remote,)),
        pltpu.SemaphoreType.DMA((count_remote,)),
    ]


def params(number):
    return pltpu.CompilerParams(
        vmem_limit_bytes=VMEM_LIMIT, collective_id=number, has_side_effects=True
    )


def start(parts, copies, heads, order, x, by, slices):
    rows, width = x.shape
    total = parts * rows
    trees = total // TREE_TOK
    n = trees * heads
    tok = ((heads, total // BLOCK, BLOCK, HEAD), HALF)
    turned = ((heads, total // BLOCK, HEAD, BLOCK), HALF)
    near = ((total // BLOCK, BLOCK, width), HALF)
    ot = ((n, HEAD, TREE_TOK), SINGLE)
    lse = ((n, 1, TREE_TOK), SINGLE)
    ctx = ((heads, parts, rows // 2, 2 * HEAD), HALF)
    outs = [near, tok, tok, tok, turned, ot, lse, ctx]
    outs += [((parts,) + w.shape, HALF) for w in slices]
    scratch = [near, ((parts, width // parts, 3 * heads * HEAD), HALF), tok, tok, tok, turned, turned, ot, lse]
    scratch += [((total // BLOCK, BLOCK, HEAD), HALF), ctx]
    return pl.pallas_call(
        functools.partial(start_kernel, parts, copies, heads),
        out_shape=[shape(*o) for o in outs],
        in_specs=[smem(), *anywhere(1), anywhere(len(by)), *anywhere(3)],
        out_specs=anywhere(len(outs)),
        scratch_shapes=[pltpu.VMEM(*s) for s in scratch]
        + copies_of(12 + 3 * heads, 32 + (parts - 1) * 24),
        compiler_params=params(0),
        name="start",
    )(order, x.reshape(rows // BLOCK, BLOCK, width), by, *slices)


def middle_kernel(
    parts,
    copies,
    heads,
    tile,
    x_hbm,
    dy_hbm,
    ctx_hbm,
    wo_hbm,
    wh_hbm,
    wp_hbm,
    sq_hbm,
    sk_hbm,
    sv_hbm,
    vec_refs,
    out_hbm,
    dh1_hbm,
    do_hbm,
    pa_hbm,
    pb_hbm,
    wq_hbm,
    wk_hbm,
    wv_hbm,
    norm_out,
    norm_ref,
    norm_s,
    norm_r,
    x_ref,
    dy_ref,
    ctx_ref,
    wo_ref,
    wh_ref,
    wp_ref,
    out_ref,
    dh1_ref,
    do_ref,
    pa_ref,
    pb_ref,
    cat_ref,
    u_ref,
    df_ref,
    da_ref,
    g_ref,
    dz_ref,
    d_s,
    local_sem,
    send_sem,
    recv_sem,
    tile_sem,
    out_sem,
):
    wire = Wire(local_sem, send_sem, recv_sem)
    spots = places(parts, copies)
    me, rep, near, core, layers, far = spots
    rows, width = x_ref.shape
    inner = wh_ref.shape[1]
    wide = heads * HEAD
    chunk = 512
    count = rows // tile
    loads = [
        wire.keep(ctx_hbm, ctx_ref),
        wire.keep(wo_hbm, wo_ref),
        wire.keep(x_hbm, x_ref),
        wire.keep(wh_hbm, wh_ref),
        wire.keep(wp_hbm, wp_ref),
        wire.keep(dy_hbm, dy_ref),
    ]
    greet([p for _, p in near] + [core] + [p for _, p in layers] + far)
    gather = Gather(wire, spots, (sq_hbm, sk_hbm, sv_hbm), (wq_hbm, wk_hbm, wv_hbm))
    gather.start()
    gain1, bias1, gain2, bias2 = [ref[...] for ref in vec_refs]
    norm_ref[...] = jnp.zeros_like(norm_ref)
    for copy in loads:
        copy.wait()

    def rows_out(i, at):
        return [
            pltpu.make_async_copy(out_ref.at[at], out_hbm.at[at], out_sem.at[2 * i]),
            pltpu.make_async_copy(dh1_ref.at[at], dh1_hbm.at[at], out_sem.at[2 * i + 1]),
        ]

    def rows_sent(i, at):
        return [
            pltpu.make_async_remote_copy(
                do_ref.at[r, at],
                do_hbm.at[r, at],
                tile_sem.at[0, i * parts + r],
                tile_sem.at[1, i * parts + r],
                device_id={p[0]: p[1]},
                device_id_type=MESH,
            )
            for r, p in near
        ] + [
            pltpu.make_async_copy(do_ref.at[0, at], do_hbm.at[0, at], tile_sem.at[0, i * parts])
        ]

    def tile_rows(i):
        return pl.ds(pl.multiple_of(i * tile, tile), tile)

    def tile_step(i, _):
        at = tile_rows(i)
        packed = pl.ds(pl.multiple_of(i * (tile // 2), tile // 2), tile // 2)
        ctx = jnp.concatenate(
            [
                unfold(ctx_ref[h, flip(me, c), packed, :])
                for c in range(parts)
                for h in range(heads)
            ],
            axis=-1,
        )
        cat_ref[at, :] = ctx
        h1 = x_ref[at, :].astype(SINGLE) + dot(ctx, wo_ref[...])
        c1 = h1 - row_mean(h1)
        r1 = lax.rsqrt(row_mean(c1 * c1) + 1e-5)
        n1 = c1 * r1
        y1 = n1 * gain1 + bias1
        u = y1.astype(HALF)
        u_ref[at, :] = u
        branch = 0.0
        spans = [slice(j, j + chunk) for j in range(0, inner, chunk)]
        later = dot(u, wh_ref[:, spans[0]])
        for n, s in enumerate(spans):
            z = later
            if n + 1 < len(spans):
                later = dot(u, wh_ref[:, spans[n + 1]])
            cdf = 0.5 * (1.0 + lax.erf(z * 0.7071067811865476))
            pdf = jnp.exp2(z * z * (-0.5 * LOG2E)) * 0.3989422804014327
            g = (z * cdf).astype(HALF)
            g_ref[at, s] = g
            d_s[:, s] = cdf + z * pdf
            branch = branch + dot(g, wp_ref[s, :])
        h2 = y1 + branch
        c2 = h2 - row_mean(h2)
        r2 = lax.rsqrt(row_mean(c2 * c2) + 1e-5)
        n2 = c2 * r2
        out_ref[at, :] = (n2 * gain2 + bias2).astype(HALF)
        dy = dy_ref[at, :].astype(SINGLE)
        norm_ref[2:3, :] += jnp.sum(dy * n2, axis=0, keepdims=True)
        norm_ref[3:4, :] += jnp.sum(dy, axis=0, keepdims=True)
        dn2 = dy * gain2
        dh2 = r2 * (dn2 - row_mean(dn2) - n2 * row_mean(dn2 * n2))
        df = dh2.astype(HALF)
        df_ref[at, :] = df
        back = 0.0
        later = dot(df, wp_ref[spans[0], :], NT)
        for n, s in enumerate(spans):
            dg = later
            if n + 1 < len(spans):
                later = dot(df, wp_ref[spans[n + 1], :], NT)
            dz = (dg * d_s[:, s]).astype(HALF)
            dz_ref[at, s] = dz
            back = back + dot(dz, wh_ref[:, s], NT)
        dy1 = dh2 + back
        norm_ref[0:1, :] += jnp.sum(dy1 * n1, axis=0, keepdims=True)
        norm_ref[1:2, :] += jnp.sum(dy1, axis=0, keepdims=True)
        dn1 = dy1 * gain1
        dh1 = r1 * (dn1 - row_mean(dn1) - n1 * row_mean(dn1 * n1))
        dh1_ref[at, :] = dh1
        da = dh1.astype(HALF)
        da_ref[at, :] = da
        dctx = dot(da, wo_ref[...], NT).astype(HALF)
        for c in range(parts):
            do_ref[flip(me, c), at, :] = dctx[:, c * wide : (c + 1) * wide]
        for copy in rows_out(i, at) + rows_sent(i, at):
            copy.start()
        for stage in (1, 2):

            @pl.when(i == 1 + (count - 2) * (stage - 1))
            def _():
                gather.step(stage)

        return 0

    lax.fori_loop(0, count, tile_step, 0)
    depth = width // parts
    cols = inner // parts
    low = depth // 2
    unit = width // LAYERS
    small = depth // SLICES

    def put(side, c, z, piece):
        to = flip(me, c)
        pa_ref[side, to, z, 0:low] = piece[:low]
        pb_ref[side, z, to] = piece[low:]

    layer = lax.rem(lax.div(rep, 2), LAYERS)
    norm_s[0] = norm_ref[...]
    norm_r[0, 0] = norm_ref[...]
    sums = [wire.send(norm_s.at[0], norm_r.at[0, j], *p) for j, p in layers]

    def norm_cores():
        for copy in sums:
            copy.wait_recv()
        total = functools.reduce(jnp.add, [norm_r[0, flip(layer, c)] for c in range(LAYERS)])
        for i, p in enumerate(far):
            norm_s[3 + i] = total
            copy = wire.send(norm_s.at[3 + i], norm_r.at[3 + i, 0], *p)
            copy.wait_recv()
            total = total + norm_r[3 + i, 0]
        norm_s[1] = total
        return [wire.send(norm_s.at[1], norm_r.at[1, 0], *core)]

    def norm_group():
        sums[0].wait_recv()
        norm_s[2] = norm_s[1] + norm_r[1, 0]
        norm_r[2, 0] = norm_s[2]
        return [wire.send(norm_s.at[2], norm_r.at[2, r], *p) for r, p in near]

    df_t = df_ref[...].T
    for c in range(parts):
        grad = dot(df_t, g_ref[:, c * cols : (c + 1) * cols]).astype(HALF)
        for z in range(LAYERS):
            piece = grad[z * unit : (z + 1) * unit]
            if cols < width:
                piece = jnp.concatenate([piece[:depth], piece[depth:]], axis=1)
            put(1, c, z, piece)
    sums = norm_cores()
    saves = [wire.keep(pb_ref.at[1], pb_hbm.at[1])]
    u_t = u_ref[...].T
    for z in range(LAYERS):
        grad = dot(u_t, dz_ref[:, z * width : (z + 1) * width]).astype(HALF)
        for c in range(parts):
            put(0, c, z, grad[c * depth : (c + 1) * depth])
    sums = norm_group()
    saves.append(wire.keep(pb_ref.at[0], pb_hbm.at[0]))
    grad = dot(cat_ref[...].T, da_ref[...]).astype(HALF)
    for c in range(parts):
        for side in range(2):
            for z in range(LAYERS):
                at = c * depth + (side * LAYERS + z) * small
                pa_ref[side, flip(me, c), z, low : low + small] = grad[at : at + small]
    saves.append(wire.keep(pa_ref, pa_hbm))

    def tile_end(i, _):
        at = tile_rows(i)
        for copy in rows_out(i, at):
            copy.wait()
        sent = rows_sent(i, at)
        for copy in sent:
            copy.wait()
        return 0

    lax.fori_loop(0, count, tile_end, 0)
    for copy in sums:
        copy.wait_recv()
    norm_out[...] = functools.reduce(jnp.add, [norm_r[2, flip(me, c)] for c in range(parts)])
    for copy in saves:
        copy.wait()
    gather.end()
    wire.finish()


def middle(parts, copies, heads, x, dy, ctx, wo, wh, wp, slices, vecs):
    rows, width = x.shape
    inner = wp.shape[0]
    tile = PAIR if rows % PAIR == 0 else BLOCK
    depth = width // parts
    wide = heads * HEAD
    tok = ((rows, width), HALF)
    full = ((rows, width), SINGLE)
    do = ((parts, rows, wide), HALF)
    pack = ((2, parts, LAYERS, depth // 2 + depth // SLICES, width), HALF)
    pack_b = ((2, LAYERS, parts, depth // 2, width), HALF)
    big = ((rows, inner), HALF)
    outs = [tok, full, do, pack, pack_b] + [((parts,) + w.shape, HALF) for w in slices]
    stages = copies.bit_length() + 1
    norm = (4, width)
    scratch = [(norm, SINGLE), ((stages,) + norm, SINGLE)]
    scratch += [((stages, max(parts, LAYERS)) + norm, SINGLE)]
    scratch += [tok, tok, (ctx.shape, HALF), ((width, width), HALF), ((width, inner), HALF)]
    scratch += [((inner, width), HALF), tok, full, do, pack, pack_b, tok, tok, tok, tok, big, big]
    scratch += [((tile, inner), SINGLE)]
    count = rows // tile
    return pl.pallas_call(
        functools.partial(middle_kernel, parts, copies, heads, tile),
        out_shape=[shape(*o) for o in outs] + [shape((4, width), SINGLE)],
        in_specs=[*anywhere(9), vmem(4)],
        out_specs=anywhere(len(outs)) + vmem(1),
        scratch_shapes=[pltpu.VMEM(*s) for s in scratch]
        + copies_of(12, 24 * parts)
        + [
            pltpu.SemaphoreType.DMA((2, count * parts)),
            pltpu.SemaphoreType.DMA((2 * count,)),
        ],
        compiler_params=params(1),
        name="middle",
    )(x, dy, ctx, wo, wh, wp, *slices, vecs)


class BackTile:
    def __init__(self, head, tree, trees, start, order_ref, ot_ref, lse_ref, do_ref, q_ref):
        here = slice(start, start + PAIR)
        self.head, self.tree, self.order_ref = head, tree, order_ref
        self.base = tree * TREE_BLOCKS
        self.first = self.base + start // BLOCK
        at = head * trees + tree
        do = jnp.concatenate([do_ref[order_ref[self.first + i]] for i in range(2)], axis=0)
        self.do = do[:, head * HEAD : (head + 1) * HEAD]
        self.delta = jnp.sum(
            self.do.astype(SINGLE).T * ot_ref[at, :, here], axis=0, keepdims=True
        )
        self.q = stack(q_ref, head, picks(order_ref, tree, start, PAIR), 0)
        self.lse = lse_ref[at, :, here]
        self.dq = 0.0

    def open(self, key, k_ref, v_ref):
        chosen = picks(self.order_ref, self.tree, key[0], key[1])
        s = dot(stack(k_ref, self.head, chosen, 0), self.q, NT)
        return self, key, chosen, s, dot(stack(v_ref, self.head, chosen, 0), self.do, NT)

    def close(self, key, chosen, s, dp, last, kt_ref, dq_s, dk_s, dv_s):
        off, size, kind = key
        out = slice(self.base + off // BLOCK, self.base + (off + size) // BLOCK)
        p = jnp.exp2(s * SCALE - self.lse)
        if kind:
            p = jnp.where(mask_of(kind), p, 0.0)
        ds = (p * (dp - self.delta)).astype(HALF)
        dv_s[out] += dot(p.astype(HALF), self.do).reshape(size // BLOCK, BLOCK, HEAD)
        dk_s[out] += dot(ds, self.q).reshape(size // BLOCK, BLOCK, HEAD)
        self.dq = self.dq + dot(stack(kt_ref, self.head, chosen, 1), ds)
        if last:
            dq_s[self.first : self.first + 2] = (self.dq * 0.125).T.reshape(2, BLOCK, HEAD)


def total_of(*refs):
    return functools.reduce(jnp.add, [r.astype(SINGLE) for r in refs])


def finish_kernel(
    parts,
    copies,
    heads,
    tile,
    order_ref,
    near_hbm,
    q_hbm,
    k_hbm,
    v_hbm,
    kt_hbm,
    ot_hbm,
    lse_hbm,
    do_hbm,
    dh1_hbm,
    wq_hbm,
    wk_hbm,
    wv_hbm,
    pa_hbm,
    pb_hbm,
    dx_hbm,
    qk_hbm,
    vv_hbm,
    wqk_hbm,
    wvv_hbm,
    fa_ref,
    fb_ref,
    dwf_ref,
    near_ref,
    q_ref,
    k_ref,
    v_ref,
    kt_ref,
    ot_ref,
    lse_ref,
    do_ref,
    dx_ref,
    wq_ref,
    dq_s,
    dk_s,
    dv_s,
    qk_ref,
    vv_ref,
    qk_in,
    vv_in,
    wqk_ref,
    wvv_ref,
    pa_ref,
    pac_ref,
    par_ref,
    pas_ref,
    paz_ref,
    pb_ref,
    pbc_ref,
    pbr_ref,
    pbs_ref,
    pbz_ref,
    far_ref,
    dws_ref,
    dwc_ref,
    dwz_ref,
    dwp_ref,
    local_sem,
    send_sem,
    recv_sem,
    row_sem,
):
    wire = Wire(local_sem, send_sem, recv_sem)
    me, rep, near, core, layers, far = places(parts, copies)
    blocks, _, width = near_ref.shape
    total = blocks * BLOCK
    rows = total // parts
    trees = total // TREE_TOK
    per = rows // BLOCK
    depth = width // parts
    side = lax.rem(rep, 2)
    layer = lax.rem(lax.div(rep, 2), LAYERS)
    other = 1 - side
    split = 2 * LAYERS // parts

    def load(source, target, head):
        return wire.keep(source.at[head], target[head])

    def load_tree(source, target, head):
        some = pl.ds(head * trees, trees)
        return wire.keep(source.at[some], target.at[some])

    def load_head(head):
        return [
            load(q_hbm, q_ref, head),
            load(k_hbm, k_ref, head),
            load(v_hbm, v_ref, head),
            load(kt_hbm, kt_ref, head),
            load_tree(ot_hbm, ot_ref, head),
            load_tree(lse_hbm, lse_ref, head),
        ]

    def arrived(copies_in):
        for copy in copies_in:
            copy.wait_recv()

    loads = [[wire.keep(do_hbm, do_ref)] + load_head(0)]
    greet([p for _, p in near] + [core] + [p for _, p in layers] + far)

    halves_out = [
        wire.send(pa_hbm.at[other], pac_ref, *core),
        wire.send(pb_hbm.at[other], pbc_ref, *core),
    ]
    halves_own = [wire.keep(pa_hbm.at[side], pa_ref), wire.keep(pb_hbm.at[side], pb_ref)]
    for h in range(1, heads):
        loads.append(load_head(h))
    near_load = wire.keep(near_hbm, near_ref)
    weight_load = [
        wire.keep(w, wq_ref.at[:, pl.ds(i * width, width)])
        for i, w in enumerate((wq_hbm, wk_hbm, wv_hbm))
    ]
    base_load = wire.keep(dh1_hbm, dx_ref)

    def beyond(value, slot):
        for i, p in enumerate(far):
            send, recv = far_ref.at[slot, i, 0], far_ref.at[slot, i, 1]
            n, m = value.shape
            send[0:n, 0:m] = value.astype(HALF)
            copy = wire.send(send, recv, *p)
            copy.wait_recv()
            value = value.astype(HALF).astype(SINGLE) + recv[0:n, 0:m].astype(SINGLE)
        return value.astype(HALF)

    low = pb_ref.shape[2]

    def pack_split():
        arrived(halves_out)
        for copy in halves_own:
            copy.wait()
        for r in range(parts):
            for z in range(LAYERS):
                pa_ref[r, z] = total_of(pa_ref[r, z], pac_ref[r, z]).astype(HALF)
        out_a = [wire.send(pa_ref.at[r], par_ref.at[r - 1], *p) for r, p in near]
        for z in range(LAYERS):
            for r in range(parts):
                pb_ref[z, r] = total_of(pb_ref[z, r], pbc_ref[z, r]).astype(HALF)
        out_b = [wire.send(pb_ref.at[flip(layer, j)], pbr_ref.at[j - 1], *p) for j, p in layers]
        return out_a, out_b

    def pack_a_scatter(waits):
        arrived(waits)
        for z in range(LAYERS):
            pas_ref[z] = total_of(
                pa_ref[0, z], *[par_ref[r, z] for r in range(parts - 1)]
            ).astype(HALF)
        return [wire.send(pas_ref.at[flip(layer, j)], paz_ref.at[j - 1], *p) for j, p in layers]

    def pack_a_spread(waits):
        arrived(waits)
        piece = total_of(pas_ref[layer], *[paz_ref[j] for j in range(LAYERS - 1)])
        fa_ref[side, layer] = beyond(piece, 0)
        here = fa_ref.at[side, layer]
        return [wire.send(here, here, *p) for _, p in layers]

    def pack_b_scatter(waits):
        arrived(waits)
        for r in range(parts):
            piece = total_of(pb_ref[layer, r], *[pbr_ref[j, r] for j in range(LAYERS - 1)])
            pbs_ref[r] = beyond(piece, 3 + r)
        return [wire.send(pbs_ref.at[r], pbz_ref.at[r - 1], *p) for r, p in near]

    def pack_b_spread(waits):
        arrived(waits)
        piece = total_of(pbs_ref[0], *[pbz_ref[r] for r in range(parts - 1)])
        fb_ref[side, layer] = piece.astype(HALF)
        here = fb_ref.at[side, layer]
        return [wire.send(here, here, *p) for _, p in layers]

    def pack_cores(waits):
        arrived(waits)
        return [
            wire.send(fa_ref.at[side], fa_ref.at[side], *core),
            wire.send(fb_ref.at[side], fb_ref.at[side], *core),
        ]

    def weights_cores(head):
        return [wire.send(dws_ref.at[head, other], dwc_ref.at[head], *core)]

    def weights_scatter(head, waits):
        arrived(waits)
        for z in range(LAYERS):
            dws_ref[head, side, z] = total_of(dws_ref[head, side, z], dwc_ref[head, z]).astype(HALF)
        return [
            wire.send(dws_ref.at[head, side, flip(layer, j)], dwz_ref.at[head, j - 1], *p)
            for j, p in layers
        ]

    to_row = layer if split == 2 else side * LAYERS + layer

    def weights_send(head, waits):
        arrived(waits)
        piece = total_of(
            dws_ref[head, side, layer], *[dwz_ref[head, j] for j in range(LAYERS - 1)]
        )
        dwp_ref[head] = beyond(piece, 1 + head)

        @pl.when(to_row == 0)
        def _():
            dwf_ref[head, side, layer] = dwp_ref[head]

        copy = pltpu.make_async_remote_copy(
            dwp_ref.at[head],
            dwf_ref.at[head, side, layer],
            row_sem.at[0, head],
            row_sem.at[1, head],
            device_id={"fsdp": flip_two(me, to_row, parts)},
            device_id_type=MESH,
        )

        @pl.when(to_row != 0)
        def _():
            copy.start()

        return copy

    def weights_spread(head, copy):
        @pl.when(to_row != 0)
        def _():
            copy.wait()

        here = dwf_ref.at[head, side, layer]
        return [wire.send(here, here, *p) for _, p in layers]

    def weights_last(head, waits):
        arrived(waits)
        return [wire.send(dwf_ref.at[head, side], dwf_ref.at[head, side], *core)]

    def unsort(head):
        last = head == heads - 1
        out = []
        for r in [*range(1, parts), 0]:

            def one(j, _):
                place = order_ref[blocks + r * per + j]
                both = jnp.concatenate([dq_s[place], dk_s[place] * 0.125], axis=1)
                qk_ref[head, r, block_at(j), :] = both.astype(HALF)
                return 0

            lax.fori_loop(0, per, one, 0)
            if r:
                to = qk_hbm.at[r] if last else qk_in.at[head, r]
                out.append(wire.send(qk_ref.at[head, r], to, *near[r - 1][1]))
        for r in range(parts):

            def two(j, _):
                place = order_ref[blocks + r * per + j]
                lower = pl.ds(pl.multiple_of(j * (BLOCK // 2), BLOCK // 2), BLOCK // 2)
                vv_ref[head, r, lower, :] = fold(dv_s[place]).astype(HALF)
                return 0

            lax.fori_loop(0, per, two, 0)
        if last:
            kept.append(wire.keep(qk_ref.at[head, 0], qk_hbm.at[0]))
            kept.append(wire.keep(vv_ref.at[head, 0], vv_hbm.at[0]))
        else:
            qk_in[head, 0] = qk_ref[head, 0]
            vv_in[head, 0] = vv_ref[head, 0]
        return out

    def send_values(head):
        if head == heads - 1:
            return [wire.send(vv_ref.at[head, r], vv_hbm.at[r], *p) for r, p in near]
        return [wire.send(vv_ref.at[head, r], vv_in.at[head, r], *p) for r, p in near]

    def weight_grads(head):
        total_dw = 0.0
        for r in range(parts):
            grads = jnp.concatenate([qk_ref[head, r], unfold(vv_ref[head, r])], axis=1)
            total_dw = total_dw + dot(
                grads.T, near_ref[r * per : (r + 1) * per].reshape(rows, width)
            )
        dw = total_dw.astype(HALF)
        for c in range(parts):
            to = flip(me, c)
            piece = dw[:, c * depth : (c + 1) * depth]
            if split == 2:
                dws_ref[head, 0, to] = piece[: piece.shape[0] // 2]
                dws_ref[head, 1, to] = piece[piece.shape[0] // 2 :]
            else:
                dws_ref[head, lax.div(to, LAYERS), lax.rem(to, LAYERS)] = piece

    def turn_weights():
        for h in range(heads):
            for c in range(parts):
                at = (c * heads + h) * HEAD
                wqk_ref[h, :, c * 2 * HEAD : (c + 1) * 2 * HEAD] = jnp.concatenate(
                    [wq_ref[:, at : at + HEAD], wq_ref[:, width + at : width + at + HEAD]], axis=1
                )
                wvv_ref[h, :, c * HEAD : (c + 1) * HEAD] = wq_ref[
                    :, 2 * width + at : 2 * width + at + HEAD
                ]

    def input_grad(head):
        def pick(ref, c, at):
            return ref[head, flip(me, c), at, :]

        def step(i, _):
            at = pl.ds(pl.multiple_of(i * tile, tile), tile)
            lower = pl.ds(pl.multiple_of(i * (tile // 2), tile // 2), tile // 2)
            qk = jnp.concatenate([pick(qk_in, c, at) for c in range(parts)], axis=1)
            vv = jnp.concatenate([unfold(pick(vv_in, c, lower)) for c in range(parts)], axis=1)
            dx_ref[at, :] += dot(qk, wqk_ref[head], NT) + dot(vv, wvv_ref[head], NT)
            return 0

        lax.fori_loop(0, rows // tile, step, 0)

    kept = []
    sent, values, chains = [], [], {}
    for h in range(heads):
        for copy in loads[h]:
            copy.wait()
        dk_s[...] = jnp.zeros_like(dk_s)
        dv_s[...] = jnp.zeros_like(dv_s)
        held = None

        def close_held():
            tile, key, chosen, s, dp, last = held
            tile.close(key, chosen, s, dp, last, kt_ref, dq_s, dk_s, dv_s)

        for number, (begin, keys) in enumerate(tile_list()):
            for tree in range(trees):
                work = BackTile(h, tree, trees, begin, order_ref, ot_ref, lse_ref, do_ref, q_ref)
                for key in keys:
                    opened = work.open(key, k_ref, v_ref)
                    if held:
                        close_held()
                    held = (*opened, key is keys[-1])
            event = (h, number)
            if event == (0, 3):
                pack_a, pack_b = pack_split()
            elif event == (1, 1):
                chains[0] = weights_scatter(0, chains[0])
            elif event == (1, 4):
                pack_a = pack_a_scatter(pack_a)
            elif event == (1, 5):
                chains[0] = weights_send(0, chains[0])
            elif event == (1, 7):
                pack_b = pack_b_scatter(pack_b)
        close_held()
        sent.append(unsort(h))
        if h == 0:
            near_load.wait()
        if h < heads - 1:
            values.append(send_values(h))
            weight_grads(h)
            chains[h] = weights_cores(h)
    end_head = heads - 1
    if heads == 1:
        pack_a = pack_a_scatter(pack_a)
        pack_b = pack_b_scatter(pack_b)
    weight_grads(end_head)
    chains[end_head] = weights_cores(end_head)
    pack_a = pack_a_spread(pack_a)
    for copy in weight_load + [base_load]:
        copy.wait()
    turn_weights()
    kept.append(wire.keep(wqk_ref.at[end_head], wqk_hbm))
    kept.append(wire.keep(wvv_ref.at[end_head], wvv_hbm))
    chains[end_head] = weights_scatter(end_head, chains[end_head])
    if heads > 1:
        arrived(sent[0] + values[0])
        input_grad(0)
    kept.append(wire.keep(dx_ref, dx_hbm))
    chains[end_head] = weights_send(end_head, chains[end_head])
    values.append(send_values(end_head))
    pack_b = pack_b_spread(pack_b)
    if heads > 1:
        chains[0] = weights_spread(0, chains[0])
    last = pack_cores(pack_a + pack_b)
    chains[end_head] = weights_spread(end_head, chains[end_head])
    for h in range(heads):
        last += weights_last(h, chains[h])
    arrived(last + sent[end_head] + values[end_head])
    for copy in kept:
        copy.wait()
    wire.finish()


def finish(parts, copies, heads, order, saved, do, dh1, wq, wk, wv, pa, pb):
    near, q, k, v, kt, ot, lse = saved
    blocks, _, width = near.shape
    total = blocks * BLOCK
    rows = total // parts
    depth = width // parts
    tile = PAIR if rows % PAIR == 0 else BLOCK
    split = 2 * LAYERS // parts
    beyonds = max(copies // (2 * LAYERS), 2).bit_length() - 1
    flat = ((blocks, BLOCK, HEAD), SINGLE)
    qk = ((heads, parts, rows, 2 * HEAD), HALF)
    vv = ((heads, parts, rows // 2, 2 * HEAD), HALF)
    a, b = pa.shape[1:], pb.shape[1:]
    dws = (LAYERS, 3 * HEAD // split, depth)
    each = lambda r: [pltpu.VMEM(r.shape[1:], r.dtype)] * heads
    scratch = [(r.shape, r.dtype) for r in (ot, lse, do)]
    scratch += [((rows, width), SINGLE), ((width, 3 * width), HALF), flat, flat, flat]
    scratch += [qk, vv, qk, vv]
    scratch += [((heads, width, 2 * HEAD * parts), HALF), ((heads, width, HEAD * parts), HALF)]
    scratch += [(n, HALF) for n in (a, a, (parts - 1,) + a[1:], a[1:])]
    scratch += [((LAYERS - 1,) + a[2:], HALF)]
    scratch += [(n, HALF) for n in (b, b, (LAYERS - 1,) + b[1:], b[1:])]
    scratch += [((parts - 1,) + b[2:], HALF)]
    scratch += [((3 + parts, beyonds, 2, max(3 * HEAD, depth), width), HALF)]
    if copies == 2 * LAYERS:
        scratch[-1] = ((1, 1, 2, 16, width), HALF)
    scratch += [((heads, 2) + dws, HALF), ((heads,) + dws, HALF)]
    scratch += [((heads, LAYERS - 1) + dws[1:], HALF), ((heads,) + dws[1:], HALF)]
    outs = [((rows, width), SINGLE), (qk[0][1:], HALF), (vv[0][1:], HALF)]
    outs += [((width, 2 * HEAD * parts), HALF), ((width, HEAD * parts), HALF)]
    small = [((2, LAYERS) + a[2:], HALF), ((2, LAYERS) + b[2:], HALF), ((heads, 2) + dws, HALF)]
    return pl.pallas_call(
        functools.partial(finish_kernel, parts, copies, heads, tile),
        out_shape=[shape(*o) for o in outs + small],
        in_specs=[smem()] + anywhere(14),
        out_specs=anywhere(len(outs)) + vmem(len(small)),
        scratch_shapes=[pltpu.VMEM(near.shape, HALF)]
        + [each(r) for r in (q, k, v, kt)]
        + [pltpu.VMEM(*s) for s in scratch]
        + copies_of(16 + 6 * heads, 48 + 12 * parts)
        + [pltpu.SemaphoreType.DMA((2, heads))],
        compiler_params=params(2),
        name="finish",
    )(order, near, q, k, v, kt, ot, lse, do, dh1, wq, wk, wv, pa, pb)


def close_kernel(
    parts,
    heads,
    base_ref,
    qk_ref,
    vv_ref,
    out_in,
    wqk_ref,
    wvv_ref,
    fa_ref,
    fb_ref,
    dwf_ref,
    norm_in,
    out_ref,
    dx_ref,
    gq_ref,
    gk_ref,
    gv_ref,
    go_ref,
    gh_ref,
    gp_ref,
    *norm_refs,
):
    me = lax.axis_index("fsdp")
    width = base_ref.shape[1]
    depth = width // parts
    split = 2 * LAYERS // parts
    qk = jnp.concatenate([qk_ref[flip(me, c)] for c in range(parts)], axis=1)
    vv = jnp.concatenate([unfold(vv_ref[flip(me, c)]) for c in range(parts)], axis=1)
    dx_ref[...] = base_ref[...] + dot(qk, wqk_ref[...], NT) + dot(vv, wvv_ref[...], NT)
    out_ref[...] = out_in[...]

    step = pl.program_id(0)
    last = pl.num_programs(0) - 1
    low = fb_ref.shape[2]
    small = depth // SLICES
    cols = gp_ref.shape[0]
    unit = width // LAYERS

    def forward_grads(z):
        here = slice(z * width, (z + 1) * width)
        gh_ref[0:low, here] = fa_ref[0, z, 0:low].astype(SINGLE)
        gh_ref[low:depth, here] = fb_ref[0, z].astype(SINGLE)
        piece = jnp.concatenate([fa_ref[1, z, 0:low], fb_ref[1, z]], axis=0).astype(SINGLE)
        if cols < width:
            piece = jnp.concatenate([piece[:, :cols], piece[:, cols:]], axis=0)
        gp_ref[:, z * unit : (z + 1) * unit] = piece.T
        for i in range(2):
            at = (i * LAYERS + z) * small
            go_ref[at : at + small, :] = fa_ref[i, z, low : low + small].astype(SINGLE)

    def attention_grads():
        for i, ref in enumerate(norm_refs):
            ref[...] = norm_in[i : i + 1, :]
        for c in range(parts):
            for h in range(heads):
                r = flip(me, c)
                if split == 2:
                    piece = jnp.concatenate([dwf_ref[h, 0, r], dwf_ref[h, 1, r]], axis=0)
                else:
                    piece = dwf_ref[h, lax.div(r, LAYERS), lax.rem(r, LAYERS)]
                turned = piece.astype(SINGLE).T
                at = (c * heads + h) * HEAD
                for ref, k in ((gq_ref, 0), (gk_ref, 1), (gv_ref, 2)):
                    ref[:, at : at + HEAD] = turned[:, k * HEAD : (k + 1) * HEAD]

    for z in range(LAYERS):
        pl.when(step == jnp.minimum(z, last))(functools.partial(forward_grads, z))
    pl.when(step == last)(attention_grads)


def close(parts, heads, output, base, qk, vv, wqk, wvv, fa, fb, dwf, norms, inner):
    rows, width = base.shape
    tile = PAIR if rows % PAIR == 0 else BLOCK
    depth = width // parts
    row = pl.BlockSpec((tile, width), lambda i: (i, 0))
    once = lambda a: pl.BlockSpec(a, lambda i: (0,) * len(a), pipeline_mode=pl.Buffered(1))
    last = lambda a: pl.BlockSpec(a, lambda i: (0,) * len(a))
    grads = [(depth, width)] * 4 + [(depth, inner), (inner // parts, width)] + [(1, width)] * 4
    return pl.pallas_call(
        functools.partial(close_kernel, parts, heads),
        grid=(rows // tile,),
        in_specs=[
            row,
            pl.BlockSpec((parts, tile, 2 * HEAD), lambda i: (0, i, 0)),
            pl.BlockSpec((parts, tile // 2, 2 * HEAD), lambda i: (0, i, 0)),
            row,
        ]
        + [once(a.shape) for a in (wqk, wvv, fa, fb, dwf, norms)],
        out_specs=[row, row] + [last(g) for g in grads],
        out_shape=[shape((rows, width), HALF), shape((rows, width), SINGLE)]
        + [shape(g, SINGLE) for g in grads],
        compiler_params=pltpu.CompilerParams(vmem_limit_bytes=VMEM_LIMIT),
        name="close",
    )(base, qk, vv, output, wqk, wvv, fa, fb, dwf, norms)


def shards(
    parts,
    copies,
    inputs,
    cotangent,
    segments,
    trees,
    parents,
    w_query,
    w_key,
    w_value,
    w_out,
    w_hidden,
    w_proj,
    norm1_gain,
    norm1_bias,
    norm2_gain,
    norm2_bias,
):
    x = inputs[0]
    rows, width = x.shape
    inner = w_hidden.shape[1]
    heads = HEADS // parts
    wide = heads * HEAD
    depth = width // parts
    me = lax.axis_index("fsdp")
    order = block_order(segments[0], trees[0], parents[0], rows, me)
    by = [w_query, w_key, w_value]
    if wide % BLOCK:
        by = jnp.concatenate([w.reshape(depth, parts, wide) for w in by], axis=2)
        by = [by.transpose(1, 0, 2)]
    cut = lambda w: w.reshape(SLICES, w.shape[0] // SLICES, w.shape[1])
    whole = lambda w: w.reshape(-1, w.shape[-1])
    slices = [cut(w) for w in (w_out, w_hidden, w_proj)]
    near, q, k, v, kt, ot, lse, ctx, *gathered = start(parts, copies, heads, order, x, by, slices)
    vecs = [n.reshape(1, width) for n in (norm1_gain, norm1_bias, norm2_gain, norm2_bias)]
    output, dh1, do, pa, pb, wq, wk, wv, norms = middle(
        parts,
        copies,
        heads,
        x,
        cotangent[0],
        ctx,
        *[whole(w) for w in gathered],
        [cut(w) for w in (w_query, w_key, w_value)],
        vecs,
    )
    saved = (near, q, k, v, kt, ot, lse)
    do = do.reshape(-1, BLOCK, wide)
    weights = [whole(w) for w in (wq, wk, wv)]
    left = finish(parts, copies, heads, order, saved, do, dh1, *weights, pa, pb)
    output, input_grad, *grads = close(parts, heads, output, *left, norms, inner)
    return (output[None], input_grad[None], *grads[:6], *[n.reshape(width) for n in grads[6:]])


def solution(mesh):
    token = P("rep", "fsdp", None)
    weight = P("fsdp", None)
    placed = (token, token, P("rep", None), P("rep", None), P("rep", None, None))
    return jax.shard_map(
        functools.partial(shards, mesh.shape["fsdp"], mesh.shape["rep"]),
        mesh=mesh,
        in_specs=placed + (weight,) * 6 + (P(),) * 4,
        out_specs=(token, token) + (weight,) * 6 + (P(),) * 4,
        check_vma=False,
    )
```

```python
import functools

import jax
import jax.numpy as jnp
from jax import lax
from jax.experimental import pallas as pl
from jax.experimental.pallas import tpu as pltpu
from jax.sharding import PartitionSpec as P

HEADS = 8
HEAD = 64
BLOCK = 128
PAIR = 2 * BLOCK
TRUNK = 8
BRANCHES = 4
LEAVES = 8
TREE_BLOCKS = TRUNK + BRANCHES + LEAVES
TREE_TOK = TREE_BLOCKS * BLOCK
SINGLE = jnp.float32
HALF = jnp.bfloat16
NN = (((1,), (0,)), ((), ()))
NT = (((1,), (1,)), ((), ()))
LOG2E = 1.4426950408889634
SCALE = 0.125 * LOG2E
VMEM_LIMIT = 58 << 20
MESH = pl.DeviceIdType.MESH
SLICES = 8
LAYERS = 4


def dot(left, right, dims=NN):
    return lax.dot_general(left, right, dims, preferred_element_type=SINGLE)


def row_mean(values):
    return jnp.mean(values, axis=-1, keepdims=True)


def block_order(segments, trees, parents, rows, me):
    seg = segments.reshape(-1, BLOCK)[:, 0]
    tree = trees.reshape(-1, BLOCK)[:, 0]
    count = seg.shape[0]
    table = parents.reshape(-1)
    slot = tree * parents.shape[1] + seg
    parent = jnp.sum(
        jnp.where(slot[:, None] == jnp.arange(table.shape[0])[None, :], table[None, :], 0), axis=1
    )
    place = jnp.arange(count, dtype=jnp.int32)
    kind = jnp.where(seg == 0, 0, jnp.where(seg <= BRANCHES, seg, 16 * parent + seg))
    key = (tree * 256 + kind) * 64 + place
    rank = jnp.sum((key[None, :] < key[:, None]).astype(jnp.int32), axis=1)
    per = rows // BLOCK
    near = ((place // per) ^ me) * per + place % per
    order = jnp.sum(jnp.where(rank[None, :] == place[:, None], near[None, :], 0), axis=1)
    back = jnp.sum(jnp.where(near[None, :] == place[:, None], rank[None, :], 0), axis=1)
    return jnp.concatenate([order, back]).astype(jnp.int32)


def tile_list():
    out = []
    trunk = TRUNK * BLOCK
    for start in range(0, trunk, PAIR):
        keys = [(0, start, None)] if start else []
        out.append((start, keys + [(start, PAIR, "causal")]))
    for pair in range(BRANCHES // 2):
        start = trunk + pair * PAIR
        out.append((start, [(0, trunk, None), (start, PAIR, "own")]))
    for branch in range(BRANCHES):
        start = trunk + BRANCHES * BLOCK + branch * PAIR
        out.append(
            (
                start,
                [(0, trunk, None), (trunk + branch * BLOCK, BLOCK, None), (start, PAIR, "own")],
            )
        )
    return out


def mask_of(kind):
    key = lax.broadcasted_iota(jnp.int32, (PAIR, PAIR), 0)
    query = lax.broadcasted_iota(jnp.int32, (PAIR, PAIR), 1)
    mask = key <= query
    if kind == "own":
        mask = mask & ((key >= BLOCK) == (query >= BLOCK))
    return mask


def flip(value, bits):
    bit = 1
    while bit <= bits:
        if bits & bit:
            value = value + bit - 2 * bit * lax.rem(lax.div(value, bit), 2)
        bit *= 2
    return value


def flip_two(one, two, size):
    out = 0
    bit = 1
    while bit < size:
        out = out + bit * lax.rem(lax.rem(lax.div(one, bit), 2) + lax.rem(lax.div(two, bit), 2), 2)
        bit *= 2
    return out


class Wire:
    def __init__(self, local_sem, send_sem, recv_sem):
        self.local_sem, self.send_sem, self.recv_sem = local_sem, send_sem, recv_sem
        self.locals = self.remotes = 0
        self.open = []

    def keep(self, source, target):
        copy = pltpu.make_async_copy(source, target, self.local_sem.at[self.locals])
        self.locals += 1
        copy.start()
        return copy

    def plan(self, source, target, axis, peer):
        copy = pltpu.make_async_remote_copy(
            source,
            target,
            self.send_sem.at[self.remotes],
            self.recv_sem.at[self.remotes],
            device_id={axis: peer},
            device_id_type=MESH,
        )
        self.remotes += 1
        self.open.append(copy)
        return copy

    def send(self, *route):
        copy = self.plan(*route)
        copy.start()
        return copy

    def finish(self):
        for copy in self.open:
            copy.wait_send()


def greet(peers):
    barrier = pltpu.get_barrier_semaphore()
    for axis, peer in peers:
        pl.semaphore_signal(barrier, inc=1, device_id={axis: peer}, device_id_type=MESH)
    pl.semaphore_wait(barrier, len(peers))


def places(parts, copies):
    me = lax.axis_index("fsdp")
    rep = lax.axis_index("rep")
    near = [(r, ("fsdp", flip(me, r))) for r in range(1, parts)]
    core = ("rep", flip(rep, 1))
    layers = [(j, ("rep", flip(rep, 2 * j))) for j in range(1, LAYERS)]
    far = []
    bit = 2 * LAYERS
    while bit < copies:
        far.append(("rep", flip(rep, bit)))
        bit *= 2
    return me, rep, near, core, layers, far


class Gather:
    def __init__(self, wire, spots, shards_in, full):
        self.wire, self.spots, self.shards_in, self.full = wire, spots, shards_in, full
        me, rep, near, core, layers, far = spots
        self.side = lax.rem(rep, 2)
        mine = self.side * LAYERS + lax.rem(lax.div(rep, 2), LAYERS)
        half = pl.ds(self.side * LAYERS, LAYERS)
        others = [flip(me, r) for r, _ in near]
        pairs = list(zip(shards_in, full))
        self.own = []
        self.stages = [
            [wire.plan(a.at[mine], b.at[me, mine], *p) for _, p in near for a, b in pairs],
            [
                wire.plan(b.at[c, mine], b.at[c, mine], *p)
                for _, p in layers
                for c in others
                for b in full
            ],
            [wire.plan(b.at[c, half], b.at[c, half], *core) for c in others for b in full],
        ]

    def start(self):
        for copy in self.stages[0]:
            copy.start()
        me = self.spots[0]
        self.own = [self.wire.keep(a, b.at[me]) for a, b in zip(self.shards_in, self.full)]

    def step(self, i):
        for copy in self.stages[i - 1]:
            copy.wait_recv()
        for copy in self.stages[i]:
            copy.start()

    def end(self):
        for copy in self.stages[2]:
            copy.wait_recv()
        for copy in self.own:
            copy.wait()


def picks(order_ref, tree, start, size):
    first = tree * TREE_BLOCKS + start // BLOCK
    return [order_ref[first + i] for i in range(size // BLOCK)]


def stack(ref, head, chosen, axis):
    blocks = [ref[head][i] for i in chosen]
    return jnp.concatenate(blocks, axis=axis) if len(blocks) > 1 else blocks[0]


def attend_head(head, trees, order_ref, q_ref, k_ref, vt_ref, ot_ref, lse_ref, flat_ref):
    def scores_of(tree, start, keys):
        q = stack(q_ref, head, picks(order_ref, tree, start, PAIR), 0)
        scores = []
        for off, size, kind in keys:
            s = dot(stack(k_ref, head, picks(order_ref, tree, off, size), 0), q, NT)
            if kind:
                s = jnp.where(mask_of(kind), s, -1e30)
            scores.append(s)
        return scores

    def finish_tile(tree, start, keys, scores):
        here = slice(start, start + PAIR)
        at = head * trees + tree
        top = functools.reduce(jnp.maximum, [jnp.max(s, axis=0, keepdims=True) for s in scores])
        top = top * SCALE
        mass = 0.0
        acc = 0.0
        for (off, size, _), s in zip(keys, scores):
            e = jnp.exp2(s * SCALE - top)
            mass = mass + jnp.sum(e, axis=0, keepdims=True)
            vt = stack(vt_ref, head, picks(order_ref, tree, off, size), 1)
            acc = acc + dot(vt, e.astype(HALF))
        out = acc * (1.0 / mass)
        lse_ref[at, :, here] = top + jnp.log2(mass)
        ot_ref[at, :, here] = out
        place = tree * TREE_BLOCKS + start // BLOCK
        flat_ref[place : place + 2] = out.T.astype(HALF).reshape(2, BLOCK, HEAD)

    held = []
    for start, keys in tile_list():
        for tree in range(trees):
            held.append((tree, start, keys, scores_of(tree, start, keys)))
            if len(held) > 2:
                finish_tile(*held.pop(0))
    for tile in held:
        finish_tile(*tile)


def fold(block):
    return jnp.concatenate([block[: BLOCK // 2], block[BLOCK // 2 :]], axis=1)


def unfold(packed):
    parts = []
    for i in range(packed.shape[0] // (BLOCK // 2)):
        piece = packed[i * (BLOCK // 2) : (i + 1) * (BLOCK // 2)]
        parts += [piece[:, :HEAD], piece[:, HEAD:]]
    return jnp.concatenate(parts, axis=0)


def block_at(index):
    return pl.ds(pl.multiple_of(index * BLOCK, BLOCK), BLOCK)


def start_kernel(
    parts,
    copies,
    heads,
    order_ref,
    x_hbm,
    by_hbm,
    so_hbm,
    sh_hbm,
    sp_hbm,
    near_hbm,
    q_hbm,
    k_hbm,
    v_hbm,
    kt_hbm,
    ot_hbm,
    lse_hbm,
    ctx_hbm,
    wo_hbm,
    wh_hbm,
    wp_hbm,
    near_ref,
    own_ref,
    q_ref,
    k_ref,
    v_ref,
    kt_ref,
    vt_ref,
    ot_ref,
    lse_ref,
    flat_ref,
    ctx_ref,
    local_sem,
    send_sem,
    recv_sem,
):
    wire = Wire(local_sem, send_sem, recv_sem)
    spots = places(parts, copies)
    me, rep, near, core, layers, far = spots
    per = x_hbm.shape[0]
    blocks = parts * per
    trees = blocks // TREE_BLOCKS
    wide = heads * HEAD
    greet([p for _, p in near] + [core] + [p for _, p in layers])

    def own_piece(device):
        if len(by_hbm) == 1:
            return [(by_hbm[0].at[device], own_ref.at[me])]
        at = pl.ds(pl.multiple_of(device * wide, wide), wide)
        return [
            (w.at[:, at], own_ref.at[me, :, pl.ds(i * wide, wide)]) for i, w in enumerate(by_hbm)
        ]

    kept = [wire.keep(*pair) for pair in own_piece(me)]
    kept.append(wire.keep(x_hbm, near_ref.at[pl.ds(0, per)]))
    own_copies = [wire.send(*pair, *p) for _, p in near for pair in own_piece(p[1])]
    gather = Gather(wire, spots, (so_hbm, sh_hbm, sp_hbm), (wo_hbm, wh_hbm, wp_hbm))
    gather.start()

    def project(first, count):
        weight = own_ref[...].reshape(parts * own_ref.shape[1], 3 * wide)
        x = near_ref[first : first + count].reshape(count * BLOCK, near_ref.shape[2])
        out = dot(x, weight).astype(HALF)
        for i in range(count):
            block = out[i * BLOCK : (i + 1) * BLOCK]
            kt = block[:, wide : 2 * wide].T
            vt = block[:, 2 * wide :].T
            for h in range(heads):
                cols = slice(h * HEAD, (h + 1) * HEAD)
                q_ref[h, first + i] = block[:, cols]
                k_ref[h, first + i] = block[:, wide:][:, cols]
                v_ref[h, first + i] = block[:, 2 * wide :][:, cols]
                kt_ref[h, first + i] = kt[cols]
                vt_ref[h, first + i] = vt[cols]

    def wait_all(copies_in):
        for copy in copies_in:
            copy.wait_recv()

    if parts == 4:
        cuts = [i * per // 4 for i in range(5)]

        def part(chunk, i):
            return pl.ds(chunk * per + cuts[i], cuts[i + 1] - cuts[i])

        (_, px), (_, py), _ = near
        one, two = {}, {}
        for a, b in zip((0, 1, 2, 3), (2, 3, 0, 1)):
            one[a] = wire.send(x_hbm.at[part(0, a)], near_ref.at[part(1, a)], *px)
            two[b] = wire.send(x_hbm.at[part(0, b)], near_ref.at[part(2, b)], *py)
        three = {}
        for a, b in ((0, 2), (1, 3)):
            one[a].wait_recv()
            three[a] = wire.send(near_ref.at[part(1, a)], near_ref.at[part(3, a)], *py)
            two[b].wait_recv()
            three[b] = wire.send(near_ref.at[part(2, b)], near_ref.at[part(3, b)], *px)
            if a == 0:
                gather.step(1)
                for copy in kept:
                    copy.wait()
                wait_all(own_copies)
                project(0, per)
        wait_all([one[2], one[3]])
        project(per, per)
        wait_all([two[0], two[1]])
        project(2 * per, per)
        wait_all([three[0], three[2]])
        project(3 * per, cuts[1])
        project(3 * per + cuts[2], cuts[3] - cuts[2])
        wait_all([three[1], three[3]])
        project(3 * per + cuts[1], cuts[2] - cuts[1])
        project(3 * per + cuts[3], cuts[4] - cuts[3])
    else:
        waits = [wire.send(x_hbm, near_ref.at[pl.ds(r * per, per)], *p) for r, p in near]
        gather.step(1)
        for copy in kept:
            copy.wait()
        wait_all(own_copies + waits)
        for r in range(parts):
            project(r * per, per)
    saves = [wire.keep(near_ref, near_hbm)]
    saves += [
        wire.keep(a, b)
        for a, b in ((q_ref, q_hbm), (k_ref, k_hbm), (v_ref, v_hbm), (kt_ref, kt_hbm))
    ]
    context = []
    for h in range(heads):
        if h == heads - 1:
            gather.step(2)
        views = [[ref.at[i] for i in range(heads)] for ref in (q_ref, k_ref, vt_ref)]
        attend_head(h, trees, order_ref, *views, ot_ref, lse_ref, flat_ref)
        for r in [*range(1, parts), 0]:

            def unsort(j, _):
                block = flat_ref[order_ref[blocks + r * per + j]]
                at = pl.ds(pl.multiple_of(j * (BLOCK // 2), BLOCK // 2), BLOCK // 2)
                ctx_ref[h, r, at, :] = fold(block)
                return 0

            lax.fori_loop(0, per, unsort, 0)
            if r:
                context.append(wire.send(ctx_ref.at[h, r], ctx_hbm.at[h, r], *near[r - 1][1]))
            else:
                saves.append(wire.keep(ctx_ref.at[h, 0], ctx_hbm.at[h, 0]))
        some = pl.ds(h * trees, trees)
        saves.append(wire.keep(ot_ref.at[some], ot_hbm.at[some]))
        saves.append(wire.keep(lse_ref.at[some], lse_hbm.at[some]))
    wait_all(context)
    gather.end()
    for copy in saves:
        copy.wait()
    wire.finish()


def anywhere(count):
    return [pl.BlockSpec(memory_space=pl.ANY)] * count


def vmem(count):
    return [pl.BlockSpec(memory_space=pltpu.VMEM)] * count


def smem():
    return pl.BlockSpec(memory_space=pltpu.SMEM)


def shape(dims, dtype):
    return jax.ShapeDtypeStruct(dims, dtype)


def copies_of(count_local, count_remote):
    return [
        pltpu.SemaphoreType.DMA((count_local,)),
        pltpu.SemaphoreType.DMA((count_remote,)),
        pltpu.SemaphoreType.DMA((count_remote,)),
    ]


def params(number):
    return pltpu.CompilerParams(
        vmem_limit_bytes=VMEM_LIMIT, collective_id=number, has_side_effects=True
    )


def start(parts, copies, heads, order, x, by, slices):
    rows, width = x.shape
    total = parts * rows
    trees = total // TREE_TOK
    n = trees * heads
    tok = ((heads, total // BLOCK, BLOCK, HEAD), HALF)
    turned = ((heads, total // BLOCK, HEAD, BLOCK), HALF)
    near = ((total // BLOCK, BLOCK, width), HALF)
    ot = ((n, HEAD, TREE_TOK), SINGLE)
    lse = ((n, 1, TREE_TOK), SINGLE)
    ctx = ((heads, parts, rows // 2, 2 * HEAD), HALF)
    outs = [near, tok, tok, tok, turned, ot, lse, ctx]
    outs += [((parts,) + w.shape, HALF) for w in slices]
    scratch = [near, ((parts, width // parts, 3 * heads * HEAD), HALF), tok, tok, tok, turned, turned, ot, lse]
    scratch += [((total // BLOCK, BLOCK, HEAD), HALF), ctx]
    return pl.pallas_call(
        functools.partial(start_kernel, parts, copies, heads),
        out_shape=[shape(*o) for o in outs],
        in_specs=[smem(), *anywhere(1), anywhere(len(by)), *anywhere(3)],
        out_specs=anywhere(len(outs)),
        scratch_shapes=[pltpu.VMEM(*s) for s in scratch]
        + copies_of(12 + 3 * heads, 32 + (parts - 1) * 24),
        compiler_params=params(0),
        name="start",
    )(order, x.reshape(rows // BLOCK, BLOCK, width), by, *slices)


def middle_kernel(
    parts,
    copies,
    heads,
    tile,
    x_hbm,
    dy_hbm,
    ctx_hbm,
    wo_hbm,
    wh_hbm,
    wp_hbm,
    sq_hbm,
    sk_hbm,
    sv_hbm,
    vec_refs,
    out_hbm,
    dh1_hbm,
    do_hbm,
    pa_hbm,
    pb_hbm,
    wq_hbm,
    wk_hbm,
    wv_hbm,
    norm_out,
    norm_ref,
    norm_s,
    norm_r,
    x_ref,
    dy_ref,
    ctx_ref,
    wo_ref,
    wh_ref,
    wp_ref,
    out_ref,
    dh1_ref,
    do_ref,
    pa_ref,
    pb_ref,
    cat_ref,
    u_ref,
    df_ref,
    da_ref,
    g_ref,
    dz_ref,
    d_s,
    local_sem,
    send_sem,
    recv_sem,
    tile_sem,
    out_sem,
):
    wire = Wire(local_sem, send_sem, recv_sem)
    spots = places(parts, copies)
    me, rep, near, core, layers, far = spots
    rows, width = x_ref.shape
    inner = wh_ref.shape[1]
    wide = heads * HEAD
    chunk = 512
    count = rows // tile
    loads = [
        wire.keep(ctx_hbm, ctx_ref),
        wire.keep(wo_hbm, wo_ref),
        wire.keep(x_hbm, x_ref),
        wire.keep(wh_hbm, wh_ref),
        wire.keep(wp_hbm, wp_ref),
        wire.keep(dy_hbm, dy_ref),
    ]
    greet([p for _, p in near] + [core] + [p for _, p in layers] + far)
    gather = Gather(wire, spots, (sq_hbm, sk_hbm, sv_hbm), (wq_hbm, wk_hbm, wv_hbm))
    gather.start()
    gain1, bias1, gain2, bias2 = [ref[...] for ref in vec_refs]
    norm_ref[...] = jnp.zeros_like(norm_ref)
    for copy in loads:
        copy.wait()

    def rows_out(i, at):
        return [
            pltpu.make_async_copy(out_ref.at[at], out_hbm.at[at], out_sem.at[2 * i]),
            pltpu.make_async_copy(dh1_ref.at[at], dh1_hbm.at[at], out_sem.at[2 * i + 1]),
        ]

    def rows_sent(i, at):
        return [
            pltpu.make_async_remote_copy(
                do_ref.at[r, at],
                do_hbm.at[r, at],
                tile_sem.at[0, i * parts + r],
                tile_sem.at[1, i * parts + r],
                device_id={p[0]: p[1]},
                device_id_type=MESH,
            )
            for r, p in near
        ] + [
            pltpu.make_async_copy(do_ref.at[0, at], do_hbm.at[0, at], tile_sem.at[0, i * parts])
        ]

    def tile_rows(i):
        return pl.ds(pl.multiple_of(i * tile, tile), tile)

    def tile_step(i, _):
        at = tile_rows(i)
        packed = pl.ds(pl.multiple_of(i * (tile // 2), tile // 2), tile // 2)
        ctx = jnp.concatenate(
            [
                unfold(ctx_ref[h, flip(me, c), packed, :])
                for c in range(parts)
                for h in range(heads)
            ],
            axis=-1,
        )
        cat_ref[at, :] = ctx
        h1 = x_ref[at, :].astype(SINGLE) + dot(ctx, wo_ref[...])
        c1 = h1 - row_mean(h1)
        r1 = lax.rsqrt(row_mean(c1 * c1) + 1e-5)
        n1 = c1 * r1
        y1 = n1 * gain1 + bias1
        u = y1.astype(HALF)
        u_ref[at, :] = u
        branch = 0.0
        spans = [slice(j, j + chunk) for j in range(0, inner, chunk)]
        later = dot(u, wh_ref[:, spans[0]])
        for n, s in enumerate(spans):
            z = later
            if n + 1 < len(spans):
                later = dot(u, wh_ref[:, spans[n + 1]])
            cdf = 0.5 * (1.0 + lax.erf(z * 0.7071067811865476))
            pdf = jnp.exp2(z * z * (-0.5 * LOG2E)) * 0.3989422804014327
            g = (z * cdf).astype(HALF)
            g_ref[at, s] = g
            d_s[:, s] = cdf + z * pdf
            branch = branch + dot(g, wp_ref[s, :])
        h2 = y1 + branch
        c2 = h2 - row_mean(h2)
        r2 = lax.rsqrt(row_mean(c2 * c2) + 1e-5)
        n2 = c2 * r2
        out_ref[at, :] = (n2 * gain2 + bias2).astype(HALF)
        dy = dy_ref[at, :].astype(SINGLE)
        norm_ref[2:3, :] += jnp.sum(dy * n2, axis=0, keepdims=True)
        norm_ref[3:4, :] += jnp.sum(dy, axis=0, keepdims=True)
        dn2 = dy * gain2
        dh2 = r2 * (dn2 - row_mean(dn2) - n2 * row_mean(dn2 * n2))
        df = dh2.astype(HALF)
        df_ref[at, :] = df
        back = 0.0
        later = dot(df, wp_ref[spans[0], :], NT)
        for n, s in enumerate(spans):
            dg = later
            if n + 1 < len(spans):
                later = dot(df, wp_ref[spans[n + 1], :], NT)
            dz = (dg * d_s[:, s]).astype(HALF)
            dz_ref[at, s] = dz
            back = back + dot(dz, wh_ref[:, s], NT)
        dy1 = dh2 + back
        norm_ref[0:1, :] += jnp.sum(dy1 * n1, axis=0, keepdims=True)
        norm_ref[1:2, :] += jnp.sum(dy1, axis=0, keepdims=True)
        dn1 = dy1 * gain1
        dh1 = r1 * (dn1 - row_mean(dn1) - n1 * row_mean(dn1 * n1))
        dh1_ref[at, :] = dh1
        da = dh1.astype(HALF)
        da_ref[at, :] = da
        dctx = dot(da, wo_ref[...], NT).astype(HALF)
        for c in range(parts):
            do_ref[flip(me, c), at, :] = dctx[:, c * wide : (c + 1) * wide]
        for copy in rows_out(i, at) + rows_sent(i, at):
            copy.start()
        for stage in (1, 2):

            @pl.when(i == 1 + (count - 2) * (stage - 1))
            def _():
                gather.step(stage)

        return 0

    lax.fori_loop(0, count, tile_step, 0)
    depth = width // parts
    cols = inner // parts
    low = depth // 2
    unit = width // LAYERS
    small = depth // SLICES

    def put(side, c, z, piece):
        to = flip(me, c)
        pa_ref[side, to, z, 0:low] = piece[:low]
        pb_ref[side, z, to] = piece[low:]

    layer = lax.rem(lax.div(rep, 2), LAYERS)
    norm_s[0] = norm_ref[...]
    norm_r[0, 0] = norm_ref[...]
    sums = [wire.send(norm_s.at[0], norm_r.at[0, j], *p) for j, p in layers]

    def norm_cores():
        for copy in sums:
            copy.wait_recv()
        total = functools.reduce(jnp.add, [norm_r[0, flip(layer, c)] for c in range(LAYERS)])
        for i, p in enumerate(far):
            norm_s[3 + i] = total
            copy = wire.send(norm_s.at[3 + i], norm_r.at[3 + i, 0], *p)
            copy.wait_recv()
            total = total + norm_r[3 + i, 0]
        norm_s[1] = total
        return [wire.send(norm_s.at[1], norm_r.at[1, 0], *core)]

    def norm_group():
        sums[0].wait_recv()
        norm_s[2] = norm_s[1] + norm_r[1, 0]
        norm_r[2, 0] = norm_s[2]
        return [wire.send(norm_s.at[2], norm_r.at[2, r], *p) for r, p in near]

    df_t = df_ref[...].T
    for c in range(parts):
        grad = dot(df_t, g_ref[:, c * cols : (c + 1) * cols]).astype(HALF)
        for z in range(LAYERS):
            piece = grad[z * unit : (z + 1) * unit]
            if cols < width:
                piece = jnp.concatenate([piece[:depth], piece[depth:]], axis=1)
            put(1, c, z, piece)
    sums = norm_cores()
    saves = [wire.keep(pb_ref.at[1], pb_hbm.at[1])]
    u_t = u_ref[...].T
    for z in range(LAYERS):
        grad = dot(u_t, dz_ref[:, z * width : (z + 1) * width]).astype(HALF)
        for c in range(parts):
            put(0, c, z, grad[c * depth : (c + 1) * depth])
    sums = norm_group()
    saves.append(wire.keep(pb_ref.at[0], pb_hbm.at[0]))
    grad = dot(cat_ref[...].T, da_ref[...]).astype(HALF)
    for c in range(parts):
        for side in range(2):
            for z in range(LAYERS):
                at = c * depth + (side * LAYERS + z) * small
                pa_ref[side, flip(me, c), z, low : low + small] = grad[at : at + small]
    saves.append(wire.keep(pa_ref, pa_hbm))

    def tile_end(i, _):
        at = tile_rows(i)
        for copy in rows_out(i, at):
            copy.wait()
        sent = rows_sent(i, at)
        for copy in sent:
            copy.wait()
        return 0

    lax.fori_loop(0, count, tile_end, 0)
    for copy in sums:
        copy.wait_recv()
    norm_out[...] = functools.reduce(jnp.add, [norm_r[2, flip(me, c)] for c in range(parts)])
    for copy in saves:
        copy.wait()
    gather.end()
    wire.finish()


def middle(parts, copies, heads, x, dy, ctx, wo, wh, wp, slices, vecs):
    rows, width = x.shape
    inner = wp.shape[0]
    tile = PAIR if rows % PAIR == 0 else BLOCK
    depth = width // parts
    wide = heads * HEAD
    tok = ((rows, width), HALF)
    full = ((rows, width), SINGLE)
    do = ((parts, rows, wide), HALF)
    pack = ((2, parts, LAYERS, depth // 2 + depth // SLICES, width), HALF)
    pack_b = ((2, LAYERS, parts, depth // 2, width), HALF)
    big = ((rows, inner), HALF)
    outs = [tok, full, do, pack, pack_b] + [((parts,) + w.shape, HALF) for w in slices]
    stages = copies.bit_length() + 1
    norm = (4, width)
    scratch = [(norm, SINGLE), ((stages,) + norm, SINGLE)]
    scratch += [((stages, max(parts, LAYERS)) + norm, SINGLE)]
    scratch += [tok, tok, (ctx.shape, HALF), ((width, width), HALF), ((width, inner), HALF)]
    scratch += [((inner, width), HALF), tok, full, do, pack, pack_b, tok, tok, tok, tok, big, big]
    scratch += [((tile, inner), SINGLE)]
    count = rows // tile
    return pl.pallas_call(
        functools.partial(middle_kernel, parts, copies, heads, tile),
        out_shape=[shape(*o) for o in outs] + [shape((4, width), SINGLE)],
        in_specs=[*anywhere(9), vmem(4)],
        out_specs=anywhere(len(outs)) + vmem(1),
        scratch_shapes=[pltpu.VMEM(*s) for s in scratch]
        + copies_of(12, 24 * parts)
        + [
            pltpu.SemaphoreType.DMA((2, count * parts)),
            pltpu.SemaphoreType.DMA((2 * count,)),
        ],
        compiler_params=params(1),
        name="middle",
    )(x, dy, ctx, wo, wh, wp, *slices, vecs)


class BackTile:
    def __init__(self, head, tree, trees, start, order_ref, ot_ref, lse_ref, do_ref, q_ref):
        here = slice(start, start + PAIR)
        self.head, self.tree, self.order_ref = head, tree, order_ref
        self.base = tree * TREE_BLOCKS
        self.first = self.base + start // BLOCK
        at = head * trees + tree
        do = jnp.concatenate([do_ref[order_ref[self.first + i]] for i in range(2)], axis=0)
        self.do = do[:, head * HEAD : (head + 1) * HEAD]
        self.delta = jnp.sum(
            self.do.astype(SINGLE).T * ot_ref[at, :, here], axis=0, keepdims=True
        )
        self.q = stack(q_ref, head, picks(order_ref, tree, start, PAIR), 0)
        self.lse = lse_ref[at, :, here]
        self.dq = 0.0

    def open(self, key, k_ref, v_ref):
        chosen = picks(self.order_ref, self.tree, key[0], key[1])
        s = dot(stack(k_ref, self.head, chosen, 0), self.q, NT)
        return self, key, chosen, s, dot(stack(v_ref, self.head, chosen, 0), self.do, NT)

    def close(self, key, chosen, s, dp, last, kt_ref, dq_s, dk_s, dv_s):
        off, size, kind = key
        out = slice(self.base + off // BLOCK, self.base + (off + size) // BLOCK)
        p = jnp.exp2(s * SCALE - self.lse)
        if kind:
            p = jnp.where(mask_of(kind), p, 0.0)
        ds = (p * (dp - self.delta)).astype(HALF)
        dv_s[out] += dot(p.astype(HALF), self.do).reshape(size // BLOCK, BLOCK, HEAD)
        dk_s[out] += dot(ds, self.q).reshape(size // BLOCK, BLOCK, HEAD)
        self.dq = self.dq + dot(stack(kt_ref, self.head, chosen, 1), ds)
        if last:
            dq_s[self.first : self.first + 2] = (self.dq * 0.125).T.reshape(2, BLOCK, HEAD)


def total_of(*refs):
    return functools.reduce(jnp.add, [r.astype(SINGLE) for r in refs])


def finish_kernel(
    parts,
    copies,
    heads,
    tile,
    order_ref,
    near_hbm,
    q_hbm,
    k_hbm,
    v_hbm,
    kt_hbm,
    ot_hbm,
    lse_hbm,
    do_hbm,
    dh1_hbm,
    wq_hbm,
    wk_hbm,
    wv_hbm,
    pa_hbm,
    pb_hbm,
    dx_hbm,
    qk_hbm,
    vv_hbm,
    wqk_hbm,
    wvv_hbm,
    fa_ref,
    fb_ref,
    dwf_ref,
    near_ref,
    q_ref,
    k_ref,
    v_ref,
    kt_ref,
    ot_ref,
    lse_ref,
    do_ref,
    dx_ref,
    wq_ref,
    dq_s,
    dk_s,
    dv_s,
    qk_ref,
    vv_ref,
    qk_in,
    vv_in,
    wqk_ref,
    wvv_ref,
    pa_ref,
    pac_ref,
    par_ref,
    pas_ref,
    paz_ref,
    pb_ref,
    pbc_ref,
    pbr_ref,
    pbs_ref,
    pbz_ref,
    far_ref,
    dws_ref,
    dwc_ref,
    dwz_ref,
    dwp_ref,
    local_sem,
    send_sem,
    recv_sem,
    row_sem,
):
    wire = Wire(local_sem, send_sem, recv_sem)
    me, rep, near, core, layers, far = places(parts, copies)
    blocks, _, width = near_ref.shape
    total = blocks * BLOCK
    rows = total // parts
    trees = total // TREE_TOK
    per = rows // BLOCK
    depth = width // parts
    side = lax.rem(rep, 2)
    layer = lax.rem(lax.div(rep, 2), LAYERS)
    other = 1 - side
    split = 2 * LAYERS // parts

    def load(source, target, head):
        return wire.keep(source.at[head], target[head])

    def load_tree(source, target, head):
        some = pl.ds(head * trees, trees)
        return wire.keep(source.at[some], target.at[some])

    def load_head(head):
        return [
            load(q_hbm, q_ref, head),
            load(k_hbm, k_ref, head),
            load(v_hbm, v_ref, head),
            load(kt_hbm, kt_ref, head),
            load_tree(ot_hbm, ot_ref, head),
            load_tree(lse_hbm, lse_ref, head),
        ]

    def arrived(copies_in):
        for copy in copies_in:
            copy.wait_recv()

    loads = [[wire.keep(do_hbm, do_ref)] + load_head(0)]
    greet([p for _, p in near] + [core] + [p for _, p in layers] + far)

    halves_out = [
        wire.send(pa_hbm.at[other], pac_ref, *core),
        wire.send(pb_hbm.at[other], pbc_ref, *core),
    ]
    halves_own = [wire.keep(pa_hbm.at[side], pa_ref), wire.keep(pb_hbm.at[side], pb_ref)]
    for h in range(1, heads):
        loads.append(load_head(h))
    near_load = wire.keep(near_hbm, near_ref)
    weight_load = [
        wire.keep(w, wq_ref.at[:, pl.ds(i * width, width)])
        for i, w in enumerate((wq_hbm, wk_hbm, wv_hbm))
    ]
    base_load = wire.keep(dh1_hbm, dx_ref)

    def beyond(value, slot):
        for i, p in enumerate(far):
            send, recv = far_ref.at[slot, i, 0], far_ref.at[slot, i, 1]
            n, m = value.shape
            send[0:n, 0:m] = value.astype(HALF)
            copy = wire.send(send, recv, *p)
            copy.wait_recv()
            value = value.astype(HALF).astype(SINGLE) + recv[0:n, 0:m].astype(SINGLE)
        return value.astype(HALF)

    low = pb_ref.shape[2]

    def pack_split():
        arrived(halves_out)
        for copy in halves_own:
            copy.wait()
        for r in range(parts):
            for z in range(LAYERS):
                pa_ref[r, z] = total_of(pa_ref[r, z], pac_ref[r, z]).astype(HALF)
        out_a = [wire.send(pa_ref.at[r], par_ref.at[r - 1], *p) for r, p in near]
        for z in range(LAYERS):
            for r in range(parts):
                pb_ref[z, r] = total_of(pb_ref[z, r], pbc_ref[z, r]).astype(HALF)
        out_b = [wire.send(pb_ref.at[flip(layer, j)], pbr_ref.at[j - 1], *p) for j, p in layers]
        return out_a, out_b

    def pack_a_scatter(waits):
        arrived(waits)
        for z in range(LAYERS):
            pas_ref[z] = total_of(
                pa_ref[0, z], *[par_ref[r, z] for r in range(parts - 1)]
            ).astype(HALF)
        return [wire.send(pas_ref.at[flip(layer, j)], paz_ref.at[j - 1], *p) for j, p in layers]

    def pack_a_spread(waits):
        arrived(waits)
        piece = total_of(pas_ref[layer], *[paz_ref[j] for j in range(LAYERS - 1)])
        fa_ref[side, layer] = beyond(piece, 0)
        here = fa_ref.at[side, layer]
        return [wire.send(here, here, *p) for _, p in layers]

    def pack_b_scatter(waits):
        arrived(waits)
        for r in range(parts):
            piece = total_of(pb_ref[layer, r], *[pbr_ref[j, r] for j in range(LAYERS - 1)])
            pbs_ref[r] = beyond(piece, 3 + r)
        return [wire.send(pbs_ref.at[r], pbz_ref.at[r - 1], *p) for r, p in near]

    def pack_b_spread(waits):
        arrived(waits)
        piece = total_of(pbs_ref[0], *[pbz_ref[r] for r in range(parts - 1)])
        fb_ref[side, layer] = piece.astype(HALF)
        here = fb_ref.at[side, layer]
        return [wire.send(here, here, *p) for _, p in layers]

    def pack_cores(waits):
        arrived(waits)
        return [
            wire.send(fa_ref.at[side], fa_ref.at[side], *core),
            wire.send(fb_ref.at[side], fb_ref.at[side], *core),
        ]

    def weights_cores(head):
        return [wire.send(dws_ref.at[head, other], dwc_ref.at[head], *core)]

    def weights_scatter(head, waits):
        arrived(waits)
        for z in range(LAYERS):
            dws_ref[head, side, z] = total_of(dws_ref[head, side, z], dwc_ref[head, z]).astype(HALF)
        return [
            wire.send(dws_ref.at[head, side, flip(layer, j)], dwz_ref.at[head, j - 1], *p)
            for j, p in layers
        ]

    to_row = layer if split == 2 else side * LAYERS + layer

    def weights_send(head, waits):
        arrived(waits)
        piece = total_of(
            dws_ref[head, side, layer], *[dwz_ref[head, j] for j in range(LAYERS - 1)]
        )
        dwp_ref[head] = beyond(piece, 1 + head)

        @pl.when(to_row == 0)
        def _():
            dwf_ref[head, side, layer] = dwp_ref[head]

        copy = pltpu.make_async_remote_copy(
            dwp_ref.at[head],
            dwf_ref.at[head, side, layer],
            row_sem.at[0, head],
            row_sem.at[1, head],
            device_id={"fsdp": flip_two(me, to_row, parts)},
            device_id_type=MESH,
        )

        @pl.when(to_row != 0)
        def _():
            copy.start()

        return copy

    def weights_spread(head, copy):
        @pl.when(to_row != 0)
        def _():
            copy.wait()

        here = dwf_ref.at[head, side, layer]
        return [wire.send(here, here, *p) for _, p in layers]

    def weights_last(head, waits):
        arrived(waits)
        return [wire.send(dwf_ref.at[head, side], dwf_ref.at[head, side], *core)]

    def unsort(head):
        last = head == heads - 1
        out = []
        for r in [*range(1, parts), 0]:

            def one(j, _):
                place = order_ref[blocks + r * per + j]
                both = jnp.concatenate([dq_s[place], dk_s[place] * 0.125], axis=1)
                qk_ref[head, r, block_at(j), :] = both.astype(HALF)
                lower = pl.ds(pl.multiple_of(j * (BLOCK // 2), BLOCK // 2), BLOCK // 2)
                vv_ref[head, r, lower, :] = fold(dv_s[place]).astype(HALF)
                return 0

            lax.fori_loop(0, per, one, 0)
            if r:
                to = qk_hbm.at[r] if last else qk_in.at[head, r]
                out.append(wire.send(qk_ref.at[head, r], to, *near[r - 1][1]))
        if last:
            kept.append(wire.keep(qk_ref.at[head, 0], qk_hbm.at[0]))
            kept.append(wire.keep(vv_ref.at[head, 0], vv_hbm.at[0]))
        else:
            qk_in[head, 0] = qk_ref[head, 0]
            vv_in[head, 0] = vv_ref[head, 0]
        return out

    def send_values(head):
        if head == heads - 1:
            return [wire.send(vv_ref.at[head, r], vv_hbm.at[r], *p) for r, p in near]
        return [wire.send(vv_ref.at[head, r], vv_in.at[head, r], *p) for r, p in near]

    def weight_grads(head):
        total_dw = 0.0
        for r in range(parts):
            grads = jnp.concatenate([qk_ref[head, r], unfold(vv_ref[head, r])], axis=1)
            total_dw = total_dw + dot(
                grads.T, near_ref[r * per : (r + 1) * per].reshape(rows, width)
            )
        dw = total_dw.astype(HALF)
        for c in range(parts):
            to = flip(me, c)
            piece = dw[:, c * depth : (c + 1) * depth]
            if split == 2:
                dws_ref[head, 0, to] = piece[: piece.shape[0] // 2]
                dws_ref[head, 1, to] = piece[piece.shape[0] // 2 :]
            else:
                dws_ref[head, lax.div(to, LAYERS), lax.rem(to, LAYERS)] = piece

    def turn_weights():
        for h in range(heads):
            for c in range(parts):
                at = (c * heads + h) * HEAD
                wqk_ref[h, :, c * 2 * HEAD : (c + 1) * 2 * HEAD] = jnp.concatenate(
                    [wq_ref[:, at : at + HEAD], wq_ref[:, width + at : width + at + HEAD]], axis=1
                )
                wvv_ref[h, :, c * HEAD : (c + 1) * HEAD] = wq_ref[
                    :, 2 * width + at : 2 * width + at + HEAD
                ]

    def input_grad(head):
        def pick(ref, c, at):
            return ref[head, flip(me, c), at, :]

        def step(i, _):
            at = pl.ds(pl.multiple_of(i * tile, tile), tile)
            lower = pl.ds(pl.multiple_of(i * (tile // 2), tile // 2), tile // 2)
            qk = jnp.concatenate([pick(qk_in, c, at) for c in range(parts)], axis=1)
            vv = jnp.concatenate([unfold(pick(vv_in, c, lower)) for c in range(parts)], axis=1)
            dx_ref[at, :] += dot(qk, wqk_ref[head], NT) + dot(vv, wvv_ref[head], NT)
            return 0

        lax.fori_loop(0, rows // tile, step, 0)

    kept = []
    sent, values, chains = [], [], {}
    for h in range(heads):
        for copy in loads[h]:
            copy.wait()
        dk_s[...] = jnp.zeros_like(dk_s)
        dv_s[...] = jnp.zeros_like(dv_s)
        held = None

        def close_held():
            tile, key, chosen, s, dp, last = held
            tile.close(key, chosen, s, dp, last, kt_ref, dq_s, dk_s, dv_s)

        for number, (begin, keys) in enumerate(tile_list()):
            for tree in range(trees):
                work = BackTile(h, tree, trees, begin, order_ref, ot_ref, lse_ref, do_ref, q_ref)
                for key in keys:
                    opened = work.open(key, k_ref, v_ref)
                    if held:
                        close_held()
                    held = (*opened, key is keys[-1])
            event = (h, number)
            if event == (0, 3):
                pack_a, pack_b = pack_split()
            elif event == (1, 1):
                chains[0] = weights_scatter(0, chains[0])
            elif event == (1, 4):
                pack_a = pack_a_scatter(pack_a)
            elif event == (1, 5):
                chains[0] = weights_send(0, chains[0])
            elif event == (1, 7):
                pack_b = pack_b_scatter(pack_b)
        close_held()
        sent.append(unsort(h))
        if h == 0:
            near_load.wait()
        if h < heads - 1:
            values.append(send_values(h))
            weight_grads(h)
            chains[h] = weights_cores(h)
    end_head = heads - 1
    if heads == 1:
        pack_a = pack_a_scatter(pack_a)
        pack_b = pack_b_scatter(pack_b)
    weight_grads(end_head)
    chains[end_head] = weights_cores(end_head)
    pack_a = pack_a_spread(pack_a)
    for copy in weight_load + [base_load]:
        copy.wait()
    turn_weights()
    kept.append(wire.keep(wqk_ref.at[end_head], wqk_hbm))
    kept.append(wire.keep(wvv_ref.at[end_head], wvv_hbm))
    chains[end_head] = weights_scatter(end_head, chains[end_head])
    if heads > 1:
        arrived(sent[0] + values[0])
        input_grad(0)
    kept.append(wire.keep(dx_ref, dx_hbm))
    chains[end_head] = weights_send(end_head, chains[end_head])
    values.append(send_values(end_head))
    pack_b = pack_b_spread(pack_b)
    if heads > 1:
        chains[0] = weights_spread(0, chains[0])
    last = pack_cores(pack_a + pack_b)
    chains[end_head] = weights_spread(end_head, chains[end_head])
    for h in range(heads):
        last += weights_last(h, chains[h])
    arrived(last + sent[end_head] + values[end_head])
    for copy in kept:
        copy.wait()
    wire.finish()


def finish(parts, copies, heads, order, saved, do, dh1, wq, wk, wv, pa, pb):
    near, q, k, v, kt, ot, lse = saved
    blocks, _, width = near.shape
    total = blocks * BLOCK
    rows = total // parts
    depth = width // parts
    tile = PAIR if rows % PAIR == 0 else BLOCK
    split = 2 * LAYERS // parts
    beyonds = max(copies // (2 * LAYERS), 2).bit_length() - 1
    flat = ((blocks, BLOCK, HEAD), SINGLE)
    qk = ((heads, parts, rows, 2 * HEAD), HALF)
    vv = ((heads, parts, rows // 2, 2 * HEAD), HALF)
    a, b = pa.shape[1:], pb.shape[1:]
    dws = (LAYERS, 3 * HEAD // split, depth)
    each = lambda r: [pltpu.VMEM(r.shape[1:], r.dtype)] * heads
    scratch = [(r.shape, r.dtype) for r in (ot, lse, do)]
    scratch += [((rows, width), SINGLE), ((width, 3 * width), HALF), flat, flat, flat]
    scratch += [qk, vv, qk, vv]
    scratch += [((heads, width, 2 * HEAD * parts), HALF), ((heads, width, HEAD * parts), HALF)]
    scratch += [(n, HALF) for n in (a, a, (parts - 1,) + a[1:], a[1:])]
    scratch += [((LAYERS - 1,) + a[2:], HALF)]
    scratch += [(n, HALF) for n in (b, b, (LAYERS - 1,) + b[1:], b[1:])]
    scratch += [((parts - 1,) + b[2:], HALF)]
    scratch += [((3 + parts, beyonds, 2, max(3 * HEAD, depth), width), HALF)]
    if copies == 2 * LAYERS:
        scratch[-1] = ((1, 1, 2, 16, width), HALF)
    scratch += [((heads, 2) + dws, HALF), ((heads,) + dws, HALF)]
    scratch += [((heads, LAYERS - 1) + dws[1:], HALF), ((heads,) + dws[1:], HALF)]
    outs = [((rows, width), SINGLE), (qk[0][1:], HALF), (vv[0][1:], HALF)]
    outs += [((width, 2 * HEAD * parts), HALF), ((width, HEAD * parts), HALF)]
    small = [((2, LAYERS) + a[2:], HALF), ((2, LAYERS) + b[2:], HALF), ((heads, 2) + dws, HALF)]
    return pl.pallas_call(
        functools.partial(finish_kernel, parts, copies, heads, tile),
        out_shape=[shape(*o) for o in outs + small],
        in_specs=[smem()] + anywhere(14),
        out_specs=anywhere(len(outs)) + vmem(len(small)),
        scratch_shapes=[pltpu.VMEM(near.shape, HALF)]
        + [each(r) for r in (q, k, v, kt)]
        + [pltpu.VMEM(*s) for s in scratch]
        + copies_of(16 + 6 * heads, 48 + 12 * parts)
        + [pltpu.SemaphoreType.DMA((2, heads))],
        compiler_params=params(2),
        name="finish",
    )(order, near, q, k, v, kt, ot, lse, do, dh1, wq, wk, wv, pa, pb)


def close_kernel(
    parts,
    heads,
    base_ref,
    qk_ref,
    vv_ref,
    out_in,
    wqk_ref,
    wvv_ref,
    fa_ref,
    fb_ref,
    dwf_ref,
    norm_in,
    out_ref,
    dx_ref,
    gq_ref,
    gk_ref,
    gv_ref,
    go_ref,
    gh_ref,
    gp_ref,
    *norm_refs,
):
    me = lax.axis_index("fsdp")
    width = base_ref.shape[1]
    depth = width // parts
    split = 2 * LAYERS // parts
    qk = jnp.concatenate([qk_ref[flip(me, c)] for c in range(parts)], axis=1)
    vv = jnp.concatenate([unfold(vv_ref[flip(me, c)]) for c in range(parts)], axis=1)
    dx_ref[...] = base_ref[...] + dot(qk, wqk_ref[...], NT) + dot(vv, wvv_ref[...], NT)
    out_ref[...] = out_in[...]

    step = pl.program_id(0)
    last = pl.num_programs(0) - 1
    low = fb_ref.shape[2]
    small = depth // SLICES
    cols = gp_ref.shape[0]
    unit = width // LAYERS

    def forward_grads(z):
        here = slice(z * width, (z + 1) * width)
        gh_ref[0:low, here] = fa_ref[0, z, 0:low].astype(SINGLE)
        gh_ref[low:depth, here] = fb_ref[0, z].astype(SINGLE)
        piece = jnp.concatenate([fa_ref[1, z, 0:low], fb_ref[1, z]], axis=0).astype(SINGLE)
        if cols < width:
            piece = jnp.concatenate([piece[:, :cols], piece[:, cols:]], axis=0)
        gp_ref[:, z * unit : (z + 1) * unit] = piece.T
        for i in range(2):
            at = (i * LAYERS + z) * small
            go_ref[at : at + small, :] = fa_ref[i, z, low : low + small].astype(SINGLE)

    def attention_grads():
        for i, ref in enumerate(norm_refs):
            ref[...] = norm_in[i : i + 1, :]
        for c in range(parts):
            for h in range(heads):
                r = flip(me, c)
                if split == 2:
                    piece = jnp.concatenate([dwf_ref[h, 0, r], dwf_ref[h, 1, r]], axis=0)
                else:
                    piece = dwf_ref[h, lax.div(r, LAYERS), lax.rem(r, LAYERS)]
                turned = piece.astype(SINGLE).T
                at = (c * heads + h) * HEAD
                for ref, k in ((gq_ref, 0), (gk_ref, 1), (gv_ref, 2)):
                    ref[:, at : at + HEAD] = turned[:, k * HEAD : (k + 1) * HEAD]

    for z in range(LAYERS):
        pl.when(step == jnp.minimum(z, last))(functools.partial(forward_grads, z))
    pl.when(step == last)(attention_grads)


def close(parts, heads, output, base, qk, vv, wqk, wvv, fa, fb, dwf, norms, inner):
    rows, width = base.shape
    tile = PAIR if rows % PAIR == 0 else BLOCK
    depth = width // parts
    row = pl.BlockSpec((tile, width), lambda i: (i, 0))
    once = lambda a: pl.BlockSpec(a, lambda i: (0,) * len(a), pipeline_mode=pl.Buffered(1))
    last = lambda a: pl.BlockSpec(a, lambda i: (0,) * len(a))
    grads = [(depth, width)] * 4 + [(depth, inner), (inner // parts, width)] + [(1, width)] * 4
    return pl.pallas_call(
        functools.partial(close_kernel, parts, heads),
        grid=(rows // tile,),
        in_specs=[
            row,
            pl.BlockSpec((parts, tile, 2 * HEAD), lambda i: (0, i, 0)),
            pl.BlockSpec((parts, tile // 2, 2 * HEAD), lambda i: (0, i, 0)),
            row,
        ]
        + [once(a.shape) for a in (wqk, wvv, fa, fb, dwf, norms)],
        out_specs=[row, row] + [last(g) for g in grads],
        out_shape=[shape((rows, width), HALF), shape((rows, width), SINGLE)]
        + [shape(g, SINGLE) for g in grads],
        compiler_params=pltpu.CompilerParams(vmem_limit_bytes=VMEM_LIMIT),
        name="close",
    )(base, qk, vv, output, wqk, wvv, fa, fb, dwf, norms)


def shards(
    parts,
    copies,
    inputs,
    cotangent,
    segments,
    trees,
    parents,
    w_query,
    w_key,
    w_value,
    w_out,
    w_hidden,
    w_proj,
    norm1_gain,
    norm1_bias,
    norm2_gain,
    norm2_bias,
):
    x = inputs[0]
    rows, width = x.shape
    inner = w_hidden.shape[1]
    heads = HEADS // parts
    wide = heads * HEAD
    depth = width // parts
    me = lax.axis_index("fsdp")
    order = block_order(segments[0], trees[0], parents[0], rows, me)
    by = [w_query, w_key, w_value]
    if wide % BLOCK:
        by = jnp.concatenate([w.reshape(depth, parts, wide) for w in by], axis=2)
        by = [by.transpose(1, 0, 2)]
    cut = lambda w: w.reshape(SLICES, w.shape[0] // SLICES, w.shape[1])
    whole = lambda w: w.reshape(-1, w.shape[-1])
    slices = [cut(w) for w in (w_out, w_hidden, w_proj)]
    near, q, k, v, kt, ot, lse, ctx, *gathered = start(parts, copies, heads, order, x, by, slices)
    vecs = [n.reshape(1, width) for n in (norm1_gain, norm1_bias, norm2_gain, norm2_bias)]
    output, dh1, do, pa, pb, wq, wk, wv, norms = middle(
        parts,
        copies,
        heads,
        x,
        cotangent[0],
        ctx,
        *[whole(w) for w in gathered],
        [cut(w) for w in (w_query, w_key, w_value)],
        vecs,
    )
    saved = (near, q, k, v, kt, ot, lse)
    do = do.reshape(-1, BLOCK, wide)
    weights = [whole(w) for w in (wq, wk, wv)]
    left = finish(parts, copies, heads, order, saved, do, dh1, *weights, pa, pb)
    output, input_grad, *grads = close(parts, heads, output, *left, norms, inner)
    return (output[None], input_grad[None], *grads[:6], *[n.reshape(width) for n in grads[6:]])


def solution(mesh):
    token = P("rep", "fsdp", None)
    weight = P("fsdp", None)
    placed = (token, token, P("rep", None), P("rep", None), P("rep", None, None))
    return jax.shard_map(
        functools.partial(shards, mesh.shape["fsdp"], mesh.shape["rep"]),
        mesh=mesh,
        in_specs=placed + (weight,) * 6 + (P(),) * 4,
        out_specs=(token, token) + (weight,) * 6 + (P(),) * 4,
        check_vma=False,
    )
```
